128 devices in a mesh: seq: 16 (over y, z), tp: 8 (over x, core).
Axes of the slice: x: 4, y: 4, z: 4, core: 2. Of those that a mesh axis runs over, the one named last changes fastest.
Arguments:
- encoded: bfloat16 [32768, 1280], P(('seq', 'tp')), may hold values from -6 to 6
- starts: int32 [128, 32], replicated, may hold values from 0 to 256, as said below
- w_up: bfloat16 [1280, 4096], P(None, 'tp'), may hold values from -0.15625 to 0.15625
- norm_gain: float32 [4096], replicated, may hold values from 0.25 to 1.75
- w_query: bfloat16 [4096, 4096], P(None, 'tp'), may hold values from -8 to 8
- w_key: bfloat16 [4096, 4096], P(None, 'tp'), may hold values from -8 to 8
- w_value: bfloat16 [4096, 4096], P(None, 'tp'), may hold values from -0.09375 to 0.09375
- w_out: bfloat16 [4096, 4096], P('tp'), may hold values from -0.09375 to 0.09375
- cotangent: bfloat16 [4096, 4096], P('seq', 'tp'), may hold values from -6 to 6
Outputs:
- latent_out: bfloat16 [4096, 4096], P('seq', 'tp')
- latent_grad: float32 [4096, 4096], P('seq', 'tp')
The draws below stay inside these ranges and needn't reach their ends.
Inputs may be any that keep to these rules, and one draw needn't show every extreme that they name: `starts`: row i lists in increasing order the distinct offsets at which patches begin in byte shard i, followed by 256 in unused slots; every shard has at least one patch and at least 8, some shard exactly 32; shard 0 begins a patch at offset 0.
All inputs are finite; a program needn't handle non-finite values.
Results may differ from the reference program's by a relative error of at most 0.014.
Values may be sent and summed in bfloat16 or wider, within the bound.
No kernel may reach another device: no remote copies, remote signals or barrier semaphores. Data moves between devices by JAX's collectives and lax.ppermute only.
A program may use at most 128 MiB of HBM per device.

```python
import jax
import jax.numpy as jnp
from jax import lax

E = 1280
D = 4096
HEADS = 32
HEAD_DIM = 128
B_DEV = 256
PATCH_CAP = 32
SHARDS = 128
PATCHES = 4096
BYTES = 32768


def shard_order(key):
    return jax.random.permutation(key, B_DEV)


def draw_starts(key, part):
    count_key, pick_key, full_key = jax.random.split(jax.random.fold_in(key, 3), 3)
    counts = jax.random.randint(count_key, (SHARDS,), max(PATCH_CAP // 4, 1), PATCH_CAP + 1)
    fullest = jax.random.randint(full_key, (), 0, SHARDS)
    counts = jnp.where(jnp.arange(SHARDS) == fullest, PATCH_CAP, counts)
    orders = jax.vmap(shard_order)(jax.random.split(pick_key, SHARDS))
    places = jnp.arange(B_DEV, dtype=jnp.int32)[None, :]
    chosen = jnp.where(orders < counts[:, None], places, B_DEV)
    ordered = jnp.sort(chosen, axis=1)[:, :PATCH_CAP]
    ordered = ordered.at[0, 0].set(0)
    return ordered.astype(jnp.int32)


def query_key_pair(key):
    first, second = jax.random.split(jax.random.fold_in(key, 17))
    query = jnp.clip(jax.random.normal(first, (D, D), jnp.float32), -5.0, 5.0) * D ** (-0.5)
    other = jnp.clip(jax.random.normal(second, (D, D), jnp.float32), -5.0, 5.0) * D ** (-0.5)
    keys = other
    return (query, keys)


def draw_w_query(key, part):
    return query_key_pair(key)[0].astype(jnp.bfloat16)


def draw_w_key(key, part):
    return query_key_pair(key)[1].astype(jnp.bfloat16)


def shard_levels(key, dims, cuts, least, high):
    def one(dim, parts):
        draws = jax.random.uniform(jax.random.fold_in(jax.random.fold_in(key, 6), dim), (parts,), jnp.float32, least / len(cuts), high / len(cuts))
        return jnp.repeat(jnp.exp(draws), dims[dim] // parts).reshape((-1,) + (1,) * (len(dims) - dim - 1))

    loudness = one(*cuts[0])
    for cut in cuts[1:]:
        loudness = loudness * one(*cut)
    return loudness


def bell_draw(rng, shape, spread, limit, cuts=(), kind=jnp.bfloat16):
    loudness = shard_levels(rng, shape, cuts, -0.22, 0.18) if cuts else 1.0
    drawn = jax.random.normal(rng, shape, jnp.float32) * spread * loudness
    return jnp.minimum(jnp.maximum(drawn, -limit), limit).astype(kind)


def setup_inputs(seed: int = 0) -> dict:
    key_list = jax.random.split(jax.random.key(seed), 10)
    encoded = bell_draw(key_list[0], (BYTES, E), 1.0, 6.0, ((0, 128),))
    starts = draw_starts(jax.random.fold_in(key_list[9], 71), 0)
    w_up = bell_draw(key_list[2], (E, D), E ** -0.5, 0.15625, ((1, 8),))
    norm_gain = jnp.clip(1.0 + 0.15 * jax.random.normal(key_list[3], (D,), jnp.float32), 0.25, 1.75)
    w_query = draw_w_query(jax.random.fold_in(key_list[9], 71), 0)
    w_key = draw_w_key(jax.random.fold_in(key_list[9], 71), 0)
    w_value = bell_draw(key_list[6], (D, D), D ** -0.5, 0.09375, ((1, 8),))
    w_out = bell_draw(key_list[7], (D, D), D ** -0.5, 0.09375, ((0, 8),))
    cotangent = bell_draw(key_list[8], (PATCHES, D), 1.0, 6.0, ((0, 16), (1, 8)))
    return {"encoded": encoded, "starts": starts, "w_up": w_up, "norm_gain": norm_gain, "w_query": w_query, "w_key": w_key, "w_value": w_value, "w_out": w_out, "cotangent": cotangent}


EPS = 1e-05
NEG = -1e+30
CONTRACT_LAST = (((1,), (1,)), ((), ()))

def pooled_patches(encoded, starts):
    shards = starts.shape[0]
    byte_blocks = encoded.reshape(shards, B_DEV, E).astype(jnp.float32)
    places = jnp.arange(B_DEV, dtype=jnp.int32)
    following = jnp.concatenate([starts[:, 1:], jnp.full((shards, 1), B_DEV, jnp.int32)], 1)
    member = ((places[None, None, :] >= starts[:, :, None]) & (places[None, None, :] < following[:, :, None])).astype(jnp.float32)
    sums = jnp.einsum('spb,sbe->spe', member, byte_blocks)
    sizes = lax.optimization_barrier(jnp.sum(member, 2))
    leading = (places[None, :] < starts[:, :1]).astype(jnp.float32)
    lead_sums = jnp.einsum('sb,sbe->se', leading, byte_blocks)
    lead_sizes = lax.optimization_barrier(jnp.sum(leading, 1))
    next_sums = jnp.concatenate([lead_sums[1:], jnp.zeros((1, E), jnp.float32)], 0)
    next_sizes = jnp.concatenate([lead_sizes[1:], jnp.zeros((1,), jnp.float32)], 0)
    counts = lax.optimization_barrier(jnp.sum((starts < B_DEV).astype(jnp.int32), 1))
    last_slot = (jnp.arange(PATCH_CAP, dtype=jnp.int32)[None, :] == (counts - 1)[:, None]).astype(jnp.float32)
    sums = sums + last_slot[:, :, None] * next_sums[:, None, :]
    sizes = sizes + last_slot * next_sizes[:, None]
    patches = sums / jnp.maximum(sizes, 1.0)[:, :, None]
    return patches.reshape(PATCHES, E).astype(jnp.bfloat16)

def split_heads(matrix):
    return matrix.reshape(PATCHES, HEADS, HEAD_DIM).transpose(1, 0, 2)

def join_heads(stacked):
    return stacked.transpose(1, 0, 2).reshape(PATCHES, D)

def reference(encoded, starts, w_up, norm_gain, w_query, w_key, w_value, w_out, cotangent):
    patches = pooled_patches(encoded, starts)
    valid = (starts < B_DEV).reshape(PATCHES)
    latent_in = jnp.dot(patches, w_up, preferred_element_type=jnp.float32).astype(jnp.bfloat16)
    wide = latent_in.astype(jnp.float32)
    rinv = lax.rsqrt(lax.optimization_barrier(jnp.sum(wide * wide, 1)) / D + EPS)
    scaled = (wide * norm_gain[None, :]).astype(jnp.bfloat16)
    query = (rinv[:, None] * jnp.dot(scaled, w_query, preferred_element_type=jnp.float32)).astype(jnp.bfloat16)
    keys = (rinv[:, None] * jnp.dot(scaled, w_key, preferred_element_type=jnp.float32)).astype(jnp.bfloat16)
    values = (rinv[:, None] * jnp.dot(scaled, w_value, preferred_element_type=jnp.float32)).astype(jnp.bfloat16)
    index = jnp.arange(PATCHES, dtype=jnp.int32)
    allowed = valid[None, :] & (index[None, :] <= index[:, None])
    scale = HEAD_DIM ** (-0.5)

    def head_forward(operands):
        head_query, head_key, head_value = operands
        scores = jnp.dot(head_query, head_key.T, preferred_element_type=jnp.float32) * scale
        peak = lax.optimization_barrier(jnp.max(jnp.where(allowed, scores, NEG), 1))
        expo = jnp.where(allowed, jnp.exp(scores - peak[:, None]), 0.0)
        total = lax.optimization_barrier(jnp.sum(expo, 1))
        mixed = jnp.dot(expo.astype(jnp.bfloat16), head_value, preferred_element_type=jnp.float32)
        return ((mixed / total[:, None]).astype(jnp.bfloat16), peak, total)
    heads_query = split_heads(query)
    heads_key = split_heads(keys)
    heads_value = split_heads(values)
    heads_attn, peaks, totals = lax.map(head_forward, (heads_query, heads_key, heads_value))
    attn = join_heads(heads_attn)
    result = wide + jnp.dot(attn, w_out, preferred_element_type=jnp.float32)
    latent_out = jnp.where(valid[:, None], result, 0.0).astype(jnp.bfloat16)
    grad_out = jnp.where(valid[:, None], cotangent, jnp.zeros_like(cotangent))
    d_attn = lax.dot_general(grad_out, w_out, CONTRACT_LAST, preferred_element_type=jnp.float32).astype(jnp.bfloat16)

    def head_backward(operands):
        head_query, head_key, head_value, head_out, head_grad, peak, total = operands
        scores = jnp.dot(head_query, head_key.T, preferred_element_type=jnp.float32) * scale
        probs = jnp.where(allowed, jnp.exp(scores - peak[:, None]), 0.0) / total[:, None]
        delta = lax.optimization_barrier(jnp.sum(head_grad.astype(jnp.float32) * head_out.astype(jnp.float32), 1))
        d_probs = jnp.dot(head_grad, head_value.T, preferred_element_type=jnp.float32)
        d_scores = (probs * (d_probs - delta[:, None])).astype(jnp.bfloat16)
        grad_query = (jnp.dot(d_scores, head_key, preferred_element_type=jnp.float32) * scale).astype(jnp.bfloat16)
        grad_key = (jnp.dot(d_scores.T, head_query, preferred_element_type=jnp.float32) * scale).astype(jnp.bfloat16)
        grad_value = jnp.dot(probs.astype(jnp.bfloat16).T, head_grad, preferred_element_type=jnp.float32).astype(jnp.bfloat16)
        return (grad_query, grad_key, grad_value)
    grads_query, grads_key, grads_value = lax.map(head_backward, (heads_query, heads_key, heads_value, heads_attn, split_heads(d_attn), peaks, totals))
    dnormed = lax.dot_general(join_heads(grads_query), w_query, CONTRACT_LAST, preferred_element_type=jnp.float32) + lax.dot_general(join_heads(grads_key), w_key, CONTRACT_LAST, preferred_element_type=jnp.float32) + lax.dot_general(join_heads(grads_value), w_value, CONTRACT_LAST, preferred_element_type=jnp.float32)
    dots = lax.optimization_barrier(jnp.sum(norm_gain[None, :] * dnormed * wide, 1))
    latent_grad = grad_out.astype(jnp.float32) + rinv[:, None] * norm_gain[None, :] * dnormed - wide * (rinv ** 3)[:, None] * dots[:, None] / D
    return (latent_out, latent_grad)
```

```python
import functools

import jax
import jax.numpy as jnp
from jax import lax
from jax.experimental import pallas as pl
from jax.experimental.pallas import tpu as pltpu
from jax.sharding import Mesh
from jax.sharding import PartitionSpec as P

HEAD = 128
SEQ = ("y", "z")
TP = ("x", "c")
ALL = ("y", "z", "x", "c")
EPS = 1e-05
NEG = -1e30
SCALE = HEAD ** (-0.5)
LOG2E = 1.4426950408889634
EXP2_SCALE = SCALE * LOG2E
F32 = jnp.float32
BF16 = jnp.bfloat16
NT = (((1,), (1,)), ((), ()))
TN = (((0,), (0,)), ((), ()))
SMEM = pl.BlockSpec(memory_space=pltpu.SMEM)
VMEM = pl.BlockSpec(memory_space=pltpu.VMEM)
PARAMS = pltpu.CompilerParams(vmem_limit_bytes=48 * 1024 * 1024)


def shape(*dims, dtype=BF16):
    return jax.ShapeDtypeStruct(dims, dtype)


def call(kernel, ins, outs, scratch=(), name=None):
    specs = [SMEM] + [VMEM] * (len(ins) - 1)
    return pl.pallas_call(
        kernel,
        in_specs=specs,
        out_specs=[VMEM] * len(outs),
        out_shape=list(outs),
        scratch_shapes=list(scratch),
        compiler_params=PARAMS,
        name=name,
    )(*ins)


def moved(block, axis, distance):
    n = lax.axis_size(axis)
    return lax.ppermute(block, axis, [(i, (i + distance) % n) for i in range(n)])


def exchanged(parts, axis):
    return [parts[0]] + [moved(parts[k], axis, k) for k in range(1, len(parts))]


def spread(block, axis):
    return exchanged([block] * lax.axis_size(axis), axis)


def bounds(starts_ref, shard, byte_rows):
    row = starts_ref[pl.ds(shard, 1), :]
    end = jnp.full((1, 1), byte_rows, jnp.int32)
    return row, jnp.concatenate([row[:, 1:], end], axis=1)


def pool_kernel(ids, starts_ref, enc_ref, sums_ref, lead_ref):
    byte_rows = enc_ref.shape[0]
    cap = starts_ref.shape[1]
    row, following = bounds(starts_ref, ids[4], byte_rows)
    places = lax.broadcasted_iota(jnp.int32, (byte_rows, cap), 0)
    inside = ((places >= row) & (places < following)).astype(F32).astype(BF16)
    enc = enc_ref[...]
    sums_ref[...] = lax.dot_general(inside, enc, TN, preferred_element_type=F32)
    leading = (places < row[:, :1]).astype(F32).astype(BF16)
    lead = lax.dot_general(leading, enc, TN, preferred_element_type=F32)
    lead_ref[...] = lead[:1]


def as_column(row, eye):
    return jnp.sum(jnp.where(eye, row, 0.0), axis=1, keepdims=True)


def as_row(column, eye):
    return jnp.sum(jnp.where(eye, column, 0.0), axis=0, keepdims=True)


def eye_of(n):
    return lax.broadcasted_iota(jnp.int32, (n, n), 0) == lax.broadcasted_iota(jnp.int32, (n, n), 1)


def patch_kernel(byte_rows, ids, starts_ref, sums_ref, next_ref, out_ref):
    shards, cap = starts_ref.shape
    shard = ids[4]
    row, following = bounds(starts_ref, shard, byte_rows)
    count = jnp.sum((row < byte_rows).astype(F32), axis=1, keepdims=True)
    slot = lax.broadcasted_iota(jnp.int32, (1, cap), 1).astype(F32)
    last = (slot == count - 1.0).astype(F32)
    after = starts_ref[pl.ds(jnp.minimum(shard + 1, shards - 1), 1), :][:, :1].astype(F32)
    after = jnp.where(shard + 1 < shards, after, 0.0)
    sizes = (following - row).astype(F32) + last * after
    eye = eye_of(cap)
    total = sums_ref[...] + as_column(last, eye) * next_ref[...]
    out_ref[...] = (total / as_column(jnp.maximum(sizes, 1.0), eye)).astype(BF16)


def latent_kernel(ids, own_ref, other_ref, w_ref, out_ref, group):
    x, c = ids[0], ids[1]
    count, rows, width = own_ref.shape
    for k in range(count):
        at = lax.rem(x + count - k, count) * 2
        group[at + c] = own_ref[k]
        group[at + 1 - c] = other_ref[k]
    whole = group[...].reshape(2 * count * rows, width)
    out_ref[...] = jnp.dot(whole, w_ref[...], preferred_element_type=F32).astype(BF16)


def project_kernel(model_width, order, ids, *refs):
    pieces, (gain_ref, wq_ref, wk_ref, wv_ref), outs = refs[:8], refs[8:12], refs[12:24]
    held, accq, acck, accv, square, heads = refs[24:]
    to_kv, to_q, qkv_refs, rinv_ref = outs[:4], outs[4:8], outs[8:11], outs[11]
    i = pl.program_id(0)

    @pl.when(i == 0)
    def _():
        for k, piece in enumerate(pieces):
            held[k] = piece[...]
        accq[...] = jnp.zeros_like(accq)
        acck[...] = jnp.zeros_like(acck)
        accv[...] = jnp.zeros_like(accv)
        square[...] = jnp.zeros_like(square)

    wide = held[i].astype(F32)
    squares = wide * wide
    square[...] += (
        squares[:, :128] + squares[:, 128:256] + squares[:, 256:384] + squares[:, 384:512]
    )
    scaled = (wide * gain_ref[...]).astype(BF16)
    accq[...] += jnp.dot(scaled, wq_ref[...], preferred_element_type=F32)
    acck[...] += jnp.dot(scaled, wk_ref[...], preferred_element_type=F32)
    accv[...] += jnp.dot(scaled, wv_ref[...], preferred_element_type=F32)

    @pl.when(i == pl.num_programs(0) - 1)
    def _():
        y = ids[2]
        total = jnp.sum(square[...], axis=1, keepdims=True)
        rinv = lax.rsqrt(total / model_width + EPS)
        rinv_ref[...] = rinv
        for n, acc in enumerate((accq, acck, accv)):
            rounded = (rinv * acc[...]).astype(BF16)
            qkv_refs[n][...] = rounded
            for h in range(4):
                heads[n * 4 + h] = rounded[:, h * HEAD : (h + 1) * HEAD]
        for k in range(4):
            h = lax.rem(y + k, 4)
            to_q[k][...] = heads[h]
            to_kv[k][:, :HEAD] = heads[4 + h]
            to_kv[k][:, HEAD:] = heads[8 + h]


def project(ids, order, pieces, gain, w_query, w_key, w_value):
    rows, columns = pieces[0].shape
    width = gain.shape[1]
    fixed = lambda *dims: pl.BlockSpec(dims, lambda i, order, ids: (0,) * len(dims))
    weight = pl.BlockSpec((columns, columns), lambda i, order, ids: (order[i], 0))
    outs = (
        [shape(rows, 2 * HEAD)] * 4
        + [shape(rows, HEAD)] * 4
        + [shape(rows, columns)] * 3
        + [shape(rows, 1, dtype=F32)]
    )
    return pl.pallas_call(
        functools.partial(project_kernel, width),
        grid_spec=pltpu.PrefetchScalarGridSpec(
            num_scalar_prefetch=2,
            grid=(8,),
            in_specs=[fixed(rows, columns)] * 8
            + [pl.BlockSpec((1, columns), lambda i, order, ids: (0, order[i]))]
            + [weight] * 3,
            out_specs=[fixed(*o.shape) for o in outs],
            scratch_shapes=[pltpu.VMEM((8, rows, columns), BF16)]
            + [pltpu.VMEM((rows, columns), F32)] * 3
            + [pltpu.VMEM((rows, 128), F32), pltpu.VMEM((12, rows, HEAD), BF16)],
        ),
        out_shape=outs,
        compiler_params=PARAMS,
        name="project",
    )(order, ids, *pieces, gain, w_query, w_key, w_value)


def d_attn_kernel(ids, valid_ref, grad_ref, w_ref, *refs):
    outs, (acc, heads) = refs[:4], refs[4:]
    i = pl.program_id(0)

    @pl.when(i == 0)
    def _():
        acc[...] = jnp.zeros_like(acc)

    acc[...] += lax.dot_general(grad_ref[0], w_ref[...], NT, preferred_element_type=F32)

    @pl.when(i == pl.num_programs(0) - 1)
    def _():
        y = ids[2]
        rounded = jnp.where(valid_ref[...] > 0.0, acc[...], 0.0).astype(BF16)
        for h in range(4):
            heads[h] = rounded[:, h * HEAD : (h + 1) * HEAD]
        for k in range(4):
            outs[k][...] = heads[lax.rem(y + k, 4)]


def d_attn_parts(ids, valid, grads, w_out):
    count, rows, columns = grads.shape
    fixed = lambda *dims: pl.BlockSpec(dims, lambda i: (0,) * len(dims))
    return pl.pallas_call(
        d_attn_kernel,
        grid=(count,),
        in_specs=[
            SMEM,
            fixed(rows, 1),
            pl.BlockSpec((1, rows, columns), lambda i: (i, 0, 0)),
            pl.BlockSpec((columns, columns), lambda i: (0, i)),
        ],
        out_specs=[fixed(rows, HEAD)] * 4,
        out_shape=[shape(rows, HEAD)] * 4,
        scratch_shapes=[pltpu.VMEM((rows, columns), F32), pltpu.VMEM((4, rows, HEAD), BF16)],
        compiler_params=PARAMS,
        name="d_attn",
    )(ids, valid, grads, w_out)


def joined_kernel(ids, *refs):
    parts, out = refs[:4], refs[4]
    rows = parts[0].shape[0]
    for k in range(4):
        at = lax.rem(ids[2] + 4 - k, 4) * rows
        out[pl.ds(pl.multiple_of(at, rows), rows), :] = parts[k][...]


def joined(ids, parts):
    rows, columns = parts[0].shape
    return call(joined_kernel, (ids, *parts), [shape(4 * rows, columns)], name="joined")[0]


def forward_kernel(ids, bias_ref, q_ref, do_ref, *refs):
    kvs, to_attn, to_dq, stats_ref = refs[:4], refs[4:8], refs[8:12], refs[12]
    scores, held_attn, held_dq = refs[13:]
    y, z = ids[2], ids[3]
    rows = 256
    eye = eye_of(rows)
    below = lax.broadcasted_iota(jnp.int32, (rows, rows), 1) <= lax.broadcasted_iota(
        jnp.int32, (rows, rows), 0
    )
    stats_ref[...] = jnp.zeros_like(stats_ref)
    for big in range(4):
        at = slice(big * rows, (big + 1) * rows)
        q = q_ref[at, :]
        do = do_ref[at, :]
        top = jnp.full((rows, rows), NEG, F32)
        for k in range(4):
            other = lax.rem(z + 4 - k, 4)
            for small in range(big + 1):
                keys = kvs[k][small * rows : (small + 1) * rows, :HEAD]
                s = lax.dot_general(q, keys, NT, preferred_element_type=F32)
                row = bias_ref[pl.ds(4 * small + other, 1), :]
                if small == big and k > 0:
                    row = row + jnp.where(z >= k, 0.0, NEG)
                s = s + row
                if small == big and k == 0:
                    s = jnp.where(below, s, NEG)
                scores[k * 4 + small] = s
                top = jnp.maximum(top, s)
        peak = jnp.max(top, axis=1, keepdims=True)
        sums = jnp.zeros((rows, rows), F32)
        mixed = jnp.zeros((rows, HEAD), F32)
        for k in range(4):
            for small in range(big + 1):
                p = jnp.exp2((scores[k * 4 + small] - peak) * EXP2_SCALE)
                sums = sums + p
                scores[k * 4 + small] = p
                values = kvs[k][small * rows : (small + 1) * rows, HEAD:]
                mixed = mixed + jnp.dot(p.astype(BF16), values, preferred_element_type=F32)
        total = jnp.sum(sums, axis=1, keepdims=True)
        inverse = 1.0 / total
        attn = (mixed * inverse).astype(BF16)
        held_attn[big] = attn
        delta = jnp.sum(do.astype(F32) * attn.astype(F32), axis=1, keepdims=True)
        dq = jnp.zeros((rows, HEAD), F32)
        for k in range(4):
            for small in range(big + 1):
                span = slice(small * rows, (small + 1) * rows)
                dp = lax.dot_general(do, kvs[k][span, HEAD:], NT, preferred_element_type=F32)
                ds = (scores[k * 4 + small] * (dp - delta)).astype(BF16)
                dq = dq + jnp.dot(ds, kvs[k][span, :HEAD], preferred_element_type=F32)
        held_dq[big] = (dq * (inverse * SCALE)).astype(BF16)
        stats_ref[0:1, at] = as_row(peak * EXP2_SCALE + jnp.log2(total), eye)
        stats_ref[1:2, at] = as_row(delta, eye)
    for k in range(4):
        to_attn[k][...] = held_attn[lax.rem(y + k, 4)]
        to_dq[k][...] = held_dq[lax.rem(y + k, 4)]


def forward(ids, bias, q, do, kvs):
    rows = q.shape[0] // 4
    return call(
        forward_kernel,
        (ids, bias, q, do, *kvs),
        [shape(rows, HEAD)] * 8 + [shape(8, 4 * rows, dtype=F32)],
        [pltpu.VMEM((16, rows, rows), F32)] + [pltpu.VMEM((4, rows, HEAD), BF16)] * 2,
        name="attention",
    )


def key_grad_kernel(ids, bias_ref, kv_ref, *refs):
    qs, dos, stats, outs, held = refs[:4], refs[4:8], refs[8:12], refs[12:16], refs[16]
    y, z = ids[2], ids[3]
    rows = 256
    eye = eye_of(rows)
    above = lax.broadcasted_iota(jnp.int32, (rows, rows), 0) <= lax.broadcasted_iota(
        jnp.int32, (rows, rows), 1
    )
    for small in range(4):
        keys = kv_ref[small * rows : (small + 1) * rows, :HEAD]
        values = kv_ref[small * rows : (small + 1) * rows, HEAD:]
        dk = jnp.zeros((rows, HEAD), F32)
        dv = jnp.zeros((rows, HEAD), F32)
        for k in range(4):
            for big in range(small, 4):
                at = slice(big * rows, (big + 1) * rows)
                q, do = qs[k][at, :], dos[k][at, :]
                level = stats[k][0:1, at]
                if big == small and k > 0:
                    level = level + jnp.where(z < k, 0.0, -NEG)
                s = lax.dot_general(keys, q, NT, preferred_element_type=F32)
                p = jnp.exp2(s * EXP2_SCALE - level)
                if big == small and k == 0:
                    p = jnp.where(above, p, 0.0)
                dv = dv + jnp.dot(p.astype(BF16), do, preferred_element_type=F32)
                dp = lax.dot_general(values, do, NT, preferred_element_type=F32)
                ds = (p * (dp - stats[k][1:2, at])).astype(BF16)
                dk = dk + jnp.dot(ds, q, preferred_element_type=F32)
        kept = as_column(bias_ref[pl.ds(4 * small + z, 1), :], eye) == 0.0
        held[small, :, :HEAD] = jnp.where(kept, dk * SCALE, 0.0).astype(BF16)
        held[small, :, HEAD:] = jnp.where(kept, dv, 0.0).astype(BF16)
    for k in range(4):
        outs[k][...] = held[lax.rem(y + k, 4)]


def key_grads(ids, bias, kv, qs, dos, stats):
    rows = kv.shape[0] // 4
    return call(
        key_grad_kernel,
        (ids, bias, kv, *qs, *dos, *stats),
        [shape(rows, 2 * HEAD)] * 4,
        [pltpu.VMEM((4, rows, 2 * HEAD), BF16)],
        name="key_grad",
    )


def out_kernel(ids, *refs):
    parts, w_ref, out_ref, wide = refs[:4], refs[4], refs[5], refs[6]

    @pl.when(pl.program_id(0) == 0)
    def _():
        for k in range(4):
            at = pl.multiple_of(lax.rem(ids[2] + 4 - k, 4) * HEAD, HEAD)
            wide[:, pl.ds(at, HEAD)] = parts[k][...]

    out_ref[0] = jnp.dot(wide[...], w_ref[...], preferred_element_type=F32).astype(BF16)


def out_partials(ids, parts, w_out):
    rows = parts[0].shape[0]
    columns, width = w_out.shape
    fixed = lambda *dims: pl.BlockSpec(dims, lambda i: (0,) * len(dims))
    return pl.pallas_call(
        out_kernel,
        grid=(width // columns,),
        in_specs=[SMEM]
        + [fixed(rows, HEAD)] * 4
        + [pl.BlockSpec((columns, columns), lambda i: (0, i))],
        out_specs=pl.BlockSpec((1, rows, columns), lambda i: (i, 0, 0)),
        out_shape=shape(width // columns, rows, columns),
        scratch_shapes=[pltpu.VMEM((rows, columns), BF16)],
        compiler_params=PARAMS,
        name="out_partial",
    )(ids, *parts, w_out)


def input_grad_kernel(model_width, order, ids, *refs):
    dqs, dkvs, qkv, rinv_ref, lats = refs[:4], refs[4:8], refs[8:11], refs[11], refs[12:16]
    gain_ref, wq_ref, wk_ref, wv_ref, out_ref = refs[16:21]
    gq, gk, gv, held, factor = refs[21:]
    i = pl.program_id(0)

    @pl.when(i == 0)
    def _():
        for k in range(4):
            held[k] = lats[k][...]
            at = pl.multiple_of(lax.rem(ids[2] + 4 - k, 4) * HEAD, HEAD)
            gq[:, pl.ds(at, HEAD)] = dqs[k][...]
            gk[:, pl.ds(at, HEAD)] = dkvs[k][:, :HEAD]
            gv[:, pl.ds(at, HEAD)] = dkvs[k][:, HEAD:]
        both = (
            gq[...].astype(F32) * qkv[0][...].astype(F32)
            + gk[...].astype(F32) * qkv[1][...].astype(F32)
            + gv[...].astype(F32) * qkv[2][...].astype(F32)
        )
        factor[...] = jnp.sum(both, axis=1, keepdims=True) * rinv_ref[...] / model_width

    acc = lax.dot_general(gq[...], wq_ref[...], NT, preferred_element_type=F32)
    acc = acc + lax.dot_general(gk[...], wk_ref[...], NT, preferred_element_type=F32)
    acc = acc + lax.dot_general(gv[...], wv_ref[...], NT, preferred_element_type=F32)
    out_ref[0] = (gain_ref[...] * acc - held[i].astype(F32) * factor[...]).astype(BF16)


def input_grads(ids, order, dqs, dkvs, qkv, rinv, lats, gain, w_query, w_key, w_value):
    rows, columns = lats[0].shape
    width = gain.shape[1]
    fixed = lambda *dims: pl.BlockSpec(dims, lambda i, order, ids: (0,) * len(dims))
    weight = pl.BlockSpec((columns, columns), lambda i, order, ids: (order[i], 0))
    return pl.pallas_call(
        functools.partial(input_grad_kernel, width),
        grid_spec=pltpu.PrefetchScalarGridSpec(
            num_scalar_prefetch=2,
            grid=(4,),
            in_specs=[fixed(rows, HEAD)] * 4
            + [fixed(rows, 2 * HEAD)] * 4
            + [fixed(rows, columns)] * 3
            + [fixed(rows, 1)]
            + [fixed(rows, columns)] * 4
            + [pl.BlockSpec((1, columns), lambda i, order, ids: (0, order[i]))]
            + [weight] * 3,
            out_specs=pl.BlockSpec((1, rows, columns), lambda i, order, ids: (i, 0, 0)),
            scratch_shapes=[pltpu.VMEM((rows, columns), BF16)] * 3
            + [pltpu.VMEM((4, rows, columns), BF16), pltpu.VMEM((rows, 1), F32)],
        ),
        out_shape=shape(4, rows, columns),
        compiler_params=PARAMS,
        name="input_grad",
    )(order, ids, *dqs, *dkvs, *qkv, rinv, *lats, gain, w_query, w_key, w_value)


def per_device(encoded, starts, w_up, norm_gain, w_query, w_key, w_value, w_out, cotangent):
    byte_rows, byte_width = encoded.shape
    patch_cap = starts.shape[1]
    columns = w_up.shape[1]
    rows = cotangent.shape[0]
    x, c, y, z = (lax.axis_index(a) for a in ("x", "c", "y", "z"))
    shard = lax.axis_index(ALL)
    ids = jnp.stack([x, c, y, z, shard]).astype(jnp.int32)
    steps = jnp.arange(4, dtype=jnp.int32)
    before = lax.rem(x + 4 - steps, 4) * 2
    beyond = lax.rem(x + steps, 4) * 2
    arrival = jnp.concatenate([before + c, before + 1 - c]).astype(jnp.int32)
    gain = norm_gain.reshape(1, -1)
    is_valid = (starts < byte_rows).reshape(-1, rows)
    bias = jnp.where(is_valid, 0.0, NEG).astype(F32)
    row_valid = lax.dynamic_slice_in_dim(is_valid, lax.axis_index(SEQ), 1, 0)
    valid = row_valid.reshape(rows, 1).astype(F32)

    cot_all = lax.all_gather(cotangent, TP)

    sums, lead = call(
        pool_kernel,
        (ids, starts, encoded),
        [shape(patch_cap, byte_width, dtype=F32), shape(1, byte_width, dtype=F32)],
        name="pool",
    )
    shards = starts.shape[0]
    next_lead = lax.ppermute(lead, ALL, [(i, i - 1) for i in range(1, shards)])
    patches = call(
        functools.partial(patch_kernel, byte_rows),
        (ids, starts, sums, next_lead),
        [shape(patch_cap, byte_width)],
        name="patch",
    )[0]
    own_core = jnp.stack(spread(patches, "x"))
    other_core = moved(own_core, "c", 1)
    latent = call(
        latent_kernel,
        (ids, own_core, other_core, w_up),
        [shape(rows, columns)],
        [pltpu.VMEM((8, patch_cap, byte_width), BF16)],
        name="latent",
    )[0]

    own_lats = spread(latent, "x")
    other_lats = [moved(a, "c", 1) for a in own_lats]
    projected = project(
        ids, arrival, own_lats + other_lats, gain, w_query, w_key, w_value
    )
    to_kv, to_q, qkv, rinv = projected[:4], projected[4:8], projected[8:11], projected[11]

    kv = joined(ids, exchanged(to_kv, "y"))
    kvs = spread(kv, "z")
    q = joined(ids, exchanged(to_q, "y"))
    do = joined(ids, exchanged(d_attn_parts(ids, valid, cot_all, w_out), "y"))
    dos = spread(do, "z")
    qs = spread(q, "z")

    made = forward(ids, bias, q, do, kvs)
    to_attn, to_dq, stats = made[:4], made[4:8], made[8]
    all_stats = spread(stats, "z")
    dkvs = exchanged(key_grads(ids, bias, kv, qs, dos, all_stats), "y")
    dqs = exchanged(to_dq, "y")
    attns = exchanged(to_attn, "y")

    partial_out = out_partials(ids, attns, w_out)
    mixed = lax.psum_scatter(partial_out, TP, scatter_dimension=0, tiled=False)
    result = latent.astype(F32) + mixed.astype(F32)
    latent_out = jnp.where(valid > 0.0, result, 0.0).astype(BF16)

    back = lambda lats: [lats[0], lats[3], lats[2], lats[1]]
    gains = (gain, w_query, w_key, w_value)
    for_other = input_grads(
        ids, (beyond + 1 - c).astype(jnp.int32), dqs, dkvs, qkv, rinv, back(other_lats), *gains
    )
    from_other = moved(for_other, "c", 1)
    for_own = input_grads(
        ids, (beyond + c).astype(jnp.int32), dqs, dkvs, qkv, rinv, back(own_lats), *gains
    )
    summed = for_own.astype(F32) + from_other.astype(F32)
    arrived = exchanged([summed[k].astype(BF16) for k in range(4)], "x")
    normed = summed[0] + sum(a.astype(F32) for a in arrived[1:])
    grad_out = jnp.where(valid > 0.0, cotangent.astype(F32), 0.0)
    latent_grad = grad_out + rinv * normed
    return latent_out, latent_grad


def solution(mesh):
    split = Mesh(mesh.devices.reshape(4, 4, 4, 2), ALL)
    in_specs = (
        P(ALL, None),
        P(),
        P(None, TP),
        P(),
        P(None, TP),
        P(None, TP),
        P(None, TP),
        P(TP, None),
        P(SEQ, TP),
    )
    out_specs = (P(SEQ, TP), P(SEQ, TP))
    return jax.shard_map(
        per_device, mesh=split, in_specs=in_specs, out_specs=out_specs, check_vma=False
    )
```

```python
import functools

import jax
import jax.numpy as jnp
from jax import lax
from jax.experimental import pallas as pl
from jax.experimental.pallas import tpu as pltpu
from jax.sharding import Mesh
from jax.sharding import PartitionSpec as P

HEAD = 128
SEQ = ("y", "z")
TP = ("x", "c")
ALL = ("y", "z", "x", "c")
EPS = 1e-05
NEG = -1e30
SCALE = HEAD ** (-0.5)
LOG2E = 1.4426950408889634
EXP2_SCALE = SCALE * LOG2E
F32 = jnp.float32
BF16 = jnp.bfloat16
NT = (((1,), (1,)), ((), ()))
TN = (((0,), (0,)), ((), ()))
VMEM = pl.BlockSpec(memory_space=pltpu.VMEM)
YZC = ("y", "z", "c")
XC = ("x", "c")


def shape(*dims, dtype=BF16):
    return jax.ShapeDtypeStruct(dims, dtype)


def call(kernel, ins, outs, scratch=(), name=None, megabytes=8, micros=1.0):
    return pl.pallas_call(
        kernel,
        in_specs=[VMEM] * len(ins),
        out_specs=[VMEM] * len(outs),
        out_shape=list(outs),
        scratch_shapes=list(scratch),
        compiler_params=pltpu.CompilerParams(vmem_limit_bytes=megabytes * 1024 * 1024),
        cost_estimate=pl.CostEstimate(
            flops=int(micros * 1e9), transcendentals=0, bytes_accessed=int(micros * 3e6)
        ),
        name=name,
    )(*ins)


def place(axis):
    return lax.axis_index(axis)


def other_core(block):
    return lax.ppermute(block, "c", [(0, 1), (1, 0)])


def to_head_owner(block, j):
    route = []
    for y in range(4):
        for z in range(4):
            for c in range(2):
                target = ((y + j) % 4) * 8 + ((z + j * c) % 4) * 2 + c
                route.append((y * 8 + z * 2 + c, target))
    return lax.ppermute(block, YZC, route)


def along_ring(block, j):
    route = []
    for y in range(4):
        for z in range(4):
            for c in range(2):
                ahead = ((y + j * c) % 4) * 8 + ((z + j * (1 - c)) % 4) * 2 + c
                route.append((y * 8 + z * 2 + c, ahead))
    return lax.ppermute(block, YZC, route)


def along_x(block):
    route = []
    for x in range(4):
        for c in range(2):
            route.append((x * 2 + c, ((x + 1 - 2 * c) % 4) * 2 + c))
    return lax.ppermute(block, XC, route)


def to_head_owners(parts):
    return [parts[0]] + [to_head_owner(parts[j], j) for j in range(1, 4)]


def gathered(low, high):
    low1, high3 = along_ring(low, 1), along_ring(high, 3)
    high1, low3 = along_ring(high, 1), along_ring(low, 3)
    low2, high2 = along_ring(low1, 1), along_ring(high3, 3)
    return [low, high, low1, high1, low2, high2, low3, high3]


def chunk(j=0):
    y, z, c = place("y"), place("z"), place("c")
    return jnp.where(c == 0, lax.rem(z + 4 - j, 4), lax.rem(z + 4 - y + j, 4))


def block_of(group, sub):
    return jnp.where(place("c") == 0, group, lax.rem(group + sub, 4))


def head_of():
    return jnp.where(place("c") == 0, place("y"), place("z"))


def bounds(starts_ref, shard, byte_rows):
    row = starts_ref[pl.ds(shard, 1), :]
    end = jnp.full((1, 1), byte_rows, jnp.int32)
    return row, jnp.concatenate([row[:, 1:], end], axis=1)


def pool_kernel(starts_ref, enc_ref, sums_ref, lead_ref):
    byte_rows = enc_ref.shape[0]
    cap = starts_ref.shape[1]
    row, following = bounds(starts_ref, place(ALL), byte_rows)
    places = lax.broadcasted_iota(jnp.int32, (byte_rows, cap), 0)
    inside = ((places >= row) & (places < following)).astype(F32).astype(BF16)
    enc = enc_ref[...]
    sums_ref[...] = lax.dot_general(inside, enc, TN, preferred_element_type=F32)
    leading = (places < row[:, :1]).astype(F32).astype(BF16)
    lead = lax.dot_general(leading, enc, TN, preferred_element_type=F32)
    lead_ref[...] = lead[:1]


def as_column(row, eye):
    return jnp.sum(jnp.where(eye, row, 0.0), axis=1, keepdims=True)


def as_row(column, eye):
    return jnp.sum(jnp.where(eye, column, 0.0), axis=0, keepdims=True)


def eye_of(n):
    return lax.broadcasted_iota(jnp.int32, (n, n), 0) == lax.broadcasted_iota(jnp.int32, (n, n), 1)


def patch_kernel(byte_rows, starts_ref, sums_ref, next_ref, out_ref):
    shards, cap = starts_ref.shape
    shard = place(ALL)
    row, following = bounds(starts_ref, shard, byte_rows)
    count = jnp.sum((row < byte_rows).astype(F32), axis=1, keepdims=True)
    slot = lax.broadcasted_iota(jnp.int32, (1, cap), 1).astype(F32)
    last = (slot == count - 1.0).astype(F32)
    after = starts_ref[pl.ds(jnp.minimum(shard + 1, shards - 1), 1), :][:, :1].astype(F32)
    after = jnp.where(shard + 1 < shards, after, 0.0)
    sizes = (following - row).astype(F32) + last * after
    eye = eye_of(cap)
    total = sums_ref[...] + as_column(last, eye) * next_ref[...]
    out_ref[...] = (total / as_column(jnp.maximum(sizes, 1.0), eye)).astype(BF16)


def latent_kernel(own_ref, other_ref, w_ref, out_ref, group):
    x, c = place("x"), place("c")
    count, rows, width = own_ref.shape
    for k in range(count):
        at = lax.rem(x + count - k, count) * 2
        group[at + c] = own_ref[k]
        group[at + 1 - c] = other_ref[k]
    whole = group[...].reshape(2 * count * rows, width)
    out_ref[...] = jnp.dot(whole, w_ref[...], preferred_element_type=F32).astype(BF16)


def tp_places():
    x, c = place("x"), place("c")
    back = lax.rem(x + 3 + 2 * c, 4) * 2
    ahead = lax.rem(x + 1 + 2 * c, 4) * 2
    far = lax.rem(x + 2, 4) * 2
    o = 1 - c
    return [2 * x + c, 2 * x + o, back + c, back + o, ahead + o, ahead + c, far + c, far + o]


def piece_rows(ref, at, size):
    return ref[pl.ds(pl.multiple_of(at * size, size), size), :]


def project_kernel(*refs):
    pieces, (gain_ref, wq_ref, wk_ref, wv_ref), outs = refs[:8], refs[8:12], refs[12:24]
    accs, heads = refs[24:27], refs[27]
    to_kv, to_q, qkv_refs, rinv_ref = outs[:4], outs[4:8], outs[8:11], outs[11]
    rows, size = pieces[0].shape
    width = gain_ref.shape[1]
    square = jnp.zeros((rows, 128), F32)
    for n, (piece, at) in enumerate(zip(pieces, tp_places())):
        wide = piece[...].astype(F32)
        squares = wide * wide
        for part in range(0, size, 128):
            square = square + squares[:, part : part + 128]
        gain = gain_ref[:, pl.ds(pl.multiple_of(at * size, size), size)]
        scaled = (wide * gain).astype(BF16)
        for acc, w_ref in zip(accs, (wq_ref, wk_ref, wv_ref)):
            made = jnp.dot(scaled, piece_rows(w_ref, at, size), preferred_element_type=F32)
            acc[...] = made if n == 0 else acc[...] + made
    total = jnp.sum(square, axis=1, keepdims=True)
    rinv = lax.rsqrt(total / width + EPS)
    rinv_ref[...] = rinv
    for n, acc in enumerate(accs):
        rounded = (rinv * acc[...]).astype(BF16)
        qkv_refs[n][...] = rounded
        for h in range(4):
            heads[n * 4 + h] = rounded[:, h * HEAD : (h + 1) * HEAD]
    first = head_of()
    for k in range(4):
        h = lax.rem(first + k, 4)
        to_q[k][...] = heads[h]
        to_kv[k][:, :HEAD] = heads[4 + h]
        to_kv[k][:, HEAD:] = heads[8 + h]


def project(pieces, gain, w_query, w_key, w_value):
    rows, size = pieces[0].shape
    outs = (
        [shape(rows, 2 * HEAD)] * 4
        + [shape(rows, HEAD)] * 4
        + [shape(rows, size)] * 3
        + [shape(rows, 1, dtype=F32)]
    )
    return call(
        project_kernel,
        (*pieces, gain, w_query, w_key, w_value),
        outs,
        [pltpu.VMEM((rows, size), F32)] * 3 + [pltpu.VMEM((12, rows, HEAD), BF16)],
        name="project",
        megabytes=24,
        micros=4.0,
    )


def d_attn_kernel(valid_ref, grads_ref, w_ref, *refs):
    outs, (acc, heads) = refs[:4], refs[4:]
    count, rows, size = grads_ref.shape
    for t in range(count):
        w = w_ref[:, t * size : (t + 1) * size]
        made = lax.dot_general(grads_ref[t], w, NT, preferred_element_type=F32)
        acc[...] = made if t == 0 else acc[...] + made
    rounded = jnp.where(valid_ref[...] > 0.0, acc[...], 0.0).astype(BF16)
    for h in range(4):
        heads[h] = rounded[:, h * HEAD : (h + 1) * HEAD]
    first = head_of()
    for k in range(4):
        outs[k][...] = heads[lax.rem(first + k, 4)]


def d_attn_parts(valid, grads, w_out):
    rows, size = grads.shape[1:]
    return call(
        d_attn_kernel,
        (valid, grads, w_out),
        [shape(rows, HEAD)] * 4,
        [pltpu.VMEM((rows, size), F32), pltpu.VMEM((4, rows, HEAD), BF16)],
        name="d_attn",
        megabytes=12,
        micros=2.0,
    )


def joined_kernel(*refs):
    parts, (low, high), held = refs[:4], refs[4:6], refs[6]
    rows = parts[0].shape[0]
    for j in range(4):
        held[lax.rem(place("y") + 4 - j, 4)] = parts[j][...]
    for half, out in enumerate((low, high)):
        for n in range(2):
            out[n * rows : (n + 1) * rows, :] = held[2 * half + n]


def joined(parts):
    rows, columns = parts[0].shape
    return call(
        joined_kernel,
        parts,
        [shape(2 * rows, columns)] * 2,
        [pltpu.VMEM((4, rows, columns), BF16)],
        name="joined",
        megabytes=4,
    )


def forward_kernel(bias_ref, *refs):
    qs, dos, kvs = refs[:2], refs[2:4], refs[4:12]
    to_attn, to_dq, stats_ref = refs[12:16], refs[16:20], refs[20]
    scores, held_attn, held_dq = refs[21:]
    rows = 256
    eye = eye_of(rows)
    below = lax.broadcasted_iota(jnp.int32, (rows, rows), 1) <= lax.broadcasted_iota(
        jnp.int32, (rows, rows), 0
    )
    groups = [chunk(j) for j in range(4)]

    def kv_of(j, small):
        at = (small % 2) * rows
        return kvs[2 * j + small // 2].at[at : at + rows, :]

    stats_ref[...] = jnp.zeros_like(stats_ref)
    for big in range(4):
        at = slice(big * rows, (big + 1) * rows)
        half = slice((big % 2) * rows, (big % 2 + 1) * rows)
        q = qs[big // 2][half, :]
        do = dos[big // 2][half, :]
        top = jnp.full((rows, rows), NEG, F32)
        mine = block_of(groups[0], big)
        for k in range(4):
            for small in range(big + 1):
                keys = kv_of(k, small)[:, :HEAD]
                s = lax.dot_general(q, keys, NT, preferred_element_type=F32)
                offset = block_of(groups[k], small)
                row = bias_ref[pl.ds(4 * small + offset, 1), :]
                if small == big and k > 0:
                    row = row + jnp.where(offset < mine, 0.0, NEG)
                s = s + row
                if small == big and k == 0:
                    s = jnp.where(below, s, NEG)
                scores[k * 4 + small] = s
                top = jnp.maximum(top, s)
        peak = jnp.max(top, axis=1, keepdims=True)
        sums = jnp.zeros((rows, rows), F32)
        mixed = jnp.zeros((rows, HEAD), F32)
        for k in range(4):
            for small in range(big + 1):
                p = jnp.exp2((scores[k * 4 + small] - peak) * EXP2_SCALE)
                sums = sums + p
                scores[k * 4 + small] = p
                values = kv_of(k, small)[:, HEAD:]
                mixed = mixed + jnp.dot(p.astype(BF16), values, preferred_element_type=F32)
        total = jnp.sum(sums, axis=1, keepdims=True)
        inverse = 1.0 / total
        attn = (mixed * inverse).astype(BF16)
        held_attn[big] = attn
        delta = jnp.sum(do.astype(F32) * attn.astype(F32), axis=1, keepdims=True)
        dq = jnp.zeros((rows, HEAD), F32)
        for k in range(4):
            for small in range(big + 1):
                kv = kv_of(k, small)
                dp = lax.dot_general(do, kv[:, HEAD:], NT, preferred_element_type=F32)
                ds = (scores[k * 4 + small] * (dp - delta)).astype(BF16)
                dq = dq + jnp.dot(ds, kv[:, :HEAD], preferred_element_type=F32)
        held_dq[big] = (dq * (inverse * SCALE)).astype(BF16)
        stats_ref[0:1, at] = as_row(peak * EXP2_SCALE + jnp.log2(total), eye)
        stats_ref[1:2, at] = as_row(delta, eye)
    for k in range(4):
        at = lax.rem(place("y") + k, 4)
        to_attn[k][...] = held_attn[at]
        to_dq[k][...] = held_dq[at]


def forward(bias, qs, dos, kvs):
    rows = qs[0].shape[0] // 2
    return call(
        forward_kernel,
        (bias, *qs, *dos, *kvs),
        [shape(rows, HEAD)] * 8 + [shape(8, 4 * rows, dtype=F32)],
        [pltpu.VMEM((16, rows, rows), F32)] + [pltpu.VMEM((4, rows, HEAD), BF16)] * 2,
        name="attention",
        megabytes=16,
        micros=9.0,
    )


def key_grad_kernel(bias_ref, *refs):
    kvs, qs, dos, stats = refs[:2], refs[2:10], refs[10:18], refs[18:22]
    outs, held = refs[22:26], refs[26]
    rows = 256
    eye = eye_of(rows)
    above = lax.broadcasted_iota(jnp.int32, (rows, rows), 0) <= lax.broadcasted_iota(
        jnp.int32, (rows, rows), 1
    )
    groups = [chunk(j) for j in range(4)]
    for small in range(4):
        half = slice((small % 2) * rows, (small % 2 + 1) * rows)
        keys = kvs[small // 2][half, :HEAD]
        values = kvs[small // 2][half, HEAD:]
        dk = jnp.zeros((rows, HEAD), F32)
        dv = jnp.zeros((rows, HEAD), F32)
        mine = block_of(groups[0], small)
        for k in range(4):
            for big in range(small, 4):
                at = slice(big * rows, (big + 1) * rows)
                part = slice((big % 2) * rows, (big % 2 + 1) * rows)
                q, do = qs[2 * k + big // 2][part, :], dos[2 * k + big // 2][part, :]
                level = stats[k][0:1, at]
                if big == small and k > 0:
                    level = level + jnp.where(mine < block_of(groups[k], big), 0.0, -NEG)
                s = lax.dot_general(keys, q, NT, preferred_element_type=F32)
                p = jnp.exp2(s * EXP2_SCALE - level)
                if big == small and k == 0:
                    p = jnp.where(above, p, 0.0)
                dv = dv + jnp.dot(p.astype(BF16), do, preferred_element_type=F32)
                dp = lax.dot_general(values, do, NT, preferred_element_type=F32)
                ds = (p * (dp - stats[k][1:2, at])).astype(BF16)
                dk = dk + jnp.dot(ds, q, preferred_element_type=F32)
        kept = as_column(bias_ref[pl.ds(4 * small + mine, 1), :], eye) == 0.0
        held[small, :, :HEAD] = jnp.where(kept, dk * SCALE, 0.0).astype(BF16)
        held[small, :, HEAD:] = jnp.where(kept, dv, 0.0).astype(BF16)
    for k in range(4):
        outs[k][...] = held[lax.rem(place("y") + k, 4)]


def key_grads(bias, kvs, qs, dos, stats):
    rows = kvs[0].shape[0] // 2
    return call(
        key_grad_kernel,
        (bias, *kvs, *qs, *dos, *stats),
        [shape(rows, 2 * HEAD)] * 4,
        [pltpu.VMEM((4, rows, 2 * HEAD), BF16)],
        name="key_grad",
        megabytes=12,
        micros=7.0,
    )


def head_columns(j):
    return pl.multiple_of(lax.rem(head_of() + 4 - j, 4) * HEAD, HEAD)


def out_kernel(*refs):
    parts, w_ref, out_ref, wide = refs[:4], refs[4], refs[5], refs[6]
    for j in range(4):
        wide[:, pl.ds(head_columns(j), HEAD)] = parts[j][...]
    count, _, size = out_ref.shape
    for t in range(count):
        w = w_ref[:, t * size : (t + 1) * size]
        out_ref[t] = jnp.dot(wide[...], w, preferred_element_type=F32).astype(BF16)


def out_partials(parts, w_out):
    rows = parts[0].shape[0]
    size, width = w_out.shape
    return call(
        out_kernel,
        (*parts, w_out),
        [shape(width // size, rows, size)],
        [pltpu.VMEM((rows, size), BF16)],
        name="out_partial",
        megabytes=12,
        micros=2.0,
    )[0]


def input_grad_kernel(which, *refs):
    dqs, dkvs, qkv, rinv_ref, lats = refs[:4], refs[4:8], refs[8:11], refs[11], refs[12:16]
    gain_ref, weights, out_ref, grads = refs[16], refs[17:20], refs[20], refs[21:]
    size = qkv[0].shape[1]
    width = gain_ref.shape[1]
    for j in range(4):
        at = head_columns(j)
        grads[0][:, pl.ds(at, HEAD)] = dqs[j][...]
        grads[1][:, pl.ds(at, HEAD)] = dkvs[j][:, :HEAD]
        grads[2][:, pl.ds(at, HEAD)] = dkvs[j][:, HEAD:]
    both = sum(g[...].astype(F32) * v[...].astype(F32) for g, v in zip(grads, qkv))
    factor = jnp.sum(both, axis=1, keepdims=True) * rinv_ref[...] / width
    places = tp_places()
    for n, kind in enumerate(which):
        at = places[kind]
        acc = sum(
            lax.dot_general(g[...], piece_rows(w, at, size), NT, preferred_element_type=F32)
            for g, w in zip(grads, weights)
        )
        gain = gain_ref[:, pl.ds(pl.multiple_of(at * size, size), size)]
        out_ref[n] = (gain * acc - lats[n][...].astype(F32) * factor).astype(BF16)


def input_grads(which, pieces, dqs, dkvs, qkv, rinv, gain, w_query, w_key, w_value):
    rows, size = pieces[0].shape
    lats = [pieces[kind] for kind in which]
    return call(
        functools.partial(input_grad_kernel, which),
        (*dqs, *dkvs, *qkv, rinv, *lats, gain, w_query, w_key, w_value),
        [shape(4, rows, size)],
        [pltpu.VMEM((rows, size), BF16)] * 3,
        name="input_grad",
        megabytes=24,
        micros=3.0,
    )[0]


def add_kernel(own_ref, other_ref, far_ref, side_ref, near_ref, kept_ref):
    for n, ref in enumerate((far_ref, near_ref, side_ref, kept_ref)):
        total = own_ref[n].astype(F32) + other_ref[n].astype(F32)
        ref[...] = total.astype(ref.dtype)


def final_kernel(valid_ref, rinv_ref, cot_ref, kept_ref, ahead_ref, side_ref, out_ref):
    total = kept_ref[...] + ahead_ref[...].astype(F32) + side_ref[...].astype(F32)
    grad_out = jnp.where(valid_ref[...] > 0.0, cot_ref[...].astype(F32), 0.0)
    out_ref[...] = grad_out + rinv_ref[...] * total


def per_device(encoded, starts, w_up, norm_gain, w_query, w_key, w_value, w_out, cotangent):
    byte_rows, byte_width = encoded.shape
    patch_cap = starts.shape[1]
    columns = w_up.shape[1]
    rows = cotangent.shape[0]
    gain = norm_gain.reshape(1, -1)
    is_valid = (starts < byte_rows).reshape(-1, rows)
    bias = jnp.where(is_valid, 0.0, NEG).astype(F32)
    row_valid = lax.dynamic_slice_in_dim(is_valid, lax.axis_index(SEQ), 1, 0)
    valid = row_valid.reshape(rows, 1).astype(F32)

    cot_all = lax.all_gather(cotangent, TP)

    sums, lead = call(
        pool_kernel,
        (starts, encoded),
        [shape(patch_cap, byte_width, dtype=F32), shape(1, byte_width, dtype=F32)],
        name="pool",
        megabytes=4,
    )
    shards = starts.shape[0]
    next_lead = lax.ppermute(lead, ALL, [(i, i - 1) for i in range(1, shards)])
    patches = call(
        functools.partial(patch_kernel, byte_rows),
        (starts, sums, next_lead),
        [shape(patch_cap, byte_width)],
        name="patch",
        megabytes=4,
    )[0]
    shifted = [lax.ppermute(patches, "x", [(i, (i + k) % 4) for i in range(4)]) for k in (1, 2, 3)]
    own_blocks = jnp.stack([patches, *shifted])
    latent = call(
        latent_kernel,
        (own_blocks, other_core(own_blocks), w_up),
        [shape(rows, columns)],
        [pltpu.VMEM((8, patch_cap, byte_width), BF16)],
        name="latent",
        megabytes=8,
    )[0]

    piece_a = along_x(latent)
    sibling = other_core(latent)
    piece_b = along_x(sibling)
    piece_f = along_x(piece_a)
    pieces = [latent, sibling, piece_a, piece_b]
    pieces += [other_core(piece_a), other_core(piece_b), piece_f, other_core(piece_f)]
    do_parts = d_attn_parts(valid, cot_all, w_out)
    pieces, do_parts = lax.optimization_barrier((pieces, do_parts))
    projected = project(pieces, gain, w_query, w_key, w_value)
    to_kv, to_q, qkv, rinv = projected[:4], projected[4:8], projected[8:11], projected[11]

    do_halves = joined(to_head_owners(do_parts))
    dos = gathered(*do_halves)
    kv_halves = joined(to_head_owners(to_kv))
    kv_halves, dos = lax.optimization_barrier((kv_halves, dos))
    kvs = gathered(*kv_halves)
    q_halves = joined(to_head_owners(to_q))
    qs = gathered(*q_halves)

    made = forward(bias, q_halves, do_halves, kvs)
    to_attn, to_dq, stats = made[:4], made[4:8], made[8]
    all_stats = [stats] + [along_ring(stats, j) for j in (1, 2, 3)]
    dkvs = to_head_owners(key_grads(bias, kv_halves, qs, dos, all_stats))
    dqs = to_head_owners(to_dq)
    attns = to_head_owners(to_attn)

    partial_out = out_partials(attns, w_out)
    mixed = lax.psum_scatter(partial_out, TP, scatter_dimension=0, tiled=False)
    result = latent.astype(F32) + mixed.astype(F32)
    latent_out = jnp.where(valid > 0.0, result, 0.0).astype(BF16)

    rest = (pieces, dqs, dkvs, qkv, rinv, gain, w_query, w_key, w_value)
    from_other = other_core(input_grads((7, 3, 2, 1), *rest))
    for_own = input_grads((6, 5, 4, 0), *rest)
    block = shape(rows, columns)
    far, side, near, kept = call(
        add_kernel,
        (for_own, from_other),
        [block, block, shape(rows, columns, dtype=F32), shape(rows, columns, dtype=F32)],
        name="add",
    )
    far_in = along_x(far)
    side_in = other_core(along_x(side))
    ahead_in = along_x((near + far_in.astype(F32)).astype(BF16))
    latent_grad = call(
        final_kernel,
        (valid, rinv, cotangent, kept, ahead_in, side_in),
        [shape(rows, columns, dtype=F32)],
        name="final",
    )[0]
    return latent_out, latent_grad


def solution(mesh):
    split = Mesh(mesh.devices.reshape(4, 4, 4, 2), ALL)
    in_specs = (
        P(ALL, None),
        P(),
        P(None, TP),
        P(),
        P(None, TP),
        P(None, TP),
        P(None, TP),
        P(TP, None),
        P(SEQ, TP),
    )
    out_specs = (P(SEQ, TP), P(SEQ, TP))
    return jax.shard_map(
        per_device, mesh=split, in_specs=in_specs, out_specs=out_specs, check_vma=False
    )
```

```python
import functools

import jax
import jax.numpy as jnp
from jax import lax
from jax.experimental import pallas as pl
from jax.experimental.pallas import tpu as pltpu
from jax.sharding import Mesh
from jax.sharding import PartitionSpec as P

HEAD = 128
SEQ = ("y", "z")
TP = ("x", "c")
ALL = ("y", "z", "x", "c")
EPS = 1e-05
NEG = -1e30
SCALE = HEAD ** (-0.5)
LOG2E = 1.4426950408889634
EXP2_SCALE = SCALE * LOG2E
F32 = jnp.float32
BF16 = jnp.bfloat16
NT = (((1,), (1,)), ((), ()))
TN = (((0,), (0,)), ((), ()))
VMEM = pl.BlockSpec(memory_space=pltpu.VMEM)
XC = ("x", "c")


def shape(*dims, dtype=BF16):
    return jax.ShapeDtypeStruct(dims, dtype)


def call(kernel, ins, outs, scratch=(), name=None, megabytes=8, micros=1.0, stay=0):
    return pl.pallas_call(
        kernel,
        in_specs=[VMEM] * (len(ins) - stay) + [pl.BlockSpec(memory_space=pl.ANY)] * stay,
        out_specs=[VMEM] * len(outs),
        out_shape=list(outs),
        scratch_shapes=list(scratch),
        compiler_params=pltpu.CompilerParams(vmem_limit_bytes=megabytes * 1024 * 1024),
        cost_estimate=pl.CostEstimate(
            flops=int(micros * 1e9), transcendentals=0, bytes_accessed=int(micros * 3e6)
        ),
        name=name,
    )(*ins)


def place(axis):
    return lax.axis_index(axis)


def other_core(block):
    return lax.ppermute(block, "c", [(0, 1), (1, 0)])


def along_x(block):
    route = []
    for x in range(4):
        for c in range(2):
            route.append((x * 2 + c, ((x + 1 - 2 * c) % 4) * 2 + c))
    return lax.ppermute(block, XC, route)


def bounds(starts_ref, shard, byte_rows):
    row = starts_ref[pl.ds(shard, 1), :]
    end = jnp.full((1, 1), byte_rows, jnp.int32)
    return row, jnp.concatenate([row[:, 1:], end], axis=1)


def pool_kernel(starts_ref, enc_ref, sums_ref, lead_ref):
    byte_rows = enc_ref.shape[0]
    cap = starts_ref.shape[1]
    row, following = bounds(starts_ref, place(ALL), byte_rows)
    places = lax.broadcasted_iota(jnp.int32, (byte_rows, cap), 0)
    inside = ((places >= row) & (places < following)).astype(F32).astype(BF16)
    enc = enc_ref[...]
    sums_ref[...] = lax.dot_general(inside, enc, TN, preferred_element_type=F32)
    leading = (places < row[:, :1]).astype(F32).astype(BF16)
    lead = lax.dot_general(leading, enc, TN, preferred_element_type=F32)
    lead_ref[...] = lead[:1]


def as_column(row, eye):
    return jnp.sum(jnp.where(eye, row, 0.0), axis=1, keepdims=True)


def as_row(column, eye):
    return jnp.sum(jnp.where(eye, column, 0.0), axis=0, keepdims=True)


def eye_of(n):
    return lax.broadcasted_iota(jnp.int32, (n, n), 0) == lax.broadcasted_iota(jnp.int32, (n, n), 1)


def patch_kernel(byte_rows, starts_ref, sums_ref, next_ref, out_ref):
    shards, cap = starts_ref.shape
    shard = place(ALL)
    row, following = bounds(starts_ref, shard, byte_rows)
    count = jnp.sum((row < byte_rows).astype(F32), axis=1, keepdims=True)
    slot = lax.broadcasted_iota(jnp.int32, (1, cap), 1).astype(F32)
    last = (slot == count - 1.0).astype(F32)
    after = starts_ref[pl.ds(jnp.minimum(shard + 1, shards - 1), 1), :][:, :1].astype(F32)
    after = jnp.where(shard + 1 < shards, after, 0.0)
    sizes = (following - row).astype(F32) + last * after
    eye = eye_of(cap)
    total = sums_ref[...] + as_column(last, eye) * next_ref[...]
    out_ref[...] = (total / as_column(jnp.maximum(sizes, 1.0), eye)).astype(BF16)


def latent_kernel(own_ref, other_ref, w_ref, out_ref, group):
    x, c = place("x"), place("c")
    count, rows, width = own_ref.shape
    for k in range(count):
        at = lax.rem(x + count - k, count) * 2
        group[at + c] = own_ref[k]
        group[at + 1 - c] = other_ref[k]
    whole = group[...].reshape(2 * count * rows, width)
    out_ref[...] = jnp.dot(whole, w_ref[...], preferred_element_type=F32).astype(BF16)


def tp_places():
    x, c = place("x"), place("c")
    back = lax.rem(x + 3 + 2 * c, 4) * 2
    ahead = lax.rem(x + 1 + 2 * c, 4) * 2
    far = lax.rem(x + 2, 4) * 2
    o = 1 - c
    return [2 * x + c, 2 * x + o, back + c, back + o, ahead + o, ahead + c, far + c, far + o]


def piece_rows(ref, at, size):
    return ref[pl.ds(pl.multiple_of(at * size, size), size), :]


def project_kernel(*refs):
    pieces, (do_ref, gain_ref), weights = refs[:8], refs[8:10], refs[10:13]
    outs, (held, sems, lats, accs, heads) = refs[13:19], refs[19:24]
    keep_ref, send_ref, qkv_refs, rinv_ref = outs[0], outs[1], outs[2:5], outs[5]
    rows, size = pieces[0].shape
    width = gain_ref.shape[1]
    c = place("c")
    places = tp_places()
    copies = []
    for t in range(8):
        for kind in range(3):
            part = weights[kind].at[t * size : (t + 1) * size, :]
            copies.append(pltpu.make_async_copy(part, held.at[t, kind], sems.at[t, kind]))
    for copy in copies:
        copy.start()
    for piece, at in zip(pieces, places):
        lats[at] = piece[...]
    for h in range(4):
        heads[12 + h] = do_ref[:, h * HEAD : (h + 1) * HEAD]
    square = jnp.zeros((rows, 128), F32)
    for t in range(8):
        wide = lats[t].astype(F32)
        squares = wide * wide
        for part in range(0, size, 128):
            square = square + squares[:, part : part + 128]
        scaled = (wide * gain_ref[:, t * size : (t + 1) * size]).astype(BF16)
        for kind in range(3):
            copies[3 * t + kind].wait()
            made = jnp.dot(scaled, held[t, kind], preferred_element_type=F32)
            accs[kind] = made if t == 0 else accs[kind] + made
    total = jnp.sum(square, axis=1, keepdims=True)
    rinv = lax.rsqrt(total / width + EPS)
    rinv_ref[...] = rinv
    for kind in range(3):
        rounded = (rinv * accs[kind]).astype(BF16)
        qkv_refs[kind][...] = rounded
        for h in range(4):
            heads[kind * 4 + h] = rounded[:, h * HEAD : (h + 1) * HEAD]
    half = rows // 2
    for out, which in ((keep_ref, c), (send_ref, 1 - c)):
        span = pl.ds(pl.multiple_of(which * half, half), half)
        for h in range(4):
            out[h, :half, :HEAD] = heads[4 + h, span, :]
            out[h, :half, HEAD:] = heads[8 + h, span, :]
            out[h, half:, :HEAD] = heads[h, span, :]
            out[h, half:, HEAD:] = heads[12 + h, span, :]


def project(pieces, d_attn, gain, weights):
    rows, size = pieces[0].shape
    both = shape(4, rows, 2 * HEAD)
    return call(
        project_kernel,
        (*pieces, d_attn, gain, *weights),
        [both, both] + [shape(rows, size)] * 3 + [shape(rows, 1, dtype=F32)],
        [
            pltpu.VMEM((8, 3, size, size), BF16),
            pltpu.SemaphoreType.DMA((8, 3)),
            pltpu.VMEM((8, rows, size), BF16),
            pltpu.VMEM((3, rows, size), F32),
            pltpu.VMEM((16, rows, HEAD), BF16),
        ],
        name="project",
        megabytes=28,
        micros=5.0,
        stay=3,
    )


def d_attn_kernel(*refs):
    grads, valid_ref, w_ref, out_ref, held, sems = refs[:8], *refs[8:]
    size = grads[0].shape[1]
    copies = []
    for h in range(4):
        span = slice(h * HEAD, (h + 1) * HEAD)
        copies.append(pltpu.make_async_copy(w_ref.at[span, :], held.at[span, :], sems.at[h]))
    for copy in copies:
        copy.start()
    valid = valid_ref[...] > 0.0
    places = tp_places()
    for h in range(4):
        copies[h].wait()
        span = slice(h * HEAD, (h + 1) * HEAD)
        acc = 0.0
        for piece, at in zip(grads, places):
            w = held[span, pl.ds(pl.multiple_of(at * size, size), size)]
            acc = acc + lax.dot_general(piece[...], w, NT, preferred_element_type=F32)
        out_ref[:, span] = jnp.where(valid, acc, 0.0).astype(BF16)


def d_attn_of(grads, valid, w_out):
    return call(
        d_attn_kernel,
        (*grads, valid, w_out),
        [shape(*grads[0].shape)],
        [pltpu.VMEM(w_out.shape, BF16), pltpu.SemaphoreType.DMA((4,))],
        name="d_attn",
        megabytes=12,
        micros=2.0,
        stay=1,
    )[0]


def pack_kernel(keep_ref, got_ref, out_ref):
    c = place("c")
    half = keep_ref.shape[1] // 2
    strip = half // 2
    for ref, core in ((keep_ref, c), (got_ref, 1 - c)):
        for h in range(4):
            for e in range(2):
                s = (core * 4 + h) * 2 + e
                out_ref[s, :half, :] = ref[h, :half, :]
                out_ref[s, half:, :] = ref[h, half + e * strip : half + (e + 1) * strip, :]


def attention_kernel(bias_ref, mine_ref, theirs_ref, keep_ref, send_ref, strip_ref, *scratch):
    scores, dks, dvs, biases = scratch
    c, e = place("c"), lax.rem(place("z"), 2)
    blocks = mine_ref.shape[0]
    half, strip, span, rows = 128, 64, 512, 256
    sources = (mine_ref, theirs_ref)

    def kv_of(side, u):
        ref = sources[side]
        keys = ref[4 * u : 4 * u + 4, :half, :HEAD].reshape(span, HEAD)
        return keys, ref[4 * u : 4 * u + 4, :half, HEAD:].reshape(span, HEAD)

    biases[0], biases[1] = bias_ref[c], bias_ref[1 - c]
    dks[...] = jnp.zeros_like(dks)
    dvs[...] = jnp.zeros_like(dvs)
    lane = lax.broadcasted_iota(jnp.int32, (1, rows), 1)
    place_q = (lane // strip) * 256 + lax.rem(lane, strip) + c * half + e * strip
    line = lax.broadcasted_iota(jnp.int32, (span, 1), 0)
    place_k = (line // half) * 256 + lax.rem(line, half)
    allowed = [place_k + which * half <= place_q for which in (c, 1 - c)]
    for t in range(4):
        q = mine_ref[4 * t : 4 * t + 4, half:, :HEAD].reshape(rows, HEAD)
        do = mine_ref[4 * t : 4 * t + 4, half:, HEAD:].reshape(rows, HEAD)
        peak = jnp.full((1, rows), NEG, F32)
        for side in range(2):
            for u in range(t + 1):
                keys, _ = kv_of(side, u)
                s = lax.dot_general(keys, q, NT, preferred_element_type=F32)
                bias = biases[side, u * span : (u + 1) * span, :]
                s = s + jnp.concatenate([bias, bias], axis=1)
                if u == t:
                    s = jnp.where(allowed[side], s, NEG)
                scores[side * 4 + u] = s
                peak = jnp.maximum(peak, jnp.max(s, axis=0, keepdims=True))
        total = jnp.zeros((1, rows), F32)
        mixed = jnp.zeros((HEAD, rows), F32)
        for side in range(2):
            for u in range(t + 1):
                _, values = kv_of(side, u)
                p = jnp.exp2((scores[side * 4 + u] - peak) * EXP2_SCALE)
                total = total + jnp.sum(p, axis=0, keepdims=True)
                scores[side * 4 + u] = p
                mixed = mixed + lax.dot_general(
                    values, p.astype(BF16), TN, preferred_element_type=F32
                )
        inverse = 1.0 / total
        attn = jnp.transpose(mixed * inverse).astype(BF16)
        products = do.astype(F32) * attn.astype(F32)
        delta = jnp.sum(jnp.transpose(products), axis=0, keepdims=True)
        dq = jnp.zeros((HEAD, rows), F32)
        for side in range(2):
            for u in range(t + 1):
                keys, values = kv_of(side, u)
                p = scores[side * 4 + u] * inverse
                dp = lax.dot_general(values, do, NT, preferred_element_type=F32)
                ds = (p * (dp - delta)).astype(BF16)
                at = slice(u * span, (u + 1) * span)
                dvs[side, at, :] += jnp.dot(p.astype(BF16), do, preferred_element_type=F32)
                dks[side, at, :] += jnp.dot(ds, q, preferred_element_type=F32)
                dq = dq + lax.dot_general(keys, ds, TN, preferred_element_type=F32)
        dq = jnp.transpose(dq * SCALE).astype(BF16)
        strip_ref[4 * t : 4 * t + 4, :, :HEAD] = dq.reshape(4, strip, HEAD)
        strip_ref[4 * t : 4 * t + 4, :, HEAD:] = attn.reshape(4, strip, HEAD)
    for side, ref in ((0, keep_ref), (1, send_ref)):
        ref[:, :, :HEAD] = (dks[side] * SCALE).astype(BF16).reshape(blocks, half, HEAD)
        ref[:, :, HEAD:] = dvs[side].astype(BF16).reshape(blocks, half, HEAD)


def attention(bias, mine, theirs):
    blocks, _, both = mine.shape
    grads = shape(blocks, 128, both)
    return call(
        attention_kernel,
        (bias, mine, theirs),
        [grads, grads, shape(blocks, 64, both)],
        [pltpu.VMEM((8, 512, 256), F32)] + [pltpu.VMEM((2, blocks * 128, HEAD), F32)] * 3,
        name="attention",
        megabytes=28,
        micros=12.0,
    )


def return_kernel(keep_ref, got_ref, strip_ref, out_ref):
    half = keep_ref.shape[1]
    out_ref[:, :half, :] = (keep_ref[...].astype(F32) + got_ref[...].astype(F32)).astype(BF16)
    out_ref[:, half:, :] = strip_ref[...]


def regroup_kernel(in_ref, keep_ref, send_ref):
    c = place("c")
    half, strip = 128, 64
    for out, core in ((keep_ref, c), (send_ref, 1 - c)):
        for h in range(4):
            s = (core * 4 + h) * 2
            total = in_ref[s, :half, :].astype(F32) + in_ref[s + 1, :half, :].astype(F32)
            out[h, :half, :] = total.astype(BF16)
            out[h, half : half + strip, :] = in_ref[s, half:, :]
            out[h, half + strip :, :] = in_ref[s + 1, half:, :]


def output_kernel(which, keep_ref, got_ref, *refs):
    qkv, rinv_ref, lats, gain_ref = refs[:3], refs[3], refs[4:8], refs[8]
    weights, w_out_ref, out_ref, wide = refs[9:12], refs[12], refs[13], refs[14]
    rows, size = qkv[0].shape
    width = gain_ref.shape[1]
    half = rows // 2
    c = place("c")
    for ref, core in ((keep_ref, c), (got_ref, 1 - c)):
        span = pl.ds(pl.multiple_of(core * half, half), half)
        for h in range(4):
            at = slice(h * HEAD, (h + 1) * HEAD)
            wide[0, span, at] = ref[h, half:, :HEAD]
            wide[1, span, at] = ref[h, :half, :HEAD]
            wide[2, span, at] = ref[h, :half, HEAD:]
            wide[3, span, at] = ref[h, half:, HEAD:]
    both = sum(wide[n].astype(F32) * qkv[n][...].astype(F32) for n in range(3))
    factor = jnp.sum(both, axis=1, keepdims=True) * rinv_ref[...] / width
    places = tp_places()
    for n, kind in enumerate(which):
        at = places[kind]
        acc = sum(
            lax.dot_general(
                wide[i], piece_rows(weights[i], at, size), NT, preferred_element_type=F32
            )
            for i in range(3)
        )
        columns = pl.ds(pl.multiple_of(at * size, size), size)
        grad = gain_ref[:, columns] * acc - lats[n][...].astype(F32) * factor
        out_ref[n, :rows, :] = grad.astype(BF16)
        mixed = jnp.dot(wide[3], w_out_ref[:, columns], preferred_element_type=F32)
        out_ref[n, rows:, :] = mixed.astype(BF16)


def outputs_for(which, pieces, keep, got, qkv, rinv, gain, weights, w_out):
    rows, size = pieces[0].shape
    lats = [pieces[kind] for kind in which]
    return call(
        functools.partial(output_kernel, which),
        (keep, got, *qkv, rinv, *lats, gain, *weights, w_out),
        [shape(4, 2 * rows, size)],
        [pltpu.VMEM((4, rows, size), BF16)],
        name="outputs",
        megabytes=28,
        micros=3.0,
    )[0]


def add_kernel(own_ref, other_ref, far_ref, side_ref, near_ref, kept_ref):
    for n, ref in enumerate((far_ref, near_ref, side_ref, kept_ref)):
        total = own_ref[n].astype(F32) + other_ref[n].astype(F32)
        ref[...] = total.astype(ref.dtype)


def pass_kernel(near_ref, far_ref, out_ref):
    out_ref[...] = (near_ref[...] + far_ref[...].astype(F32)).astype(BF16)


def final_kernel(valid_ref, rinv_ref, cot_ref, lat_ref, kept_ref, ahead_ref, side_ref, *outs):
    out_ref, grad_ref = outs
    rows = cot_ref.shape[0]
    total = kept_ref[...] + ahead_ref[...].astype(F32) + side_ref[...].astype(F32)
    valid = valid_ref[...] > 0.0
    grad_out = jnp.where(valid, cot_ref[...].astype(F32), 0.0)
    grad_ref[...] = grad_out + rinv_ref[...] * total[:rows]
    result = lat_ref[...].astype(F32) + total[rows:]
    out_ref[...] = jnp.where(valid, result, 0.0).astype(BF16)


def tp_pieces(block):
    piece_a = along_x(block)
    sibling = other_core(block)
    piece_b = along_x(sibling)
    piece_f = along_x(piece_a)
    pieces = [block, sibling, piece_a, piece_b]
    return pieces + [other_core(piece_a), other_core(piece_b), piece_f, other_core(piece_f)]


def per_device(encoded, starts, w_up, norm_gain, w_query, w_key, w_value, w_out, cotangent):
    byte_rows, byte_width = encoded.shape
    shards, patch_cap = starts.shape
    columns = w_up.shape[1]
    rows = cotangent.shape[0]
    gain = norm_gain.reshape(1, -1)
    weights = (w_query, w_key, w_value)
    is_valid = (starts < byte_rows).reshape(-1, rows)
    by_half = jnp.moveaxis(is_valid.reshape(-1, 2, rows // 2), 1, 0).reshape(2, -1, 1)
    bias = jnp.broadcast_to(jnp.where(by_half, 0.0, NEG), (*by_half.shape[:2], 128))
    row_valid = lax.dynamic_slice_in_dim(is_valid, lax.axis_index(SEQ), 1, 0)
    valid = row_valid.reshape(rows, 1).astype(F32)

    cots = tp_pieces(cotangent)
    sums, lead = call(
        pool_kernel,
        (starts, encoded),
        [shape(patch_cap, byte_width, dtype=F32), shape(1, byte_width, dtype=F32)],
        name="pool",
        megabytes=4,
    )
    next_lead = lax.ppermute(lead, ALL, [(i, i - 1) for i in range(1, shards)])
    patches = call(
        functools.partial(patch_kernel, byte_rows),
        (starts, sums, next_lead),
        [shape(patch_cap, byte_width)],
        name="patch",
        megabytes=4,
    )[0]
    shifted = [lax.ppermute(patches, "x", [(i, (i + k) % 4) for i in range(4)]) for k in (1, 2, 3)]
    own_blocks = jnp.stack([patches, *shifted])
    other_blocks = other_core(own_blocks)
    other_blocks, cots = lax.optimization_barrier((other_blocks, cots))
    latent = call(
        latent_kernel,
        (own_blocks, other_blocks, w_up),
        [shape(rows, columns)],
        [pltpu.VMEM((8, patch_cap, byte_width), BF16)],
        name="latent",
        megabytes=8,
    )[0]

    d_attn = d_attn_of(cots, valid, w_out)
    pieces = tp_pieces(latent)
    keep, send, *qkv, rinv = project(pieces, d_attn, gain, weights)
    half = rows // 2
    packed = shape(shards // 8, half + half // 2, 2 * HEAD)
    sent = call(pack_kernel, (keep, other_core(send)), [packed], name="pack")[0]
    mine = lax.all_to_all(sent, SEQ, 0, 0, tiled=True)
    keep, send, strips = attention(bias, mine, other_core(mine))
    back = call(return_kernel, (keep, other_core(send), strips), [packed], name="return")[0]
    back = lax.all_to_all(back, SEQ, 0, 0, tiled=True)
    both = shape(4, rows, 2 * HEAD)
    keep, send = call(regroup_kernel, (back,), [both, both], name="regroup")
    rest = (pieces, keep, other_core(send), qkv, rinv, gain, weights, w_out)

    from_other = other_core(outputs_for((7, 3, 2, 1), *rest))
    for_own = outputs_for((6, 5, 4, 0), *rest)
    block = (2 * rows, columns)
    far, side, near, kept = call(
        add_kernel,
        (for_own, from_other),
        [shape(*block), shape(*block), shape(*block, dtype=F32), shape(*block, dtype=F32)],
        name="add",
        megabytes=16,
    )
    far_in = along_x(far)
    side_in = other_core(along_x(side))
    ahead = call(pass_kernel, (near, far_in), [shape(*block)], name="pass")[0]
    return tuple(
        call(
            final_kernel,
            (valid, rinv, cotangent, latent, kept, along_x(ahead), side_in),
            [shape(rows, columns), shape(rows, columns, dtype=F32)],
            name="final",
        )
    )


def solution(mesh):
    split = Mesh(mesh.devices.reshape(4, 4, 4, 2), ALL)
    in_specs = (
        P(ALL, None),
        P(),
        P(None, TP),
        P(),
        P(None, TP),
        P(None, TP),
        P(None, TP),
        P(TP, None),
        P(SEQ, TP),
    )
    out_specs = (P(SEQ, TP), P(SEQ, TP))
    return jax.shard_map(
        per_device, mesh=split, in_specs=in_specs, out_specs=out_specs, check_vma=False
    )
```

```python
import functools

import jax
import jax.numpy as jnp
from jax import lax
from jax.experimental import pallas as pl
from jax.experimental.pallas import tpu as pltpu
from jax.sharding import Mesh
from jax.sharding import PartitionSpec as P

HEAD = 128
SEQ = ("y", "z")
TP = ("x", "c")
ALL = ("y", "z", "x", "c")
EPS = 1e-05
NEG = -1e30
SCALE = HEAD ** (-0.5)
LOG2E = 1.4426950408889634
EXP2_SCALE = SCALE * LOG2E
F32 = jnp.float32
BF16 = jnp.bfloat16
NT = (((1,), (1,)), ((), ()))
TN = (((0,), (0,)), ((), ()))
VMEM = pl.BlockSpec(memory_space=pltpu.VMEM)
XC = ("x", "c")


def shape(*dims, dtype=BF16):
    return jax.ShapeDtypeStruct(dims, dtype)


def call(kernel, ins, outs, scratch=(), name=None, megabytes=8, micros=1.0, stay=0):
    here = len(ins) - stay
    ins = [*ins[:here], *(pltpu.with_memory_space_constraint(a, pltpu.HBM) for a in ins[here:])]
    return pl.pallas_call(
        kernel,
        in_specs=[VMEM] * (len(ins) - stay) + [pl.BlockSpec(memory_space=pltpu.HBM)] * stay,
        out_specs=[VMEM] * len(outs),
        out_shape=list(outs),
        scratch_shapes=list(scratch),
        compiler_params=pltpu.CompilerParams(vmem_limit_bytes=megabytes * 1024 * 1024),
        cost_estimate=pl.CostEstimate(
            flops=int(micros * 1e9), transcendentals=0, bytes_accessed=int(micros * 3e6)
        ),
        name=name,
    )(*ins)


def place(axis):
    return lax.axis_index(axis)


def other_core(block):
    return lax.ppermute(block, "c", [(0, 1), (1, 0)])


def along_x(block):
    route = []
    for x in range(4):
        for c in range(2):
            route.append((x * 2 + c, ((x + 1 - 2 * c) % 4) * 2 + c))
    return lax.ppermute(block, XC, route)


def bounds(starts_ref, shard, byte_rows):
    row = starts_ref[pl.ds(shard, 1), :]
    end = jnp.full((1, 1), byte_rows, jnp.int32)
    return row, jnp.concatenate([row[:, 1:], end], axis=1)


def pool_kernel(starts_ref, enc_ref, sums_ref, lead_ref):
    byte_rows = enc_ref.shape[0]
    cap = starts_ref.shape[1]
    row, following = bounds(starts_ref, place(ALL), byte_rows)
    places = lax.broadcasted_iota(jnp.int32, (byte_rows, cap), 0)
    inside = ((places >= row) & (places < following)).astype(F32).astype(BF16)
    enc = enc_ref[...]
    sums_ref[...] = lax.dot_general(inside, enc, TN, preferred_element_type=F32)
    leading = (places < row[:, :1]).astype(F32).astype(BF16)
    lead = lax.dot_general(leading, enc, TN, preferred_element_type=F32)
    lead_ref[...] = lead[:1]


def as_column(row, eye):
    return jnp.sum(jnp.where(eye, row, 0.0), axis=1, keepdims=True)


def as_row(column, eye):
    return jnp.sum(jnp.where(eye, column, 0.0), axis=0, keepdims=True)


def eye_of(n):
    return lax.broadcasted_iota(jnp.int32, (n, n), 0) == lax.broadcasted_iota(jnp.int32, (n, n), 1)


def patch_kernel(byte_rows, starts_ref, sums_ref, next_ref, out_ref):
    shards, cap = starts_ref.shape
    shard = place(ALL)
    row, following = bounds(starts_ref, shard, byte_rows)
    count = jnp.sum((row < byte_rows).astype(F32), axis=1, keepdims=True)
    slot = lax.broadcasted_iota(jnp.int32, (1, cap), 1).astype(F32)
    last = (slot == count - 1.0).astype(F32)
    after = starts_ref[pl.ds(jnp.minimum(shard + 1, shards - 1), 1), :][:, :1].astype(F32)
    after = jnp.where(shard + 1 < shards, after, 0.0)
    sizes = (following - row).astype(F32) + last * after
    eye = eye_of(cap)
    total = sums_ref[...] + as_column(last, eye) * next_ref[...]
    out_ref[...] = (total / as_column(jnp.maximum(sizes, 1.0), eye)).astype(BF16)


def latent_kernel(own_ref, other_ref, w_ref, out_ref, group):
    x, c = place("x"), place("c")
    count, rows, width = own_ref.shape
    for k in range(count):
        at = lax.rem(x + count - k, count) * 2
        group[at + c] = own_ref[k]
        group[at + 1 - c] = other_ref[k]
    whole = group[...].reshape(2 * count * rows, width)
    out_ref[...] = jnp.dot(whole, w_ref[...], preferred_element_type=F32).astype(BF16)


def tp_places():
    x, c = place("x"), place("c")
    back = lax.rem(x + 3 + 2 * c, 4) * 2
    ahead = lax.rem(x + 1 + 2 * c, 4) * 2
    far = lax.rem(x + 2, 4) * 2
    o = 1 - c
    return [2 * x + c, 2 * x + o, back + c, back + o, ahead + o, ahead + c, far + c, far + o]


def piece_rows(ref, at, size):
    return ref[pl.ds(pl.multiple_of(at * size, size), size), :]


def project_kernel(*refs):
    pieces, (do_ref, gain_ref), weights = refs[:8], refs[8:10], refs[10:13]
    outs, (held, sems, lats, accs, heads) = refs[13:19], refs[19:24]
    keep_ref, send_ref, qkv_refs, rinv_ref = outs[0], outs[1], outs[2:5], outs[5]
    rows, size = pieces[0].shape
    width = gain_ref.shape[1]
    c = place("c")
    places = tp_places()
    copies = []
    for t in range(8):
        for kind in range(3):
            part = weights[kind].at[t * size : (t + 1) * size, :]
            copies.append(pltpu.make_async_copy(part, held.at[t, kind], sems.at[t, kind]))
    for copy in copies:
        copy.start()
    for piece, at in zip(pieces, places):
        lats[at] = piece[...]
    for h in range(4):
        heads[12 + h] = do_ref[:, h * HEAD : (h + 1) * HEAD]
    square = jnp.zeros((rows, 128), F32)
    for t in range(8):
        wide = lats[t].astype(F32)
        squares = wide * wide
        for part in range(0, size, 128):
            square = square + squares[:, part : part + 128]
        scaled = (wide * gain_ref[:, t * size : (t + 1) * size]).astype(BF16)
        for kind in range(3):
            copies[3 * t + kind].wait()
            made = jnp.dot(scaled, held[t, kind], preferred_element_type=F32)
            accs[kind] = made if t == 0 else accs[kind] + made
    total = jnp.sum(square, axis=1, keepdims=True)
    rinv = lax.rsqrt(total / width + EPS)
    rinv_ref[...] = rinv
    for kind in range(3):
        rounded = (rinv * accs[kind]).astype(BF16)
        qkv_refs[kind][...] = rounded
        for h in range(4):
            heads[kind * 4 + h] = rounded[:, h * HEAD : (h + 1) * HEAD]
    half = rows // 2
    for out, which in ((keep_ref, c), (send_ref, 1 - c)):
        span = pl.ds(pl.multiple_of(which * half, half), half)
        for h in range(4):
            out[h, :half, :HEAD] = heads[4 + h, span, :]
            out[h, :half, HEAD:] = heads[8 + h, span, :]
            out[h, half:, :HEAD] = heads[h, span, :]
            out[h, half:, HEAD:] = heads[12 + h, span, :]


def project(pieces, d_attn, gain, weights):
    rows, size = pieces[0].shape
    both = shape(4, rows, 2 * HEAD)
    return call(
        project_kernel,
        (*pieces, d_attn, gain, *weights),
        [both, both] + [shape(rows, size)] * 3 + [shape(rows, 1, dtype=F32)],
        [
            pltpu.VMEM((8, 3, size, size), BF16),
            pltpu.SemaphoreType.DMA((8, 3)),
            pltpu.VMEM((8, rows, size), BF16),
            pltpu.VMEM((3, rows, size), F32),
            pltpu.VMEM((16, rows, HEAD), BF16),
        ],
        name="project",
        megabytes=28,
        micros=5.0,
        stay=3,
    )


def d_attn_kernel(valid_ref, *refs):
    grads, w_ref, out_ref, pieces, held, grad_sems, sems = refs[:8], *refs[8:]
    rows, size = grads[0].shape
    copies = [
        pltpu.make_async_copy(grad, pieces.at[n], grad_sems.at[n]) for n, grad in enumerate(grads)
    ]
    for h in range(4):
        span = slice(h * HEAD, (h + 1) * HEAD)
        copies.append(pltpu.make_async_copy(w_ref.at[span, :], held.at[span, :], sems.at[h]))
    for copy in copies:
        copy.start()
    for copy in copies[:8]:
        copy.wait()
    valid = valid_ref[...] > 0.0
    places = tp_places()
    for h in range(0, 4, 2):
        copies[8 + h].wait()
        copies[9 + h].wait()
        span = slice(h * HEAD, (h + 2) * HEAD)
        acc = 0.0
        for n, at in enumerate(places):
            w = held[span, pl.ds(pl.multiple_of(at * size, size), size)]
            acc = acc + lax.dot_general(pieces[n], w, NT, preferred_element_type=F32)
        out_ref[:, span] = jnp.where(valid, acc, 0.0).astype(BF16)


def d_attn_of(grads, valid, w_out):
    rows, size = grads[0].shape
    return call(
        d_attn_kernel,
        (valid, *grads, w_out),
        [shape(rows, size)],
        [
            pltpu.VMEM((8, rows, size), BF16),
            pltpu.VMEM(w_out.shape, BF16),
            pltpu.SemaphoreType.DMA((8,)),
            pltpu.SemaphoreType.DMA((4,)),
        ],
        name="d_attn",
        megabytes=12,
        micros=2.0,
        stay=9,
    )[0]


def pack_kernel(keep_ref, got_ref, out_ref):
    c = place("c")
    half = keep_ref.shape[1] // 2
    strip = half // 2
    for ref, core in ((keep_ref, c), (got_ref, 1 - c)):
        for h in range(4):
            for e in range(2):
                s = (core * 4 + h) * 2 + e
                out_ref[s, :half, :] = ref[h, :half, :]
                out_ref[s, half:, :] = ref[h, half + e * strip : half + (e + 1) * strip, :]


def attention_kernel(bias_ref, mine_ref, theirs_ref, keep_ref, send_ref, strip_ref, *scratch):
    scores, dks, dvs, biases = scratch
    c, e = place("c"), lax.rem(place("z"), 2)
    blocks = mine_ref.shape[0]
    half, strip, span, rows = 128, 64, 512, 256
    sources = (mine_ref, theirs_ref)

    def kv_of(side, u):
        ref = sources[side]
        keys = ref[4 * u : 4 * u + 4, :half, :HEAD].reshape(span, HEAD)
        return keys, ref[4 * u : 4 * u + 4, :half, HEAD:].reshape(span, HEAD)

    biases[0], biases[1] = bias_ref[c], bias_ref[1 - c]
    dks[...] = jnp.zeros_like(dks)
    dvs[...] = jnp.zeros_like(dvs)
    lane = lax.broadcasted_iota(jnp.int32, (1, rows), 1)
    place_q = (lane // strip) * 256 + lax.rem(lane, strip) + c * half + e * strip
    line = lax.broadcasted_iota(jnp.int32, (span, 1), 0)
    place_k = (line // half) * 256 + lax.rem(line, half)
    allowed = [place_k + which * half <= place_q for which in (c, 1 - c)]
    for t in range(4):
        q = mine_ref[4 * t : 4 * t + 4, half:, :HEAD].reshape(rows, HEAD)
        do = mine_ref[4 * t : 4 * t + 4, half:, HEAD:].reshape(rows, HEAD)
        peak = jnp.full((1, rows), NEG, F32)
        for side in range(2):
            for u in range(t + 1):
                keys, _ = kv_of(side, u)
                s = lax.dot_general(keys, q, NT, preferred_element_type=F32)
                bias = biases[side, u * span : (u + 1) * span, :]
                s = s + jnp.concatenate([bias, bias], axis=1)
                if u == t:
                    s = jnp.where(allowed[side], s, NEG)
                scores[side * 4 + u] = s
                peak = jnp.maximum(peak, jnp.max(s, axis=0, keepdims=True))
        total = jnp.zeros((1, rows), F32)
        mixed = jnp.zeros((HEAD, rows), F32)
        for side in range(2):
            for u in range(t + 1):
                _, values = kv_of(side, u)
                p = jnp.exp2((scores[side * 4 + u] - peak) * EXP2_SCALE)
                total = total + jnp.sum(p, axis=0, keepdims=True)
                scores[side * 4 + u] = p
                mixed = mixed + lax.dot_general(
                    values, p.astype(BF16), TN, preferred_element_type=F32
                )
        inverse = 1.0 / total
        attn = jnp.transpose(mixed * inverse).astype(BF16)
        products = do.astype(F32) * attn.astype(F32)
        delta = jnp.sum(jnp.transpose(products), axis=0, keepdims=True)
        dq = jnp.zeros((HEAD, rows), F32)
        for side in range(2):
            for u in range(t + 1):
                keys, values = kv_of(side, u)
                p = scores[side * 4 + u] * inverse
                dp = lax.dot_general(values, do, NT, preferred_element_type=F32)
                ds = (p * (dp - delta)).astype(BF16)
                at = slice(u * span, (u + 1) * span)
                dvs[side, at, :] += jnp.dot(p.astype(BF16), do, preferred_element_type=F32)
                dks[side, at, :] += jnp.dot(ds, q, preferred_element_type=F32)
                dq = dq + lax.dot_general(keys, ds, TN, preferred_element_type=F32)
        dq = jnp.transpose(dq * SCALE).astype(BF16)
        strip_ref[4 * t : 4 * t + 4, :, :HEAD] = dq.reshape(4, strip, HEAD)
        strip_ref[4 * t : 4 * t + 4, :, HEAD:] = attn.reshape(4, strip, HEAD)
    for side, ref in ((0, keep_ref), (1, send_ref)):
        ref[:, :, :HEAD] = (dks[side] * SCALE).astype(BF16).reshape(blocks, half, HEAD)
        ref[:, :, HEAD:] = dvs[side].astype(BF16).reshape(blocks, half, HEAD)


def attention(bias, mine, theirs):
    blocks, _, both = mine.shape
    grads = shape(blocks, 128, both)
    return call(
        attention_kernel,
        (bias, mine, theirs),
        [grads, grads, shape(blocks, 64, both)],
        [pltpu.VMEM((8, 512, 256), F32)] + [pltpu.VMEM((2, blocks * 128, HEAD), F32)] * 3,
        name="attention",
        megabytes=28,
        micros=12.0,
    )


def return_kernel(keep_ref, got_ref, strip_ref, out_ref):
    half = keep_ref.shape[1]
    out_ref[:, :half, :] = (keep_ref[...].astype(F32) + got_ref[...].astype(F32)).astype(BF16)
    out_ref[:, half:, :] = strip_ref[...]


def regroup_kernel(in_ref, keep_ref, send_ref):
    c = place("c")
    half, strip = 128, 64
    for out, core in ((keep_ref, c), (send_ref, 1 - c)):
        for h in range(4):
            s = (core * 4 + h) * 2
            total = in_ref[s, :half, :].astype(F32) + in_ref[s + 1, :half, :].astype(F32)
            out[h, :half, :] = total.astype(BF16)
            out[h, half : half + strip, :] = in_ref[s, half:, :]
            out[h, half + strip :, :] = in_ref[s + 1, half:, :]


def output_kernel(which, keep_ref, got_ref, *refs):
    qkv, rinv_ref, lats, gain_ref = refs[:3], refs[3], refs[4:8], refs[8]
    weights, w_out_ref, out_ref, wide = refs[9:12], refs[12], refs[13], refs[14]
    rows, size = qkv[0].shape
    width = gain_ref.shape[1]
    half = rows // 2
    c = place("c")
    for ref, core in ((keep_ref, c), (got_ref, 1 - c)):
        span = pl.ds(pl.multiple_of(core * half, half), half)
        for h in range(4):
            at = slice(h * HEAD, (h + 1) * HEAD)
            wide[0, span, at] = ref[h, half:, :HEAD]
            wide[1, span, at] = ref[h, :half, :HEAD]
            wide[2, span, at] = ref[h, :half, HEAD:]
            wide[3, span, at] = ref[h, half:, HEAD:]
    both = sum(wide[n].astype(F32) * qkv[n][...].astype(F32) for n in range(3))
    factor = jnp.sum(both, axis=1, keepdims=True) * rinv_ref[...] / width
    places = tp_places()
    for n, kind in enumerate(which):
        at = places[kind]
        acc = sum(
            lax.dot_general(
                wide[i], piece_rows(weights[i], at, size), NT, preferred_element_type=F32
            )
            for i in range(3)
        )
        columns = pl.ds(pl.multiple_of(at * size, size), size)
        grad = gain_ref[:, columns] * acc - lats[n][...].astype(F32) * factor
        out_ref[n, :rows, :] = grad.astype(BF16)
        mixed = jnp.dot(wide[3], w_out_ref[:, columns], preferred_element_type=F32)
        out_ref[n, rows:, :] = mixed.astype(BF16)


def outputs_for(which, pieces, keep, got, qkv, rinv, gain, weights, w_out):
    rows, size = pieces[0].shape
    lats = [pieces[kind] for kind in which]
    return call(
        functools.partial(output_kernel, which),
        (keep, got, *qkv, rinv, *lats, gain, *weights, w_out),
        [shape(4, 2 * rows, size)],
        [pltpu.VMEM((4, rows, size), BF16)],
        name="outputs",
        megabytes=28,
        micros=3.0,
    )[0]


def add_kernel(own_ref, other_ref, far_ref, side_ref, near_ref, kept_ref):
    for n, ref in enumerate((far_ref, near_ref, side_ref, kept_ref)):
        total = own_ref[n].astype(F32) + other_ref[n].astype(F32)
        ref[...] = total.astype(ref.dtype)


def pass_kernel(near_ref, far_ref, out_ref):
    out_ref[...] = (near_ref[...] + far_ref[...].astype(F32)).astype(BF16)


def final_kernel(valid_ref, rinv_ref, cot_ref, lat_ref, kept_ref, ahead_ref, side_ref, *outs):
    out_ref, grad_ref = outs
    rows = cot_ref.shape[0]
    total = kept_ref[...] + ahead_ref[...].astype(F32) + side_ref[...].astype(F32)
    valid = valid_ref[...] > 0.0
    grad_out = jnp.where(valid, cot_ref[...].astype(F32), 0.0)
    grad_ref[...] = grad_out + rinv_ref[...] * total[:rows]
    result = lat_ref[...].astype(F32) + total[rows:]
    out_ref[...] = jnp.where(valid, result, 0.0).astype(BF16)


def tp_pieces(block, beside=None):
    piece_a = along_x(block)
    sibling = other_core(block)
    if beside is not None:
        piece_a, beside = lax.optimization_barrier((piece_a, beside))
    piece_b = along_x(sibling)
    piece_f = along_x(piece_a)
    pieces = [block, sibling, piece_a, piece_b]
    pieces += [other_core(piece_a), other_core(piece_b), piece_f, other_core(piece_f)]
    return pieces if beside is None else (pieces, beside)


def per_device(encoded, starts, w_up, norm_gain, w_query, w_key, w_value, w_out, cotangent):
    byte_rows, byte_width = encoded.shape
    shards, patch_cap = starts.shape
    columns = w_up.shape[1]
    rows = cotangent.shape[0]
    gain = norm_gain.reshape(1, -1)
    weights = (w_query, w_key, w_value)
    is_valid = (starts < byte_rows).reshape(-1, rows)
    by_half = jnp.moveaxis(is_valid.reshape(-1, 2, rows // 2), 1, 0).reshape(2, -1, 1)
    bias = jnp.broadcast_to(jnp.where(by_half, 0.0, NEG), (*by_half.shape[:2], 128))
    row_valid = lax.dynamic_slice_in_dim(is_valid, lax.axis_index(SEQ), 1, 0)
    valid = row_valid.reshape(rows, 1).astype(F32)

    cots = tp_pieces(cotangent)
    sums, lead = call(
        pool_kernel,
        (starts, encoded),
        [shape(patch_cap, byte_width, dtype=F32), shape(1, byte_width, dtype=F32)],
        name="pool",
        megabytes=4,
    )
    next_lead = lax.ppermute(lead, ALL, [(i, i - 1) for i in range(1, shards)])
    patches = call(
        functools.partial(patch_kernel, byte_rows),
        (starts, sums, next_lead),
        [shape(patch_cap, byte_width)],
        name="patch",
        megabytes=4,
    )[0]
    shifted = [lax.ppermute(patches, "x", [(i, (i + k) % 4) for i in range(4)]) for k in (1, 2, 3)]
    own_blocks = jnp.stack([patches, *shifted])
    other_blocks = other_core(own_blocks)
    other_blocks, cots = lax.optimization_barrier((other_blocks, cots))
    latent = call(
        latent_kernel,
        (own_blocks, other_blocks, w_up),
        [shape(rows, columns)],
        [pltpu.VMEM((8, patch_cap, byte_width), BF16)],
        name="latent",
        megabytes=8,
    )[0]

    d_attn = d_attn_of(cots, valid, w_out)
    pieces, d_attn = tp_pieces(latent, d_attn)
    keep, send, *qkv, rinv = project(pieces, d_attn, gain, weights)
    half = rows // 2
    packed = shape(shards // 8, half + half // 2, 2 * HEAD)
    sent = call(pack_kernel, (keep, other_core(send)), [packed], name="pack")[0]
    mine = lax.all_to_all(sent, SEQ, 0, 0, tiled=True)
    keep, send, strips = attention(bias, mine, other_core(mine))
    back = call(return_kernel, (keep, other_core(send), strips), [packed], name="return")[0]
    back = lax.all_to_all(back, SEQ, 0, 0, tiled=True)
    both = shape(4, rows, 2 * HEAD)
    keep, send = call(regroup_kernel, (back,), [both, both], name="regroup")
    rest = (pieces, keep, other_core(send), qkv, rinv, gain, weights, w_out)

    from_other = other_core(outputs_for((7, 3, 2, 1), *rest))
    for_own = outputs_for((6, 5, 4, 0), *rest)
    block = (2 * rows, columns)
    far, side, near, kept = call(
        add_kernel,
        (for_own, from_other),
        [shape(*block), shape(*block), shape(*block, dtype=F32), shape(*block, dtype=F32)],
        name="add",
        megabytes=16,
    )
    far_in = along_x(far)
    far_in, side = lax.optimization_barrier((far_in, side))
    side_in = other_core(along_x(side))
    ahead = call(pass_kernel, (near, far_in), [shape(*block)], name="pass")[0]
    return tuple(
        call(
            final_kernel,
            (valid, rinv, cotangent, latent, kept, along_x(ahead), side_in),
            [shape(rows, columns), shape(rows, columns, dtype=F32)],
            name="final",
        )
    )


def solution(mesh):
    split = Mesh(mesh.devices.reshape(4, 4, 4, 2), ALL)
    in_specs = (
        P(ALL, None),
        P(),
        P(None, TP),
        P(),
        P(None, TP),
        P(None, TP),
        P(None, TP),
        P(TP, None),
        P(SEQ, TP),
    )
    out_specs = (P(SEQ, TP), P(SEQ, TP))
    return jax.shard_map(
        per_device, mesh=split, in_specs=in_specs, out_specs=out_specs, check_vma=False
    )
```

```python
import functools

import jax
import jax.numpy as jnp
from jax import lax
from jax.experimental import pallas as pl
from jax.experimental.pallas import tpu as pltpu
from jax.sharding import Mesh
from jax.sharding import PartitionSpec as P

HEAD = 128
SEQ = ("y", "z")
TP = ("x", "c")
ALL = ("y", "z", "x", "c")
EPS = 1e-05
NEG = -1e30
SCALE = HEAD ** (-0.5)
LOG2E = 1.4426950408889634
EXP2_SCALE = SCALE * LOG2E
DELAY = 8.0
F32 = jnp.float32
BF16 = jnp.bfloat16
NT = (((1,), (1,)), ((), ()))
TN = (((0,), (0,)), ((), ()))
VMEM = pl.BlockSpec(memory_space=pltpu.VMEM)
XC = ("x", "c")


def shape(*dims, dtype=BF16):
    return jax.ShapeDtypeStruct(dims, dtype)


def call(kernel, ins, outs, scratch=(), name=None, megabytes=8, micros=1.0, stay=0):
    here = len(ins) - stay
    ins = [*ins[:here], *(pltpu.with_memory_space_constraint(a, pltpu.HBM) for a in ins[here:])]
    return pl.pallas_call(
        kernel,
        in_specs=[VMEM] * (len(ins) - stay) + [pl.BlockSpec(memory_space=pltpu.HBM)] * stay,
        out_specs=[VMEM] * len(outs),
        out_shape=list(outs),
        scratch_shapes=list(scratch),
        compiler_params=pltpu.CompilerParams(vmem_limit_bytes=megabytes * 1024 * 1024),
        cost_estimate=pl.CostEstimate(
            flops=int(micros * 1e9), transcendentals=0, bytes_accessed=int(micros * 3e6)
        ),
        name=name,
    )(*ins)


def place(axis):
    return lax.axis_index(axis)


def other_core(block):
    return lax.ppermute(block, "c", [(0, 1), (1, 0)])


def along_x(block):
    route = []
    for x in range(4):
        for c in range(2):
            route.append((x * 2 + c, ((x + 1 - 2 * c) % 4) * 2 + c))
    return lax.ppermute(block, XC, route)


def bounds(starts_ref, shard, byte_rows):
    row = starts_ref[pl.ds(shard, 1), :]
    end = jnp.full((1, 1), byte_rows, jnp.int32)
    return row, jnp.concatenate([row[:, 1:], end], axis=1)


def pool_kernel(starts_ref, enc_ref, sums_ref, lead_ref):
    byte_rows = enc_ref.shape[0]
    cap = starts_ref.shape[1]
    row, following = bounds(starts_ref, place(ALL), byte_rows)
    places = lax.broadcasted_iota(jnp.int32, (byte_rows, cap), 0)
    inside = ((places >= row) & (places < following)).astype(F32).astype(BF16)
    enc = enc_ref[...]
    sums_ref[...] = lax.dot_general(inside, enc, TN, preferred_element_type=F32)
    leading = (places < row[:, :1]).astype(F32).astype(BF16)
    lead = lax.dot_general(leading, enc, TN, preferred_element_type=F32)
    lead_ref[...] = lead[:1]


def as_column(row, eye):
    return jnp.sum(jnp.where(eye, row, 0.0), axis=1, keepdims=True)


def as_row(column, eye):
    return jnp.sum(jnp.where(eye, column, 0.0), axis=0, keepdims=True)


def eye_of(n):
    return lax.broadcasted_iota(jnp.int32, (n, n), 0) == lax.broadcasted_iota(jnp.int32, (n, n), 1)


def patch_kernel(byte_rows, starts_ref, sums_ref, next_ref, out_ref):
    shards, cap = starts_ref.shape
    shard = place(ALL)
    row, following = bounds(starts_ref, shard, byte_rows)
    count = jnp.sum((row < byte_rows).astype(F32), axis=1, keepdims=True)
    slot = lax.broadcasted_iota(jnp.int32, (1, cap), 1).astype(F32)
    last = (slot == count - 1.0).astype(F32)
    after = starts_ref[pl.ds(jnp.minimum(shard + 1, shards - 1), 1), :][:, :1].astype(F32)
    after = jnp.where(shard + 1 < shards, after, 0.0)
    sizes = (following - row).astype(F32) + last * after
    eye = eye_of(cap)
    total = sums_ref[...] + as_column(last, eye) * next_ref[...]
    out_ref[...] = (total / as_column(jnp.maximum(sizes, 1.0), eye)).astype(BF16)


def latent_kernel(own_ref, other_ref, w_ref, out_ref, group):
    x, c = place("x"), place("c")
    count, rows, width = own_ref.shape
    for k in range(count):
        at = lax.rem(x + count - k, count) * 2
        group[at + c] = own_ref[k]
        group[at + 1 - c] = other_ref[k]
    whole = group[...].reshape(2 * count * rows, width)
    out_ref[...] = jnp.dot(whole, w_ref[...], preferred_element_type=F32).astype(BF16)


def tp_places():
    x, c = place("x"), place("c")
    back = lax.rem(x + 3 + 2 * c, 4) * 2
    ahead = lax.rem(x + 1 + 2 * c, 4) * 2
    far = lax.rem(x + 2, 4) * 2
    o = 1 - c
    return [2 * x + c, 2 * x + o, back + c, back + o, ahead + o, ahead + c, far + c, far + o]


def in_order(refs):
    own, sibling, piece_a, piece_b, piece_f, theirs = refs
    a, b, f = (theirs.at[n] for n in range(3))
    return [own, sibling, piece_a, piece_b, a, b, piece_f, f]


def piece_rows(ref, at, size):
    return ref[pl.ds(pl.multiple_of(at * size, size), size), :]


def project_kernel(*refs):
    pieces, (do_ref, gain_ref), weights = in_order(refs[:6]), refs[6:8], refs[8:11]
    outs, (accs, heads) = refs[11:17], refs[17:19]
    keep_ref, send_ref, qkv_refs, rinv_ref = outs[0], outs[1], outs[2:5], outs[5]
    rows, size = pieces[0].shape
    width = gain_ref.shape[1]
    c = place("c")
    square = jnp.zeros((rows, 128), F32)
    for n, (piece, at) in enumerate(zip(pieces, tp_places())):
        wide = piece[...].astype(F32)
        squares = wide * wide
        for part in range(0, size, 128):
            square = square + squares[:, part : part + 128]
        gain = gain_ref[:, pl.ds(pl.multiple_of(at * size, size), size)]
        scaled = (wide * gain).astype(BF16)
        for kind in range(3):
            w = piece_rows(weights[kind], at, size)
            made = jnp.dot(scaled, w, preferred_element_type=F32)
            accs[kind] = made if n == 0 else accs[kind] + made
    total = jnp.sum(square, axis=1, keepdims=True)
    rinv = lax.rsqrt(total / width + EPS)
    rinv_ref[...] = rinv
    for h in range(4):
        heads[12 + h] = do_ref[:, h * HEAD : (h + 1) * HEAD]
    for kind in range(3):
        rounded = (rinv * accs[kind]).astype(BF16)
        qkv_refs[kind][...] = rounded
        for h in range(4):
            heads[kind * 4 + h] = rounded[:, h * HEAD : (h + 1) * HEAD]
    half = rows // 2
    for out, which in ((keep_ref, c), (send_ref, 1 - c)):
        span = pl.ds(pl.multiple_of(which * half, half), half)
        for h in range(4):
            out[h, :half, :HEAD] = heads[4 + h, span, :]
            out[h, :half, HEAD:] = heads[8 + h, span, :]
            out[h, half:, :HEAD] = heads[h, span, :]
            out[h, half:, HEAD:] = heads[12 + h, span, :]


def project(pieces, d_attn, gain, weights):
    rows, size = pieces[0].shape
    both = shape(4, rows, 2 * HEAD)
    return call(
        project_kernel,
        (*pieces, d_attn, gain, *weights),
        [both, both] + [shape(rows, size)] * 3 + [shape(rows, 1, dtype=F32)],
        [pltpu.VMEM((3, rows, size), F32), pltpu.VMEM((16, rows, HEAD), BF16)],
        name="project",
        megabytes=24,
        micros=5.0,
    )


def d_attn_kernel(valid_ref, *refs):
    grads, w_ref, out_ref, pieces, held, grad_sems, sems = in_order(refs[:6]), *refs[6:]
    rows, size = grads[0].shape
    copies = [
        pltpu.make_async_copy(grad, pieces.at[n], grad_sems.at[n]) for n, grad in enumerate(grads)
    ]
    for h in range(4):
        span = slice(h * HEAD, (h + 1) * HEAD)
        copies.append(pltpu.make_async_copy(w_ref.at[span, :], held.at[span, :], sems.at[h]))
    for copy in copies:
        copy.start()
    for copy in copies[:8]:
        copy.wait()
    valid = valid_ref[...] > 0.0
    places = tp_places()
    for h in range(0, 4, 2):
        copies[8 + h].wait()
        copies[9 + h].wait()
        span = slice(h * HEAD, (h + 2) * HEAD)
        acc = 0.0
        for n, at in enumerate(places):
            w = held[span, pl.ds(pl.multiple_of(at * size, size), size)]
            acc = acc + lax.dot_general(pieces[n], w, NT, preferred_element_type=F32)
        out_ref[:, span] = jnp.where(valid, acc, 0.0).astype(BF16)


def d_attn_of(grads, valid, w_out):
    rows, size = grads[0].shape
    return call(
        d_attn_kernel,
        (valid, *grads, w_out),
        [shape(rows, size)],
        [
            pltpu.VMEM((8, rows, size), BF16),
            pltpu.VMEM(w_out.shape, BF16),
            pltpu.SemaphoreType.DMA((8,)),
            pltpu.SemaphoreType.DMA((4,)),
        ],
        name="d_attn",
        megabytes=12,
        micros=DELAY,
        stay=7,
    )[0]


def pack_kernel(keep_ref, got_ref, out_ref):
    c = place("c")
    half = keep_ref.shape[1] // 2
    strip = half // 2
    for ref, core in ((keep_ref, c), (got_ref, 1 - c)):
        for h in range(4):
            for e in range(2):
                s = (core * 4 + h) * 2 + e
                out_ref[s, :half, :] = ref[h, :half, :]
                out_ref[s, half:, :] = ref[h, half + e * strip : half + (e + 1) * strip, :]


def attention_kernel(bias_ref, mine_ref, theirs_ref, keep_ref, send_ref, strip_ref, *scratch):
    scores, dks, dvs, biases = scratch
    c, e = place("c"), lax.rem(place("z"), 2)
    blocks = mine_ref.shape[0]
    half, strip, span, rows = 128, 64, 512, 256
    sources = (mine_ref, theirs_ref)

    def kv_of(side, u):
        ref = sources[side]
        keys = ref[4 * u : 4 * u + 4, :half, :HEAD].reshape(span, HEAD)
        return keys, ref[4 * u : 4 * u + 4, :half, HEAD:].reshape(span, HEAD)

    biases[0], biases[1] = bias_ref[c], bias_ref[1 - c]
    dks[...] = jnp.zeros_like(dks)
    dvs[...] = jnp.zeros_like(dvs)
    lane = lax.broadcasted_iota(jnp.int32, (1, rows), 1)
    place_q = (lane // strip) * 256 + lax.rem(lane, strip) + c * half + e * strip
    line = lax.broadcasted_iota(jnp.int32, (span, 1), 0)
    place_k = (line // half) * 256 + lax.rem(line, half)
    allowed = [place_k + which * half <= place_q for which in (c, 1 - c)]
    for t in range(4):
        q = mine_ref[4 * t : 4 * t + 4, half:, :HEAD].reshape(rows, HEAD)
        do = mine_ref[4 * t : 4 * t + 4, half:, HEAD:].reshape(rows, HEAD)
        peak = jnp.full((1, rows), NEG, F32)
        for side in range(2):
            for u in range(t + 1):
                keys, _ = kv_of(side, u)
                s = lax.dot_general(keys, q, NT, preferred_element_type=F32)
                bias = biases[side, u * span : (u + 1) * span, :]
                s = s + jnp.concatenate([bias, bias], axis=1)
                if u == t:
                    s = jnp.where(allowed[side], s, NEG)
                scores[side * 4 + u] = s
                peak = jnp.maximum(peak, jnp.max(s, axis=0, keepdims=True))
        total = jnp.zeros((1, rows), F32)
        mixed = jnp.zeros((HEAD, rows), F32)
        for side in range(2):
            for u in range(t + 1):
                _, values = kv_of(side, u)
                p = jnp.exp2((scores[side * 4 + u] - peak) * EXP2_SCALE)
                total = total + jnp.sum(p, axis=0, keepdims=True)
                scores[side * 4 + u] = p
                mixed = mixed + lax.dot_general(
                    values, p.astype(BF16), TN, preferred_element_type=F32
                )
        inverse = 1.0 / total
        attn = jnp.transpose(mixed * inverse).astype(BF16)
        products = do.astype(F32) * attn.astype(F32)
        delta = jnp.sum(jnp.transpose(products), axis=0, keepdims=True)
        dq = jnp.zeros((HEAD, rows), F32)
        for side in range(2):
            for u in range(t + 1):
                keys, values = kv_of(side, u)
                p = scores[side * 4 + u] * inverse
                dp = lax.dot_general(values, do, NT, preferred_element_type=F32)
                ds = (p * (dp - delta)).astype(BF16)
                at = slice(u * span, (u + 1) * span)
                dvs[side, at, :] += jnp.dot(p.astype(BF16), do, preferred_element_type=F32)
                dks[side, at, :] += jnp.dot(ds, q, preferred_element_type=F32)
                dq = dq + lax.dot_general(keys, ds, TN, preferred_element_type=F32)
        dq = jnp.transpose(dq * SCALE).astype(BF16)
        strip_ref[4 * t : 4 * t + 4, :, :HEAD] = dq.reshape(4, strip, HEAD)
        strip_ref[4 * t : 4 * t + 4, :, HEAD:] = attn.reshape(4, strip, HEAD)
    for side, ref in ((0, keep_ref), (1, send_ref)):
        ref[:, :, :HEAD] = (dks[side] * SCALE).astype(BF16).reshape(blocks, half, HEAD)
        ref[:, :, HEAD:] = dvs[side].astype(BF16).reshape(blocks, half, HEAD)


def attention(bias, mine, theirs):
    blocks, _, both = mine.shape
    grads = shape(blocks, 128, both)
    return call(
        attention_kernel,
        (bias, mine, theirs),
        [grads, grads, shape(blocks, 64, both)],
        [pltpu.VMEM((8, 512, 256), F32)] + [pltpu.VMEM((2, blocks * 128, HEAD), F32)] * 3,
        name="attention",
        megabytes=28,
        micros=12.0,
    )


def return_kernel(keep_ref, got_ref, strip_ref, out_ref):
    half = keep_ref.shape[1]
    out_ref[:, :half, :] = (keep_ref[...].astype(F32) + got_ref[...].astype(F32)).astype(BF16)
    out_ref[:, half:, :] = strip_ref[...]


def regroup_kernel(in_ref, keep_ref, send_ref):
    c = place("c")
    half, strip = 128, 64
    for out, core in ((keep_ref, c), (send_ref, 1 - c)):
        for h in range(4):
            s = (core * 4 + h) * 2
            total = in_ref[s, :half, :].astype(F32) + in_ref[s + 1, :half, :].astype(F32)
            out[h, :half, :] = total.astype(BF16)
            out[h, half : half + strip, :] = in_ref[s, half:, :]
            out[h, half + strip :, :] = in_ref[s + 1, half:, :]


def output_kernel(which, keep_ref, got_ref, *refs):
    qkv, rinv_ref, lats, gain_ref = refs[:3], refs[3], in_order(refs[4:10]), refs[10]
    weights, w_out_ref, out_ref, wide = refs[11:14], refs[14], refs[15], refs[16]
    rows, size = qkv[0].shape
    width = gain_ref.shape[1]
    half = rows // 2
    c = place("c")
    for ref, core in ((keep_ref, c), (got_ref, 1 - c)):
        span = pl.ds(pl.multiple_of(core * half, half), half)
        for h in range(4):
            at = slice(h * HEAD, (h + 1) * HEAD)
            wide[0, span, at] = ref[h, half:, :HEAD]
            wide[1, span, at] = ref[h, :half, :HEAD]
            wide[2, span, at] = ref[h, :half, HEAD:]
            wide[3, span, at] = ref[h, half:, HEAD:]
    both = sum(wide[n].astype(F32) * qkv[n][...].astype(F32) for n in range(3))
    factor = jnp.sum(both, axis=1, keepdims=True) * rinv_ref[...] / width
    places = tp_places()
    for n, kind in enumerate(which):
        at = places[kind]
        acc = sum(
            lax.dot_general(
                wide[i], piece_rows(weights[i], at, size), NT, preferred_element_type=F32
            )
            for i in range(3)
        )
        columns = pl.ds(pl.multiple_of(at * size, size), size)
        grad = gain_ref[:, columns] * acc - lats[kind][...].astype(F32) * factor
        out_ref[n, :rows, :] = grad.astype(BF16)
        mixed = jnp.dot(wide[3], w_out_ref[:, columns], preferred_element_type=F32)
        out_ref[n, rows:, :] = mixed.astype(BF16)


def outputs_for(which, pieces, keep, got, qkv, rinv, gain, weights, w_out):
    rows, size = pieces[0].shape
    return call(
        functools.partial(output_kernel, which),
        (keep, got, *qkv, rinv, *pieces, gain, *weights, w_out),
        [shape(4, 2 * rows, size)],
        [pltpu.VMEM((4, rows, size), BF16)],
        name="outputs",
        megabytes=28,
        micros=3.0,
    )[0]


def add_kernel(own_ref, other_ref, far_ref, side_ref, near_ref, kept_ref):
    for n, ref in enumerate((far_ref, near_ref, side_ref, kept_ref)):
        total = own_ref[n].astype(F32) + other_ref[n].astype(F32)
        ref[...] = total.astype(ref.dtype)


def pass_kernel(near_ref, far_ref, out_ref):
    out_ref[...] = (near_ref[...] + far_ref[...].astype(F32)).astype(BF16)


def final_kernel(valid_ref, rinv_ref, cot_ref, lat_ref, kept_ref, ahead_ref, side_ref, *outs):
    out_ref, grad_ref = outs
    rows = cot_ref.shape[0]
    total = kept_ref[...] + ahead_ref[...].astype(F32) + side_ref[...].astype(F32)
    valid = valid_ref[...] > 0.0
    grad_out = jnp.where(valid, cot_ref[...].astype(F32), 0.0)
    grad_ref[...] = grad_out + rinv_ref[...] * total[:rows]
    result = lat_ref[...].astype(F32) + total[rows:]
    out_ref[...] = jnp.where(valid, result, 0.0).astype(BF16)


def tp_pieces(block, beside=None):
    piece_a = along_x(block)
    sibling = other_core(block)
    if beside is not None:
        piece_a, beside = lax.optimization_barrier((piece_a, beside))
    piece_f = along_x(piece_a)
    piece_b = along_x(sibling)
    theirs = other_core(jnp.stack([piece_a, piece_b, piece_f]))
    pieces = [block, sibling, piece_a, piece_b, piece_f, theirs]
    return pieces if beside is None else (pieces, beside)


def per_device(encoded, starts, w_up, norm_gain, w_query, w_key, w_value, w_out, cotangent):
    byte_rows, byte_width = encoded.shape
    shards, patch_cap = starts.shape
    columns = w_up.shape[1]
    rows = cotangent.shape[0]
    gain = norm_gain.reshape(1, -1)
    weights = (w_query, w_key, w_value)
    is_valid = (starts < byte_rows).reshape(-1, rows)
    by_half = jnp.moveaxis(is_valid.reshape(-1, 2, rows // 2), 1, 0).reshape(2, -1, 1)
    bias = jnp.broadcast_to(jnp.where(by_half, 0.0, NEG), (*by_half.shape[:2], 128))
    row_valid = lax.dynamic_slice_in_dim(is_valid, lax.axis_index(SEQ), 1, 0)
    valid = row_valid.reshape(rows, 1).astype(F32)

    cot_a, cot_sibling = along_x(cotangent), other_core(cotangent)
    sums, lead = call(
        pool_kernel,
        (starts, encoded),
        [shape(patch_cap, byte_width, dtype=F32), shape(1, byte_width, dtype=F32)],
        name="pool",
        megabytes=4,
    )
    next_lead = lax.ppermute(lead, ALL, [(i, i - 1) for i in range(1, shards)])
    patches = call(
        functools.partial(patch_kernel, byte_rows),
        (starts, sums, next_lead),
        [shape(patch_cap, byte_width)],
        name="patch",
        megabytes=4,
    )[0]
    patches, cot_a, cot_sibling = lax.optimization_barrier((patches, cot_a, cot_sibling))
    cot_f, cot_b = along_x(cot_a), along_x(cot_sibling)
    shifted = [lax.ppermute(patches, "x", [(i, (i + k) % 4) for i in range(4)]) for k in (1, 2, 3)]
    own_blocks = jnp.stack([patches, *shifted])
    own_blocks, cot_b, cot_f = lax.optimization_barrier((own_blocks, cot_b, cot_f))
    other_blocks = other_core(own_blocks)
    cot_theirs = other_core(jnp.stack([cot_a, cot_b, cot_f]))
    cots = [cotangent, cot_sibling, cot_a, cot_b, cot_f, cot_theirs]
    latent = call(
        latent_kernel,
        (own_blocks, other_blocks, w_up),
        [shape(rows, columns)],
        [pltpu.VMEM((8, patch_cap, byte_width), BF16)],
        name="latent",
        megabytes=8,
        micros=DELAY,
    )[0]

    d_attn = d_attn_of(cots, valid, w_out)
    pieces, (d_attn, bias) = tp_pieces(latent, (d_attn, bias))
    keep, send, *qkv, rinv = project(pieces, d_attn, gain, weights)
    half = rows // 2
    packed = shape(shards // 8, half + half // 2, 2 * HEAD)
    sent = call(pack_kernel, (keep, other_core(send)), [packed], name="pack")[0]
    mine = lax.all_to_all(sent, SEQ, 0, 0, tiled=True)
    keep, send, strips = attention(bias, mine, other_core(mine))
    back = call(return_kernel, (keep, other_core(send), strips), [packed], name="return")[0]
    back = lax.all_to_all(back, SEQ, 0, 0, tiled=True)
    both = shape(4, rows, 2 * HEAD)
    keep, send = call(regroup_kernel, (back,), [both, both], name="regroup")
    rest = (pieces, keep, other_core(send), qkv, rinv, gain, weights, w_out)

    from_other = other_core(outputs_for((7, 3, 2, 1), *rest))
    for_own = outputs_for((6, 5, 4, 0), *rest)
    block = (2 * rows, columns)
    far, side, near, kept = call(
        add_kernel,
        (for_own, from_other),
        [shape(*block), shape(*block), shape(*block, dtype=F32), shape(*block, dtype=F32)],
        name="add",
        megabytes=16,
    )
    far_in = along_x(far)
    far_in, side = lax.optimization_barrier((far_in, side))
    side_in = other_core(along_x(side))
    ahead = call(pass_kernel, (near, far_in), [shape(*block)], name="pass")[0]
    return tuple(
        call(
            final_kernel,
            (valid, rinv, cotangent, latent, kept, along_x(ahead), side_in),
            [shape(rows, columns), shape(rows, columns, dtype=F32)],
            name="final",
        )
    )


def solution(mesh):
    split = Mesh(mesh.devices.reshape(4, 4, 4, 2), ALL)
    in_specs = (
        P(ALL, None),
        P(),
        P(None, TP),
        P(),
        P(None, TP),
        P(None, TP),
        P(None, TP),
        P(TP, None),
        P(SEQ, TP),
    )
    out_specs = (P(SEQ, TP), P(SEQ, TP))
    return jax.shard_map(
        per_device, mesh=split, in_specs=in_specs, out_specs=out_specs, check_vma=False
    )
```

```python
import functools

import jax
import jax.numpy as jnp
from jax import lax
from jax.experimental import pallas as pl
from jax.experimental.pallas import tpu as pltpu
from jax.sharding import Mesh
from jax.sharding import PartitionSpec as P

HEAD = 128
SEQ = ("y", "z")
TP = ("x", "c")
ALL = ("y", "z", "x", "c")
EPS = 1e-05
NEG = -1e30
SCALE = HEAD ** (-0.5)
LOG2E = 1.4426950408889634
EXP2_SCALE = SCALE * LOG2E
DELAY = 8.0
F32 = jnp.float32
BF16 = jnp.bfloat16
NT = (((1,), (1,)), ((), ()))
TN = (((0,), (0,)), ((), ()))
VMEM = pl.BlockSpec(memory_space=pltpu.VMEM)
XC = ("x", "c")


def shape(*dims, dtype=BF16):
    return jax.ShapeDtypeStruct(dims, dtype)


def call(kernel, ins, outs, scratch=(), name=None, megabytes=8, micros=1.0, stay=0):
    here = len(ins) - stay
    ins = [*ins[:here], *(pltpu.with_memory_space_constraint(a, pltpu.HBM) for a in ins[here:])]
    return pl.pallas_call(
        kernel,
        in_specs=[VMEM] * (len(ins) - stay) + [pl.BlockSpec(memory_space=pltpu.HBM)] * stay,
        out_specs=[VMEM] * len(outs),
        out_shape=list(outs),
        scratch_shapes=list(scratch),
        compiler_params=pltpu.CompilerParams(vmem_limit_bytes=megabytes * 1024 * 1024),
        cost_estimate=pl.CostEstimate(
            flops=int(micros * 1e9), transcendentals=0, bytes_accessed=int(micros * 3e6)
        ),
        name=name,
    )(*ins)


def place(axis):
    return lax.axis_index(axis)


def other_core(block):
    return lax.ppermute(block, "c", [(0, 1), (1, 0)])


def along_x(block):
    route = []
    for x in range(4):
        for c in range(2):
            route.append((x * 2 + c, ((x + 1 - 2 * c) % 4) * 2 + c))
    return lax.ppermute(block, XC, route)


def bounds(starts_ref, shard, byte_rows):
    row = starts_ref[pl.ds(shard, 1), :]
    end = jnp.full((1, 1), byte_rows, jnp.int32)
    return row, jnp.concatenate([row[:, 1:], end], axis=1)


def pool_kernel(starts_ref, enc_ref, sums_ref, lead_ref):
    byte_rows = enc_ref.shape[0]
    cap = starts_ref.shape[1]
    row, following = bounds(starts_ref, place(ALL), byte_rows)
    places = lax.broadcasted_iota(jnp.int32, (byte_rows, cap), 0)
    inside = ((places >= row) & (places < following)).astype(F32).astype(BF16)
    enc = enc_ref[...]
    sums_ref[...] = lax.dot_general(inside, enc, TN, preferred_element_type=F32)
    leading = (places < row[:, :1]).astype(F32).astype(BF16)
    lead = lax.dot_general(leading, enc, TN, preferred_element_type=F32)
    lead_ref[...] = lead[:1]


def as_column(row, eye):
    return jnp.sum(jnp.where(eye, row, 0.0), axis=1, keepdims=True)


def as_row(column, eye):
    return jnp.sum(jnp.where(eye, column, 0.0), axis=0, keepdims=True)


def eye_of(n):
    return lax.broadcasted_iota(jnp.int32, (n, n), 0) == lax.broadcasted_iota(jnp.int32, (n, n), 1)


def patch_kernel(byte_rows, starts_ref, sums_ref, next_ref, out_ref):
    shards, cap = starts_ref.shape
    shard = place(ALL)
    row, following = bounds(starts_ref, shard, byte_rows)
    count = jnp.sum((row < byte_rows).astype(F32), axis=1, keepdims=True)
    slot = lax.broadcasted_iota(jnp.int32, (1, cap), 1).astype(F32)
    last = (slot == count - 1.0).astype(F32)
    after = starts_ref[pl.ds(jnp.minimum(shard + 1, shards - 1), 1), :][:, :1].astype(F32)
    after = jnp.where(shard + 1 < shards, after, 0.0)
    sizes = (following - row).astype(F32) + last * after
    eye = eye_of(cap)
    total = sums_ref[...] + as_column(last, eye) * next_ref[...]
    out_ref[...] = (total / as_column(jnp.maximum(sizes, 1.0), eye)).astype(BF16)


def latent_kernel(own_ref, other_ref, w_ref, out_ref, group):
    x, c = place("x"), place("c")
    count, rows, width = own_ref.shape
    for k in range(count):
        at = lax.rem(x + count - k, count) * 2
        group[at + c] = own_ref[k]
        group[at + 1 - c] = other_ref[k]
    whole = group[...].reshape(2 * count * rows, width)
    out_ref[...] = jnp.dot(whole, w_ref[...], preferred_element_type=F32).astype(BF16)


def tp_places():
    x, c = place("x"), place("c")
    back = lax.rem(x + 3 + 2 * c, 4) * 2
    ahead = lax.rem(x + 1 + 2 * c, 4) * 2
    far = lax.rem(x + 2, 4) * 2
    o = 1 - c
    return [2 * x + c, 2 * x + o, back + c, back + o, ahead + o, ahead + c, far + c, far + o]


def in_order(refs):
    own, sibling, piece_a, piece_b, piece_f, theirs = refs
    a, b, f = (theirs.at[n] for n in range(3))
    return [own, sibling, piece_a, piece_b, a, b, piece_f, f]


def piece_rows(ref, at, size):
    return ref[pl.ds(pl.multiple_of(at * size, size), size), :]


def project_kernel(*refs):
    pieces, (do_ref, gain_ref), weights = in_order(refs[:6]), refs[6:8], refs[8:11]
    outs, (accs, heads) = refs[11:17], refs[17:19]
    keep_ref, send_ref, qkv_refs, rinv_ref = outs[0], outs[1], outs[2:5], outs[5]
    rows, size = pieces[0].shape
    width = gain_ref.shape[1]
    c = place("c")
    square = jnp.zeros((rows, 128), F32)
    for n, (piece, at) in enumerate(zip(pieces, tp_places())):
        wide = piece[...].astype(F32)
        squares = wide * wide
        for part in range(0, size, 128):
            square = square + squares[:, part : part + 128]
        gain = gain_ref[:, pl.ds(pl.multiple_of(at * size, size), size)]
        scaled = (wide * gain).astype(BF16)
        for kind in range(3):
            w = piece_rows(weights[kind], at, size)
            made = jnp.dot(scaled, w, preferred_element_type=F32)
            accs[kind] = made if n == 0 else accs[kind] + made
    total = jnp.sum(square, axis=1, keepdims=True)
    rinv = lax.rsqrt(total / width + EPS)
    rinv_ref[...] = rinv
    for h in range(4):
        heads[12 + h] = do_ref[:, h * HEAD : (h + 1) * HEAD]
    for kind in range(3):
        rounded = (rinv * accs[kind]).astype(BF16)
        qkv_refs[kind][...] = rounded
        for h in range(4):
            heads[kind * 4 + h] = rounded[:, h * HEAD : (h + 1) * HEAD]
    half = rows // 2
    for out, which in ((keep_ref, c), (send_ref, 1 - c)):
        span = pl.ds(pl.multiple_of(which * half, half), half)
        for h in range(4):
            out[h, :half, :HEAD] = heads[4 + h, span, :]
            out[h, :half, HEAD:] = heads[8 + h, span, :]
            out[h, half:, :HEAD] = heads[h, span, :]
            out[h, half:, HEAD:] = heads[12 + h, span, :]


def project(pieces, d_attn, gain, weights):
    rows, size = pieces[0].shape
    both = shape(4, rows, 2 * HEAD)
    return call(
        project_kernel,
        (*pieces, d_attn, gain, *weights),
        [both, both] + [shape(rows, size)] * 3 + [shape(rows, 1, dtype=F32)],
        [pltpu.VMEM((3, rows, size), F32), pltpu.VMEM((16, rows, HEAD), BF16)],
        name="project",
        megabytes=24,
        micros=5.0,
    )


def d_attn_kernel(valid_ref, *refs):
    grads, w_ref, out_ref, pieces, held, grad_sems, sems = in_order(refs[:6]), *refs[6:]
    rows, size = grads[0].shape
    copies = [
        pltpu.make_async_copy(grad, pieces.at[n], grad_sems.at[n]) for n, grad in enumerate(grads)
    ]
    for h in range(4):
        span = slice(h * HEAD, (h + 1) * HEAD)
        copies.append(pltpu.make_async_copy(w_ref.at[span, :], held.at[span, :], sems.at[h]))
    for copy in copies:
        copy.start()
    for copy in copies[:8]:
        copy.wait()
    valid = valid_ref[...] > 0.0
    places = tp_places()
    for h in range(0, 4, 2):
        copies[8 + h].wait()
        copies[9 + h].wait()
        span = slice(h * HEAD, (h + 2) * HEAD)
        acc = 0.0
        for n, at in enumerate(places):
            w = held[span, pl.ds(pl.multiple_of(at * size, size), size)]
            acc = acc + lax.dot_general(pieces[n], w, NT, preferred_element_type=F32)
        out_ref[:, span] = jnp.where(valid, acc, 0.0).astype(BF16)


def d_attn_of(grads, valid, w_out):
    rows, size = grads[0].shape
    return call(
        d_attn_kernel,
        (valid, *grads, w_out),
        [shape(rows, size)],
        [
            pltpu.VMEM((8, rows, size), BF16),
            pltpu.VMEM(w_out.shape, BF16),
            pltpu.SemaphoreType.DMA((8,)),
            pltpu.SemaphoreType.DMA((4,)),
        ],
        name="d_attn",
        megabytes=12,
        micros=DELAY,
        stay=7,
    )[0]


def pack_kernel(keep_ref, got_ref, out_ref):
    c = place("c")
    half = keep_ref.shape[1] // 2
    strip = half // 2
    for ref, core in ((keep_ref, c), (got_ref, 1 - c)):
        for h in range(4):
            for e in range(2):
                s = (core * 4 + h) * 2 + e
                out_ref[s, :half, :] = ref[h, :half, :]
                out_ref[s, half:, :] = ref[h, half + e * strip : half + (e + 1) * strip, :]


def attention_kernel(bias_ref, mine_ref, theirs_ref, keep_ref, send_ref, strip_ref, *scratch):
    scores, dks, dvs, biases = scratch
    c, e = place("c"), lax.rem(place("z"), 2)
    blocks = mine_ref.shape[0]
    half, strip, span, rows = 128, 64, 512, 256
    sources = (mine_ref, theirs_ref)

    def kv_of(side, u):
        ref = sources[side]
        keys = ref[4 * u : 4 * u + 4, :half, :HEAD].reshape(span, HEAD)
        return keys, ref[4 * u : 4 * u + 4, :half, HEAD:].reshape(span, HEAD)

    biases[0], biases[1] = bias_ref[c], bias_ref[1 - c]
    dks[...] = jnp.zeros_like(dks)
    dvs[...] = jnp.zeros_like(dvs)
    lane = lax.broadcasted_iota(jnp.int32, (1, rows), 1)
    place_q = (lane // strip) * 256 + lax.rem(lane, strip) + c * half + e * strip
    line = lax.broadcasted_iota(jnp.int32, (span, 1), 0)
    place_k = (line // half) * 256 + lax.rem(line, half)
    allowed = [place_k + which * half <= place_q for which in (c, 1 - c)]
    for t in range(4):
        q = mine_ref[4 * t : 4 * t + 4, half:, :HEAD].reshape(rows, HEAD)
        do = mine_ref[4 * t : 4 * t + 4, half:, HEAD:].reshape(rows, HEAD)
        peak = jnp.full((1, rows), NEG, F32)
        for side in range(2):
            for u in range(t + 1):
                keys, _ = kv_of(side, u)
                s = lax.dot_general(keys, q, NT, preferred_element_type=F32)
                bias = biases[side, u * span : (u + 1) * span, :]
                s = s + jnp.concatenate([bias, bias], axis=1)
                if u == t:
                    s = jnp.where(allowed[side], s, NEG)
                scores[side * 4 + u] = s
                peak = jnp.maximum(peak, jnp.max(s, axis=0, keepdims=True))
        total = jnp.zeros((1, rows), F32)
        mixed = jnp.zeros((HEAD, rows), F32)
        for side in range(2):
            for u in range(t + 1):
                _, values = kv_of(side, u)
                p = jnp.exp2((scores[side * 4 + u] - peak) * EXP2_SCALE)
                total = total + jnp.sum(p, axis=0, keepdims=True)
                scores[side * 4 + u] = p
                mixed = mixed + lax.dot_general(
                    values, p.astype(BF16), TN, preferred_element_type=F32
                )
        inverse = 1.0 / total
        attn = jnp.transpose(mixed * inverse).astype(BF16)
        products = do.astype(F32) * attn.astype(F32)
        delta = jnp.sum(jnp.transpose(products), axis=0, keepdims=True)
        dq = jnp.zeros((HEAD, rows), F32)
        for side in range(2):
            for u in range(t + 1):
                keys, values = kv_of(side, u)
                p = scores[side * 4 + u] * inverse
                dp = lax.dot_general(values, do, NT, preferred_element_type=F32)
                ds = (p * (dp - delta)).astype(BF16)
                at = slice(u * span, (u + 1) * span)
                dvs[side, at, :] += jnp.dot(p.astype(BF16), do, preferred_element_type=F32)
                dks[side, at, :] += jnp.dot(ds, q, preferred_element_type=F32)
                dq = dq + lax.dot_general(keys, ds, TN, preferred_element_type=F32)
        dq = jnp.transpose(dq * SCALE).astype(BF16)
        strip_ref[4 * t : 4 * t + 4, :, :HEAD] = dq.reshape(4, strip, HEAD)
        strip_ref[4 * t : 4 * t + 4, :, HEAD:] = attn.reshape(4, strip, HEAD)
    for side, ref in ((0, keep_ref), (1, send_ref)):
        ref[:, :, :HEAD] = (dks[side] * SCALE).astype(BF16).reshape(blocks, half, HEAD)
        ref[:, :, HEAD:] = dvs[side].astype(BF16).reshape(blocks, half, HEAD)


def attention(bias, mine, theirs):
    blocks, _, both = mine.shape
    grads = shape(blocks, 128, both)
    return call(
        attention_kernel,
        (bias, mine, theirs),
        [grads, grads, shape(blocks, 64, both)],
        [pltpu.VMEM((8, 512, 256), F32)] + [pltpu.VMEM((2, blocks * 128, HEAD), F32)] * 3,
        name="attention",
        megabytes=28,
        micros=12.0,
    )


def return_kernel(keep_ref, got_ref, strip_ref, out_ref):
    half = keep_ref.shape[1]
    out_ref[:, :half, :] = (keep_ref[...].astype(F32) + got_ref[...].astype(F32)).astype(BF16)
    out_ref[:, half:, :] = strip_ref[...]


def regroup_kernel(in_ref, keep_ref, send_ref):
    c = place("c")
    half, strip = 128, 64
    for out, core in ((keep_ref, c), (send_ref, 1 - c)):
        for h in range(4):
            s = (core * 4 + h) * 2
            total = in_ref[s, :half, :].astype(F32) + in_ref[s + 1, :half, :].astype(F32)
            out[h, :half, :] = total.astype(BF16)
            out[h, half : half + strip, :] = in_ref[s, half:, :]
            out[h, half + strip :, :] = in_ref[s + 1, half:, :]


def output_kernel(which, keep_ref, got_ref, *refs):
    qkv, rinv_ref, lats, gain_ref = refs[:3], refs[3], in_order(refs[4:10]), refs[10]
    weights, w_out_ref, outs, wide = refs[11:14], refs[14], refs[15:-1], refs[-1]
    rows, size = qkv[0].shape
    width = gain_ref.shape[1]
    half = rows // 2
    c = place("c")
    for ref, core in ((keep_ref, c), (got_ref, 1 - c)):
        span = pl.ds(pl.multiple_of(core * half, half), half)
        for h in range(4):
            at = slice(h * HEAD, (h + 1) * HEAD)
            wide[0, span, at] = ref[h, half:, :HEAD]
            wide[1, span, at] = ref[h, :half, :HEAD]
            wide[2, span, at] = ref[h, :half, HEAD:]
            wide[3, span, at] = ref[h, half:, HEAD:]
    both = sum(wide[n].astype(F32) * qkv[n][...].astype(F32) for n in range(3))
    factor = jnp.sum(both, axis=1, keepdims=True) * rinv_ref[...] / width
    places = tp_places()
    order = [(out, n, kind) for out, kinds in zip(outs, which) for n, kind in enumerate(kinds)]
    for out_ref, n, kind in order:
        at = places[kind]
        acc = sum(
            lax.dot_general(
                wide[i], piece_rows(weights[i], at, size), NT, preferred_element_type=F32
            )
            for i in range(3)
        )
        columns = pl.ds(pl.multiple_of(at * size, size), size)
        grad = gain_ref[:, columns] * acc - lats[kind][...].astype(F32) * factor
        out_ref[n, :rows, :] = grad.astype(BF16)
        mixed = jnp.dot(wide[3], w_out_ref[:, columns], preferred_element_type=F32)
        out_ref[n, rows:, :] = mixed.astype(BF16)


def outputs_for(which, pieces, keep, got, qkv, rinv, gain, weights, w_out):
    rows, size = pieces[0].shape
    return call(
        functools.partial(output_kernel, which),
        (keep, got, *qkv, rinv, *pieces, gain, *weights, w_out),
        [shape(len(kinds), 2 * rows, size) for kinds in which],
        [pltpu.VMEM((4, rows, size), BF16)],
        name="outputs",
        megabytes=28,
        micros=2.0,
    )


def far_kernel(own_ref, other_ref, out_ref):
    out_ref[...] = (own_ref[0].astype(F32) + other_ref[0].astype(F32)).astype(BF16)


def add_kernel(own_ref, other_ref, near_ref, side_ref, kept_ref):
    for n, ref in enumerate((near_ref, side_ref, kept_ref)):
        total = own_ref[n].astype(F32) + other_ref[n].astype(F32)
        ref[...] = total.astype(ref.dtype)


def pass_kernel(near_ref, far_ref, out_ref):
    out_ref[...] = (near_ref[...] + far_ref[...].astype(F32)).astype(BF16)


def final_kernel(valid_ref, rinv_ref, cot_ref, lat_ref, kept_ref, ahead_ref, side_ref, *outs):
    out_ref, grad_ref = outs
    rows = cot_ref.shape[0]
    total = kept_ref[...] + ahead_ref[...].astype(F32) + side_ref[...].astype(F32)
    valid = valid_ref[...] > 0.0
    grad_out = jnp.where(valid, cot_ref[...].astype(F32), 0.0)
    grad_ref[...] = grad_out + rinv_ref[...] * total[:rows]
    result = lat_ref[...].astype(F32) + total[rows:]
    out_ref[...] = jnp.where(valid, result, 0.0).astype(BF16)


def per_device(encoded, starts, w_up, norm_gain, w_query, w_key, w_value, w_out, cotangent):
    byte_rows, byte_width = encoded.shape
    shards, patch_cap = starts.shape
    columns = w_up.shape[1]
    rows = cotangent.shape[0]
    gain = norm_gain.reshape(1, -1)
    weights = (w_query, w_key, w_value)
    is_valid = (starts < byte_rows).reshape(-1, rows)
    by_half = jnp.moveaxis(is_valid.reshape(-1, 2, rows // 2), 1, 0).reshape(2, -1, 1)
    bias = jnp.broadcast_to(jnp.where(by_half, 0.0, NEG), (*by_half.shape[:2], 128))
    row_valid = lax.dynamic_slice_in_dim(is_valid, lax.axis_index(SEQ), 1, 0)
    valid = row_valid.reshape(rows, 1).astype(F32)

    cot_a, cot_sibling = along_x(cotangent), other_core(cotangent)
    sums, lead = call(
        pool_kernel,
        (starts, encoded),
        [shape(patch_cap, byte_width, dtype=F32), shape(1, byte_width, dtype=F32)],
        name="pool",
        megabytes=4,
    )
    next_lead = lax.ppermute(lead, ALL, [(i, i - 1) for i in range(1, shards)])
    patches = call(
        functools.partial(patch_kernel, byte_rows),
        (starts, sums, next_lead),
        [shape(patch_cap, byte_width)],
        name="patch",
        megabytes=4,
    )[0]
    patches, cot_a, cot_sibling = lax.optimization_barrier((patches, cot_a, cot_sibling))
    cot_f, cot_b = along_x(cot_a), along_x(cot_sibling)
    shifted = [lax.ppermute(patches, "x", [(i, (i + k) % 4) for i in range(4)]) for k in (1, 2, 3)]
    own_blocks = jnp.stack([patches, *shifted])
    other_blocks = other_core(own_blocks)
    latent = call(
        latent_kernel,
        (own_blocks, other_blocks, w_up),
        [shape(rows, columns)],
        [pltpu.VMEM((8, patch_cap, byte_width), BF16)],
        name="latent",
        megabytes=8,
        micros=DELAY,
    )[0]

    latent, cot_b, cot_f = lax.optimization_barrier((latent, cot_b, cot_f))
    piece_a, sibling = along_x(latent), other_core(latent)
    cot_theirs = other_core(jnp.stack([cot_a, cot_b, cot_f]))
    piece_a, cot_theirs = lax.optimization_barrier((piece_a, cot_theirs))
    piece_f, piece_b = along_x(piece_a), along_x(sibling)
    cots = [cotangent, cot_sibling, cot_a, cot_b, cot_f, cot_theirs]
    d_attn = d_attn_of(cots, valid, w_out)
    piece_f, piece_b, d_attn, bias = lax.optimization_barrier((piece_f, piece_b, d_attn, bias))
    theirs = other_core(jnp.stack([piece_a, piece_b, piece_f]))
    pieces = [latent, sibling, piece_a, piece_b, piece_f, theirs]
    keep, send, *qkv, rinv = project(pieces, d_attn, gain, weights)
    half = rows // 2
    packed = shape(shards // 8, half + half // 2, 2 * HEAD)
    sent = call(pack_kernel, (keep, other_core(send)), [packed], name="pack")[0]
    mine = lax.all_to_all(sent, SEQ, 0, 0, tiled=True)
    keep, send, strips = attention(bias, mine, other_core(mine[:, :half]))
    back = call(return_kernel, (keep, other_core(send), strips), [packed], name="return")[0]
    back = lax.all_to_all(back, SEQ, 0, 0, tiled=True)
    both = shape(4, rows, 2 * HEAD)
    keep, send = call(regroup_kernel, (back,), [both, both], name="regroup")
    got = other_core(send)
    rest = (qkv, rinv, gain, weights, w_out)
    block = (2 * rows, columns)
    far_given, far_own, given = outputs_for(((7,), (6,), (3, 2, 1)), pieces, keep, got, *rest)
    far_other = other_core(far_given)
    far_other, given = lax.optimization_barrier((far_other, given))
    from_other = other_core(given)
    far = call(far_kernel, (far_own, far_other), [shape(*block)], name="far")[0]
    far, got = lax.optimization_barrier((far, got))
    (for_own,) = outputs_for(((5, 4, 0),), pieces, keep, got, *rest)
    near, side, kept = call(
        add_kernel,
        (for_own, from_other),
        [shape(*block, dtype=F32), shape(*block), shape(*block, dtype=F32)],
        name="add",
        megabytes=16,
    )
    far_in = along_x(far)
    far_in, side = lax.optimization_barrier((far_in, side))
    side_in = other_core(along_x(side))
    ahead = call(pass_kernel, (near, far_in), [shape(*block)], name="pass")[0]
    return tuple(
        call(
            final_kernel,
            (valid, rinv, cotangent, latent, kept, along_x(ahead), side_in),
            [shape(rows, columns), shape(rows, columns, dtype=F32)],
            name="final",
        )
    )


def solution(mesh):
    split = Mesh(mesh.devices.reshape(4, 4, 4, 2), ALL)
    in_specs = (
        P(ALL, None),
        P(),
        P(None, TP),
        P(),
        P(None, TP),
        P(None, TP),
        P(None, TP),
        P(TP, None),
        P(SEQ, TP),
    )
    out_specs = (P(SEQ, TP), P(SEQ, TP))
    return jax.shard_map(
        per_device, mesh=split, in_specs=in_specs, out_specs=out_specs, check_vma=False
    )
```

```python
import functools

import jax
import jax.numpy as jnp
from jax import lax
from jax.experimental import pallas as pl
from jax.experimental.pallas import tpu as pltpu
from jax.sharding import Mesh
from jax.sharding import PartitionSpec as P

HEAD = 128
SEQ = ("y", "z")
TP = ("x", "c")
ALL = ("y", "z", "x", "c")
EPS = 1e-05
NEG = -1e30
SCALE = HEAD ** (-0.5)
LOG2E = 1.4426950408889634
EXP2_SCALE = SCALE * LOG2E
DELAY = 8.0
F32 = jnp.float32
BF16 = jnp.bfloat16
NT = (((1,), (1,)), ((), ()))
TN = (((0,), (0,)), ((), ()))
VMEM = pl.BlockSpec(memory_space=pltpu.VMEM)
XC = ("x", "c")


def shape(*dims, dtype=BF16):
    return jax.ShapeDtypeStruct(dims, dtype)


def call(kernel, ins, outs, scratch=(), name=None, megabytes=8, micros=1.0, stay=0):
    here = len(ins) - stay
    ins = [*ins[:here], *(pltpu.with_memory_space_constraint(a, pltpu.HBM) for a in ins[here:])]
    return pl.pallas_call(
        kernel,
        in_specs=[VMEM] * (len(ins) - stay) + [pl.BlockSpec(memory_space=pltpu.HBM)] * stay,
        out_specs=[VMEM] * len(outs),
        out_shape=list(outs),
        scratch_shapes=list(scratch),
        compiler_params=pltpu.CompilerParams(vmem_limit_bytes=megabytes * 1024 * 1024),
        cost_estimate=pl.CostEstimate(
            flops=int(micros * 1e9), transcendentals=0, bytes_accessed=int(micros * 3e6)
        ),
        name=name,
    )(*ins)


def place(axis):
    return lax.axis_index(axis)


def other_core(block):
    return lax.ppermute(block, "c", [(0, 1), (1, 0)])


def along_x(block):
    route = []
    for x in range(4):
        for c in range(2):
            route.append((x * 2 + c, ((x + 1 - 2 * c) % 4) * 2 + c))
    return lax.ppermute(block, XC, route)


def bounds(starts_ref, shard, byte_rows):
    row = starts_ref[pl.ds(shard, 1), :]
    end = jnp.full((1, 1), byte_rows, jnp.int32)
    return row, jnp.concatenate([row[:, 1:], end], axis=1)


def pool_kernel(starts_ref, enc_ref, sums_ref, lead_ref):
    byte_rows = enc_ref.shape[0]
    cap = starts_ref.shape[1]
    row, following = bounds(starts_ref, place(ALL), byte_rows)
    places = lax.broadcasted_iota(jnp.int32, (byte_rows, cap), 0)
    inside = ((places >= row) & (places < following)).astype(F32).astype(BF16)
    enc = enc_ref[...]
    sums_ref[...] = lax.dot_general(inside, enc, TN, preferred_element_type=F32)
    leading = (places < row[:, :1]).astype(F32).astype(BF16)
    lead = lax.dot_general(leading, enc, TN, preferred_element_type=F32)
    lead_ref[...] = lead[:1]


def as_column(row, eye):
    return jnp.sum(jnp.where(eye, row, 0.0), axis=1, keepdims=True)


def as_row(column, eye):
    return jnp.sum(jnp.where(eye, column, 0.0), axis=0, keepdims=True)


def eye_of(n):
    return lax.broadcasted_iota(jnp.int32, (n, n), 0) == lax.broadcasted_iota(jnp.int32, (n, n), 1)


def patch_kernel(byte_rows, starts_ref, sums_ref, next_ref, out_ref):
    shards, cap = starts_ref.shape
    shard = place(ALL)
    row, following = bounds(starts_ref, shard, byte_rows)
    count = jnp.sum((row < byte_rows).astype(F32), axis=1, keepdims=True)
    slot = lax.broadcasted_iota(jnp.int32, (1, cap), 1).astype(F32)
    last = (slot == count - 1.0).astype(F32)
    after = starts_ref[pl.ds(jnp.minimum(shard + 1, shards - 1), 1), :][:, :1].astype(F32)
    after = jnp.where(shard + 1 < shards, after, 0.0)
    sizes = (following - row).astype(F32) + last * after
    eye = eye_of(cap)
    total = sums_ref[...] + as_column(last, eye) * next_ref[...]
    out_ref[...] = (total / as_column(jnp.maximum(sizes, 1.0), eye)).astype(BF16)


def latent_kernel(own_ref, other_ref, w_ref, sibling_w_ref, out_ref, group):
    x, c = place("x"), place("c")
    count, rows, width = own_ref.shape
    for k in range(count):
        at = lax.rem(x + count - k, count) * 2
        group[at + c] = own_ref[k]
        group[at + 1 - c] = other_ref[k]
    whole = group[...].reshape(2 * count * rows, width)
    for n, ref in enumerate((w_ref, sibling_w_ref)):
        out_ref[n] = jnp.dot(whole, ref[...], preferred_element_type=F32).astype(BF16)


def tp_places():
    x, c = place("x"), place("c")
    back = lax.rem(x + 3 + 2 * c, 4) * 2
    ahead = lax.rem(x + 1 + 2 * c, 4) * 2
    far = lax.rem(x + 2, 4) * 2
    o = 1 - c
    return [2 * x + c, 2 * x + o, back + c, back + o, ahead + o, ahead + c, far + c, far + o]


def in_order(refs):
    pair, both, far, theirs = refs
    a, b, f = (theirs.at[n] for n in range(3))
    return [pair.at[0], pair.at[1], both.at[0], both.at[1], a, b, far.at[0], f]


def piece_rows(ref, at, size):
    return ref[pl.ds(pl.multiple_of(at * size, size), size), :]


def project_kernel(*refs):
    pieces, (do_ref, gain_ref), weights = in_order(refs[:4]), refs[4:6], refs[6:9]
    outs, (accs, heads) = refs[9:15], refs[15:17]
    keep_ref, send_ref, qkv_refs, rinv_ref = outs[0], outs[1], outs[2:5], outs[5]
    rows, size = pieces[0].shape
    width = gain_ref.shape[1]
    c = place("c")
    square = jnp.zeros((rows, 128), F32)
    for n, (piece, at) in enumerate(zip(pieces, tp_places())):
        wide = piece[...].astype(F32)
        squares = wide * wide
        for part in range(0, size, 128):
            square = square + squares[:, part : part + 128]
        gain = gain_ref[:, pl.ds(pl.multiple_of(at * size, size), size)]
        scaled = (wide * gain).astype(BF16)
        for kind in range(3):
            w = piece_rows(weights[kind], at, size)
            made = jnp.dot(scaled, w, preferred_element_type=F32)
            accs[kind] = made if n == 0 else accs[kind] + made
    total = jnp.sum(square, axis=1, keepdims=True)
    rinv = lax.rsqrt(total / width + EPS)
    rinv_ref[...] = rinv
    for h in range(4):
        heads[12 + h] = do_ref[:, h * HEAD : (h + 1) * HEAD]
    for kind in range(3):
        rounded = (rinv * accs[kind]).astype(BF16)
        qkv_refs[kind][...] = rounded
        for h in range(4):
            heads[kind * 4 + h] = rounded[:, h * HEAD : (h + 1) * HEAD]
    half = rows // 2
    for out, which in ((keep_ref, c), (send_ref, 1 - c)):
        span = pl.ds(pl.multiple_of(which * half, half), half)
        for h in range(4):
            out[h, :half, :HEAD] = heads[4 + h, span, :]
            out[h, :half, HEAD:] = heads[8 + h, span, :]
            out[h, half:, :HEAD] = heads[h, span, :]
            out[h, half:, HEAD:] = heads[12 + h, span, :]


def project(pieces, d_attn, gain, weights):
    rows, size = pieces[0].shape[1:]
    both = shape(4, rows, 2 * HEAD)
    return call(
        project_kernel,
        (*pieces, d_attn, gain, *weights),
        [both, both] + [shape(rows, size)] * 3 + [shape(rows, 1, dtype=F32)],
        [pltpu.VMEM((3, rows, size), F32), pltpu.VMEM((16, rows, HEAD), BF16)],
        name="project",
        megabytes=24,
        micros=5.0,
    )


def d_attn_kernel(valid_ref, w_ref, *refs):
    grads, (out_ref, pieces, sems) = in_order(refs[:4]), refs[4:]
    rows, size = grads[0].shape
    copies = [
        pltpu.make_async_copy(grad, pieces.at[n], sems.at[n]) for n, grad in enumerate(grads)
    ]
    for copy in copies:
        copy.start()
    acc = 0.0
    for n, at in enumerate(tp_places()):
        copies[n].wait()
        w = w_ref[:, pl.ds(pl.multiple_of(at * size, size), size)]
        acc = acc + lax.dot_general(pieces[n], w, NT, preferred_element_type=F32)
    out_ref[...] = jnp.where(valid_ref[...] > 0.0, acc, 0.0).astype(BF16)


def d_attn_of(grads, valid, w_out):
    rows, size = grads[0].shape[1:]
    return call(
        d_attn_kernel,
        (valid, w_out, *grads),
        [shape(rows, size)],
        [pltpu.VMEM((8, rows, size), BF16), pltpu.SemaphoreType.DMA((8,))],
        name="d_attn",
        megabytes=12,
        micros=DELAY,
        stay=4,
    )[0]


def pack_kernel(keep_ref, got_ref, out_ref):
    c = place("c")
    half = keep_ref.shape[1] // 2
    strip = half // 2
    for ref, core in ((keep_ref, c), (got_ref, 1 - c)):
        for h in range(4):
            for e in range(2):
                s = (core * 4 + h) * 2 + e
                out_ref[s, :half, :] = ref[h, :half, :]
                out_ref[s, half:, :] = ref[h, half + e * strip : half + (e + 1) * strip, :]


def attention_kernel(bias_ref, mine_ref, theirs_ref, keep_ref, send_ref, strip_ref, *scratch):
    scores, dks, dvs, biases = scratch
    c, e = place("c"), lax.rem(place("z"), 2)
    blocks = mine_ref.shape[0]
    half, strip, span, rows = 128, 64, 512, 256
    sources = (mine_ref, theirs_ref)

    def kv_of(side, u):
        ref = sources[side]
        keys = ref[4 * u : 4 * u + 4, :half, :HEAD].reshape(span, HEAD)
        return keys, ref[4 * u : 4 * u + 4, :half, HEAD:].reshape(span, HEAD)

    biases[0], biases[1] = bias_ref[c], bias_ref[1 - c]
    dks[...] = jnp.zeros_like(dks)
    dvs[...] = jnp.zeros_like(dvs)
    lane = lax.broadcasted_iota(jnp.int32, (1, rows), 1)
    place_q = (lane // strip) * 256 + lax.rem(lane, strip) + c * half + e * strip
    line = lax.broadcasted_iota(jnp.int32, (span, 1), 0)
    place_k = (line // half) * 256 + lax.rem(line, half)
    allowed = [place_k + which * half <= place_q for which in (c, 1 - c)]
    for t in range(4):
        q = mine_ref[4 * t : 4 * t + 4, half:, :HEAD].reshape(rows, HEAD)
        do = mine_ref[4 * t : 4 * t + 4, half:, HEAD:].reshape(rows, HEAD)
        peak = jnp.full((1, rows), NEG, F32)
        for side in range(2):
            for u in range(t + 1):
                keys, _ = kv_of(side, u)
                s = lax.dot_general(keys, q, NT, preferred_element_type=F32)
                bias = biases[side, u * span : (u + 1) * span, :]
                s = s + jnp.concatenate([bias, bias], axis=1)
                if u == t:
                    s = jnp.where(allowed[side], s, NEG)
                scores[side * 4 + u] = s
                peak = jnp.maximum(peak, jnp.max(s, axis=0, keepdims=True))
        total = jnp.zeros((1, rows), F32)
        mixed = jnp.zeros((HEAD, rows), F32)
        for side in range(2):
            for u in range(t + 1):
                _, values = kv_of(side, u)
                p = jnp.exp2((scores[side * 4 + u] - peak) * EXP2_SCALE)
                total = total + jnp.sum(p, axis=0, keepdims=True)
                scores[side * 4 + u] = p
                mixed = mixed + lax.dot_general(
                    values, p.astype(BF16), TN, preferred_element_type=F32
                )
        inverse = 1.0 / total
        attn = jnp.transpose(mixed * inverse).astype(BF16)
        products = do.astype(F32) * attn.astype(F32)
        delta = jnp.sum(jnp.transpose(products), axis=0, keepdims=True)
        dq = jnp.zeros((HEAD, rows), F32)
        for side in range(2):
            for u in range(t + 1):
                keys, values = kv_of(side, u)
                p = scores[side * 4 + u] * inverse
                dp = lax.dot_general(values, do, NT, preferred_element_type=F32)
                ds = (p * (dp - delta)).astype(BF16)
                at = slice(u * span, (u + 1) * span)
                dvs[side, at, :] += jnp.dot(p.astype(BF16), do, preferred_element_type=F32)
                dks[side, at, :] += jnp.dot(ds, q, preferred_element_type=F32)
                dq = dq + lax.dot_general(keys, ds, TN, preferred_element_type=F32)
        dq = jnp.transpose(dq * SCALE).astype(BF16)
        strip_ref[4 * t : 4 * t + 4, :, :HEAD] = dq.reshape(4, strip, HEAD)
        strip_ref[4 * t : 4 * t + 4, :, HEAD:] = attn.reshape(4, strip, HEAD)
    for side, ref in ((0, keep_ref), (1, send_ref)):
        ref[:, :, :HEAD] = (dks[side] * SCALE).astype(BF16).reshape(blocks, half, HEAD)
        ref[:, :, HEAD:] = dvs[side].astype(BF16).reshape(blocks, half, HEAD)


def attention(bias, mine, theirs):
    blocks, _, both = mine.shape
    grads = shape(blocks, 128, both)
    return call(
        attention_kernel,
        (bias, mine, theirs),
        [grads, grads, shape(blocks, 64, both)],
        [pltpu.VMEM((8, 512, 256), F32)] + [pltpu.VMEM((2, blocks * 128, HEAD), F32)] * 3,
        name="attention",
        megabytes=28,
        micros=12.0,
    )


def return_kernel(keep_ref, got_ref, strip_ref, out_ref):
    half = keep_ref.shape[1]
    out_ref[:, :half, :] = (keep_ref[...].astype(F32) + got_ref[...].astype(F32)).astype(BF16)
    out_ref[:, half:, :] = strip_ref[...]


def regroup_kernel(in_ref, keep_ref, send_ref):
    c = place("c")
    half, strip = 128, 64
    for out, core in ((keep_ref, c), (send_ref, 1 - c)):
        for h in range(4):
            s = (core * 4 + h) * 2
            total = in_ref[s, :half, :].astype(F32) + in_ref[s + 1, :half, :].astype(F32)
            out[h, :half, :] = total.astype(BF16)
            out[h, half : half + strip, :] = in_ref[s, half:, :]
            out[h, half + strip :, :] = in_ref[s + 1, half:, :]


def output_kernel(which, keep_ref, got_ref, *refs):
    qkv, rinv_ref, lats, gain_ref = refs[:3], refs[3], in_order(refs[4:8]), refs[8]
    weights, w_out_ref, outs, wide = refs[9:12], refs[12], refs[13:-1], refs[-1]
    rows, size = qkv[0].shape
    width = gain_ref.shape[1]
    half = rows // 2
    c = place("c")
    for ref, core in ((keep_ref, c), (got_ref, 1 - c)):
        span = pl.ds(pl.multiple_of(core * half, half), half)
        for h in range(4):
            at = slice(h * HEAD, (h + 1) * HEAD)
            wide[0, span, at] = ref[h, half:, :HEAD]
            wide[1, span, at] = ref[h, :half, :HEAD]
            wide[2, span, at] = ref[h, :half, HEAD:]
            wide[3, span, at] = ref[h, half:, HEAD:]
    both = sum(wide[n].astype(F32) * qkv[n][...].astype(F32) for n in range(3))
    factor = jnp.sum(both, axis=1, keepdims=True) * rinv_ref[...] / width
    places = tp_places()
    order = [(out, n, kind) for out, kinds in zip(outs, which) for n, kind in enumerate(kinds)]
    for out_ref, n, kind in order:
        at = places[kind]
        acc = sum(
            lax.dot_general(
                wide[i], piece_rows(weights[i], at, size), NT, preferred_element_type=F32
            )
            for i in range(3)
        )
        columns = pl.ds(pl.multiple_of(at * size, size), size)
        grad = gain_ref[:, columns] * acc - lats[kind][...].astype(F32) * factor
        out_ref[n, :rows, :] = grad.astype(BF16)
        mixed = jnp.dot(wide[3], w_out_ref[:, columns], preferred_element_type=F32)
        out_ref[n, rows:, :] = mixed.astype(BF16)


def outputs_for(which, pieces, keep, got, qkv, rinv, gain, weights, w_out):
    rows, size = pieces[0].shape[1:]
    return call(
        functools.partial(output_kernel, which),
        (keep, got, *qkv, rinv, *pieces, gain, *weights, w_out),
        [shape(len(kinds), 2 * rows, size) for kinds in which],
        [pltpu.VMEM((4, rows, size), BF16)],
        name="outputs",
        megabytes=28,
        micros=2.0,
    )


def far_kernel(own_ref, other_ref, out_ref):
    out_ref[...] = (own_ref[0].astype(F32) + other_ref[0].astype(F32)).astype(BF16)


def add_kernel(own_ref, other_ref, near_ref, side_ref, kept_ref):
    for n, ref in enumerate((near_ref, side_ref, kept_ref)):
        total = own_ref[n].astype(F32) + other_ref[n].astype(F32)
        ref[...] = total.astype(ref.dtype)


def pass_kernel(near_ref, far_ref, out_ref):
    out_ref[...] = (near_ref[...] + far_ref[...].astype(F32)).astype(BF16)


def final_kernel(valid_ref, rinv_ref, cot_ref, lat_ref, kept_ref, ahead_ref, side_ref, *outs):
    out_ref, grad_ref = outs
    rows = cot_ref.shape[0]
    total = kept_ref[...] + ahead_ref[...].astype(F32) + side_ref[...].astype(F32)
    valid = valid_ref[...] > 0.0
    grad_out = jnp.where(valid, cot_ref[...].astype(F32), 0.0)
    grad_ref[...] = grad_out + rinv_ref[...] * total[:rows]
    result = lat_ref[0].astype(F32) + total[rows:]
    out_ref[...] = jnp.where(valid, result, 0.0).astype(BF16)


def per_device(encoded, starts, w_up, norm_gain, w_query, w_key, w_value, w_out, cotangent):
    byte_rows, byte_width = encoded.shape
    shards, patch_cap = starts.shape
    columns = w_up.shape[1]
    rows = cotangent.shape[0]
    gain = norm_gain.reshape(1, -1)
    weights = (w_query, w_key, w_value)
    is_valid = (starts < byte_rows).reshape(-1, rows)
    by_half = jnp.moveaxis(is_valid.reshape(-1, 2, rows // 2), 1, 0).reshape(2, -1, 1)
    bias = jnp.broadcast_to(jnp.where(by_half, 0.0, NEG), (*by_half.shape[:2], 128))
    row_valid = lax.dynamic_slice_in_dim(is_valid, lax.axis_index(SEQ), 1, 0)
    valid = row_valid.reshape(rows, 1).astype(F32)

    cot_a, cot_sibling, sibling_up = along_x(cotangent), other_core(cotangent), other_core(w_up)
    sibling_up = pltpu.with_memory_space_constraint(sibling_up, pltpu.HBM)
    sums, lead = call(
        pool_kernel,
        (starts, encoded),
        [shape(patch_cap, byte_width, dtype=F32), shape(1, byte_width, dtype=F32)],
        name="pool",
        megabytes=4,
    )
    next_lead = lax.ppermute(lead, ALL, [(i, i - 1) for i in range(1, shards)])
    patches = call(
        functools.partial(patch_kernel, byte_rows),
        (starts, sums, next_lead),
        [shape(patch_cap, byte_width)],
        name="patch",
        megabytes=4,
    )[0]
    patches, cot_a, cot_sibling = lax.optimization_barrier((patches, cot_a, cot_sibling))
    cot_f, cot_b = along_x(cot_a), along_x(cot_sibling)
    shifted = [lax.ppermute(patches, "x", [(i, (i + k) % 4) for i in range(4)]) for k in (1, 2, 3)]
    own_blocks = jnp.stack([patches, *shifted])
    own_blocks, cot_b, cot_f = lax.optimization_barrier((own_blocks, cot_b, cot_f))
    pair = call(
        latent_kernel,
        (own_blocks, other_core(own_blocks), w_up, sibling_up),
        [shape(2, rows, columns)],
        [pltpu.VMEM((8, patch_cap, byte_width), BF16)],
        name="latent",
        megabytes=8,
        micros=DELAY,
    )[0]
    lat_both = along_x(pair)
    cot_both = jnp.stack([cot_a, cot_b])
    cot_theirs = other_core(jnp.concatenate([cot_both, cot_f[None]]))
    cot_pair = jnp.stack([cotangent, cot_sibling])
    lat_both, cot_theirs = lax.optimization_barrier((lat_both, cot_theirs))
    lat_far = along_x(lat_both[:1])
    d_attn = d_attn_of([cot_pair, cot_both, cot_f[None], cot_theirs], valid, w_out)
    lat_far, d_attn, bias = lax.optimization_barrier((lat_far, d_attn, bias))
    theirs = other_core(jnp.concatenate([lat_both, lat_far]))
    pieces = [pair, lat_both, lat_far, theirs]
    keep, send, *qkv, rinv = project(pieces, d_attn, gain, weights)
    half = rows // 2
    packed = shape(shards // 8, half + half // 2, 2 * HEAD)
    sent = call(pack_kernel, (keep, other_core(send)), [packed], name="pack")[0]
    mine = lax.all_to_all(sent, SEQ, 0, 0, tiled=True)
    keep, send, strips = attention(bias, mine, other_core(mine[:, :half]))
    back = call(return_kernel, (keep, other_core(send), strips), [packed], name="return")[0]
    back = lax.all_to_all(back, SEQ, 0, 0, tiled=True)
    both = shape(4, rows, 2 * HEAD)
    keep, send = call(regroup_kernel, (back,), [both, both], name="regroup")
    got = other_core(send)
    rest = (qkv, rinv, gain, weights, w_out)
    block = (2 * rows, columns)
    far_given, far_own, given = outputs_for(((7,), (6,), (3, 2, 1)), pieces, keep, got, *rest)
    far_other = other_core(far_given)
    far_other, given = lax.optimization_barrier((far_other, given))
    from_other = other_core(given)
    far = call(far_kernel, (far_own, far_other), [shape(*block)], name="far")[0]
    far, got = lax.optimization_barrier((far, got))
    (for_own,) = outputs_for(((5, 4, 0),), pieces, keep, got, *rest)
    near, side, kept = call(
        add_kernel,
        (for_own, from_other),
        [shape(*block, dtype=F32), shape(*block), shape(*block, dtype=F32)],
        name="add",
        megabytes=16,
    )
    far_in = along_x(far)
    side_in = other_core(along_x(side))
    ahead = call(pass_kernel, (near, far_in), [shape(*block)], name="pass")[0]
    return tuple(
        call(
            final_kernel,
            (valid, rinv, cotangent, pair, kept, along_x(ahead), side_in),
            [shape(rows, columns), shape(rows, columns, dtype=F32)],
            name="final",
        )
    )


def solution(mesh):
    split = Mesh(mesh.devices.reshape(4, 4, 4, 2), ALL)
    in_specs = (
        P(ALL, None),
        P(),
        P(None, TP),
        P(),
        P(None, TP),
        P(None, TP),
        P(None, TP),
        P(TP, None),
        P(SEQ, TP),
    )
    out_specs = (P(SEQ, TP), P(SEQ, TP))
    return jax.shard_map(
        per_device, mesh=split, in_specs=in_specs, out_specs=out_specs, check_vma=False
    )
```

```python
import functools

import jax
import jax.numpy as jnp
from jax import lax
from jax.experimental import pallas as pl
from jax.experimental.pallas import tpu as pltpu
from jax.sharding import Mesh
from jax.sharding import PartitionSpec as P

HEAD = 128
SEQ = ("y", "z")
TP = ("x", "c")
ALL = ("y", "z", "x", "c")
EPS = 1e-05
NEG = -1e30
SCALE = HEAD ** (-0.5)
LOG2E = 1.4426950408889634
EXP2_SCALE = SCALE * LOG2E
DELAY = 8.0
F32 = jnp.float32
BF16 = jnp.bfloat16
NT = (((1,), (1,)), ((), ()))
TN = (((0,), (0,)), ((), ()))
VMEM = pl.BlockSpec(memory_space=pltpu.VMEM)
XC = ("x", "c")


def shape(*dims, dtype=BF16):
    return jax.ShapeDtypeStruct(dims, dtype)


def call(kernel, ins, outs, scratch=(), name=None, megabytes=8, micros=1.0, stay=0):
    here = len(ins) - stay
    ins = [*ins[:here], *(pltpu.with_memory_space_constraint(a, pltpu.HBM) for a in ins[here:])]
    return pl.pallas_call(
        kernel,
        in_specs=[VMEM] * (len(ins) - stay) + [pl.BlockSpec(memory_space=pltpu.HBM)] * stay,
        out_specs=[VMEM] * len(outs),
        out_shape=list(outs),
        scratch_shapes=list(scratch),
        compiler_params=pltpu.CompilerParams(vmem_limit_bytes=megabytes * 1024 * 1024),
        cost_estimate=pl.CostEstimate(
            flops=int(micros * 1e9), transcendentals=0, bytes_accessed=int(micros * 3e6)
        ),
        name=name,
    )(*ins)


def place(axis):
    return lax.axis_index(axis)


def other_core(block):
    return lax.ppermute(block, "c", [(0, 1), (1, 0)])


def along_x(block):
    route = []
    for x in range(4):
        for c in range(2):
            route.append((x * 2 + c, ((x + 1 - 2 * c) % 4) * 2 + c))
    return lax.ppermute(block, XC, route)


def lane_of(table, lane):
    lanes = lax.broadcasted_iota(jnp.int32, table.shape, 1)
    return jnp.sum(jnp.where(lanes == lane, table.astype(F32), 0.0), axis=1, keepdims=True)


def bounds(starts_ref, shard, byte_rows):
    first = lane_of(starts_ref[...], shard)
    return first, jnp.concatenate([first[1:], jnp.full((1, 1), byte_rows, F32)], axis=0)


def pool_kernel(starts_ref, enc_ref, sums_ref, lead_ref, held, sems):
    byte_rows = enc_ref.shape[0]
    cap = starts_ref.shape[0]
    part = byte_rows // 4
    spans = [slice(n * part, (n + 1) * part) for n in range(4)]
    copies = [
        pltpu.make_async_copy(enc_ref.at[span, :], held.at[span, :], sems.at[n])
        for n, span in enumerate(spans)
    ]
    for copy in copies:
        copy.start()
    start, following = bounds(starts_ref, place(ALL), byte_rows)
    places = lax.broadcasted_iota(jnp.int32, (cap, byte_rows), 1).astype(F32)
    inside = ((places >= start) & (places < following)).astype(F32).astype(BF16)
    leading = (places[:8] < start[:1]).astype(F32).astype(BF16)
    for copy in copies:
        copy.wait()
    enc = held[...]
    sums_ref[...] = jnp.dot(inside, enc, preferred_element_type=F32)
    lead_ref[...] = jnp.dot(leading, enc, preferred_element_type=F32)[:1]


def patch_kernel(byte_rows, starts_ref, sums_ref, next_ref, out_ref):
    cap, shards = starts_ref.shape
    shard = place(ALL)
    start, following = bounds(starts_ref, shard, byte_rows)
    count = jnp.sum((start < byte_rows).astype(F32), axis=0, keepdims=True)
    slot = lax.broadcasted_iota(jnp.int32, (cap, 1), 0).astype(F32)
    last = (slot == count - 1.0).astype(F32)
    after = lane_of(starts_ref[...], jnp.minimum(shard + 1, shards - 1))[:1]
    after = jnp.where(shard + 1 < shards, after, 0.0)
    sizes = following - start + last * after
    total = sums_ref[...] + last * next_ref[...]
    out_ref[...] = (total / jnp.maximum(sizes, 1.0)).astype(BF16)


def latent_kernel(own_ref, other_ref, w_ref, sibling_w_ref, out_ref, group):
    x, c = place("x"), place("c")
    count, rows, width = own_ref.shape
    for k in range(count):
        at = lax.rem(x + count - k, count) * 2
        group[at + c] = own_ref[k]
        group[at + 1 - c] = other_ref[k]
    whole = group[...].reshape(2 * count * rows, width)
    for n, ref in enumerate((w_ref, sibling_w_ref)):
        out_ref[n] = jnp.dot(whole, ref[...], preferred_element_type=F32).astype(BF16)


def tp_places():
    x, c = place("x"), place("c")
    back = lax.rem(x + 3 + 2 * c, 4) * 2
    ahead = lax.rem(x + 1 + 2 * c, 4) * 2
    far = lax.rem(x + 2, 4) * 2
    o = 1 - c
    return [2 * x + c, 2 * x + o, back + c, back + o, ahead + o, ahead + c, far + c, far + o]


def in_order(refs):
    pair, both, far, theirs = refs
    a, b, f = (theirs.at[n] for n in range(3))
    return [pair.at[0], pair.at[1], both.at[0], both.at[1], a, b, far.at[0], f]


def piece_rows(ref, at, size):
    return ref[pl.ds(pl.multiple_of(at * size, size), size), :]


def project_kernel(*refs):
    pieces, (do_ref, gain_ref), weights = in_order(refs[:4]), refs[4:6], refs[6:9]
    outs, (accs, heads) = refs[9:15], refs[15:17]
    keep_ref, send_ref, qkv_refs, rinv_ref = outs[0], outs[1], outs[2:5], outs[5]
    rows, size = pieces[0].shape
    width = gain_ref.shape[1]
    c = place("c")
    square = jnp.zeros((rows, 128), F32)
    for n, (piece, at) in enumerate(zip(pieces, tp_places())):
        wide = piece[...].astype(F32)
        squares = wide * wide
        for part in range(0, size, 128):
            square = square + squares[:, part : part + 128]
        gain = gain_ref[:, pl.ds(pl.multiple_of(at * size, size), size)]
        scaled = (wide * gain).astype(BF16)
        for kind in range(3):
            w = piece_rows(weights[kind], at, size)
            made = jnp.dot(scaled, w, preferred_element_type=F32)
            accs[kind] = made if n == 0 else accs[kind] + made
    total = jnp.sum(square, axis=1, keepdims=True)
    rinv = lax.rsqrt(total / width + EPS)
    rinv_ref[...] = rinv
    for h in range(4):
        heads[12 + h] = do_ref[:, h * HEAD : (h + 1) * HEAD]
    for kind in range(3):
        rounded = (rinv * accs[kind]).astype(BF16)
        qkv_refs[kind][...] = rounded
        for h in range(4):
            heads[kind * 4 + h] = rounded[:, h * HEAD : (h + 1) * HEAD]
    half = rows // 2
    for out, which in ((keep_ref, c), (send_ref, 1 - c)):
        span = pl.ds(pl.multiple_of(which * half, half), half)
        for h in range(4):
            out[h, :half, :HEAD] = heads[4 + h, span, :]
            out[h, :half, HEAD:] = heads[8 + h, span, :]
            out[h, half:, :HEAD] = heads[h, span, :]
            out[h, half:, HEAD:] = heads[12 + h, span, :]


def project(pieces, d_attn, gain, weights):
    rows, size = pieces[0].shape[1:]
    both = shape(4, rows, 2 * HEAD)
    return call(
        project_kernel,
        (*pieces, d_attn, gain, *weights),
        [both, both] + [shape(rows, size)] * 3 + [shape(rows, 1, dtype=F32)],
        [pltpu.VMEM((3, rows, size), F32), pltpu.VMEM((16, rows, HEAD), BF16)],
        name="project",
        megabytes=24,
        micros=5.0,
    )


def d_attn_kernel(valid_ref, w_ref, *refs):
    grads, (theirs, out_ref, pieces, sems) = refs[:5], refs[5:]
    grads = [*grads[:4], theirs.at[0], theirs.at[1], grads[4], theirs.at[2]]
    rows, size = grads[0].shape
    copies = [
        pltpu.make_async_copy(grad, pieces.at[n], sems.at[n]) for n, grad in enumerate(grads)
    ]
    for copy in copies:
        copy.start()
    acc = 0.0
    for n, at in enumerate(tp_places()):
        copies[n].wait()
        w = w_ref[:, pl.ds(pl.multiple_of(at * size, size), size)]
        acc = acc + lax.dot_general(pieces[n], w, NT, preferred_element_type=F32)
    out_ref[...] = jnp.where(valid_ref[...] > 0.0, acc, 0.0).astype(BF16)


def d_attn_of(grads, valid, w_out):
    rows, size = grads[0].shape
    return call(
        d_attn_kernel,
        (valid, w_out, *grads),
        [shape(rows, size)],
        [pltpu.VMEM((8, rows, size), BF16), pltpu.SemaphoreType.DMA((8,))],
        name="d_attn",
        megabytes=12,
        micros=DELAY,
        stay=6,
    )[0]


def pack_kernel(keep_ref, got_ref, out_ref):
    c = place("c")
    half = keep_ref.shape[1] // 2
    strip = half // 2
    for ref, core in ((keep_ref, c), (got_ref, 1 - c)):
        for h in range(4):
            for e in range(2):
                s = (core * 4 + h) * 2 + e
                out_ref[s, :half, :] = ref[h, :half, :]
                out_ref[s, half:, :] = ref[h, half + e * strip : half + (e + 1) * strip, :]


def attention_kernel(bias_ref, mine_ref, theirs_ref, keep_ref, send_ref, strip_ref, *scratch):
    scores, dks, dvs, biases = scratch
    c, e = place("c"), lax.rem(place("z"), 2)
    blocks = mine_ref.shape[0]
    half, strip, span, rows = 128, 64, 512, 256
    sources = (mine_ref, theirs_ref)

    def kv_of(side, u):
        ref = sources[side]
        keys = ref[4 * u : 4 * u + 4, :half, :HEAD].reshape(span, HEAD)
        return keys, ref[4 * u : 4 * u + 4, :half, HEAD:].reshape(span, HEAD)

    biases[0], biases[1] = bias_ref[c], bias_ref[1 - c]
    dks[...] = jnp.zeros_like(dks)
    dvs[...] = jnp.zeros_like(dvs)
    lane = lax.broadcasted_iota(jnp.int32, (1, rows), 1)
    place_q = (lane // strip) * 256 + lax.rem(lane, strip) + c * half + e * strip
    line = lax.broadcasted_iota(jnp.int32, (span, 1), 0)
    place_k = (line // half) * 256 + lax.rem(line, half)
    allowed = [place_k + which * half <= place_q for which in (c, 1 - c)]
    for t in range(4):
        q = mine_ref[4 * t : 4 * t + 4, half:, :HEAD].reshape(rows, HEAD)
        do = mine_ref[4 * t : 4 * t + 4, half:, HEAD:].reshape(rows, HEAD)
        peak = jnp.full((1, rows), NEG, F32)
        for side in range(2):
            for u in range(t + 1):
                keys, _ = kv_of(side, u)
                s = lax.dot_general(keys, q, NT, preferred_element_type=F32)
                bias = biases[side, u * span : (u + 1) * span, :]
                s = s + jnp.concatenate([bias, bias], axis=1)
                if u == t:
                    s = jnp.where(allowed[side], s, NEG)
                scores[side * 4 + u] = s
                peak = jnp.maximum(peak, jnp.max(s, axis=0, keepdims=True))
        total = jnp.zeros((1, rows), F32)
        mixed = jnp.zeros((HEAD, rows), F32)
        for side in range(2):
            for u in range(t + 1):
                _, values = kv_of(side, u)
                p = jnp.exp2((scores[side * 4 + u] - peak) * EXP2_SCALE)
                total = total + jnp.sum(p, axis=0, keepdims=True)
                scores[side * 4 + u] = p
                mixed = mixed + lax.dot_general(
                    values, p.astype(BF16), TN, preferred_element_type=F32
                )
        inverse = 1.0 / total
        attn = jnp.transpose(mixed * inverse).astype(BF16)
        products = do.astype(F32) * attn.astype(F32)
        delta = jnp.sum(jnp.transpose(products), axis=0, keepdims=True)
        dq = jnp.zeros((HEAD, rows), F32)
        for side in range(2):
            for u in range(t + 1):
                keys, values = kv_of(side, u)
                p = scores[side * 4 + u] * inverse
                dp = lax.dot_general(values, do, NT, preferred_element_type=F32)
                ds = (p * (dp - delta)).astype(BF16)
                at = slice(u * span, (u + 1) * span)
                dvs[side, at, :] += jnp.dot(p.astype(BF16), do, preferred_element_type=F32)
                dks[side, at, :] += jnp.dot(ds, q, preferred_element_type=F32)
                dq = dq + lax.dot_general(keys, ds, TN, preferred_element_type=F32)
        dq = jnp.transpose(dq * SCALE).astype(BF16)
        strip_ref[4 * t : 4 * t + 4, :, :HEAD] = dq.reshape(4, strip, HEAD)
        strip_ref[4 * t : 4 * t + 4, :, HEAD:] = attn.reshape(4, strip, HEAD)
    for side, ref in ((0, keep_ref), (1, send_ref)):
        ref[:, :, :HEAD] = (dks[side] * SCALE).astype(BF16).reshape(blocks, half, HEAD)
        ref[:, :, HEAD:] = dvs[side].astype(BF16).reshape(blocks, half, HEAD)


def attention(bias, mine, theirs):
    blocks, _, both = mine.shape
    grads = shape(blocks, 128, both)
    return call(
        attention_kernel,
        (bias, mine, theirs),
        [grads, grads, shape(blocks, 64, both)],
        [pltpu.VMEM((8, 512, 256), F32)] + [pltpu.VMEM((2, blocks * 128, HEAD), F32)] * 3,
        name="attention",
        megabytes=28,
        micros=12.0,
    )


def return_kernel(keep_ref, got_ref, strip_ref, out_ref):
    half = keep_ref.shape[1]
    out_ref[:, :half, :] = (keep_ref[...].astype(F32) + got_ref[...].astype(F32)).astype(BF16)
    out_ref[:, half:, :] = strip_ref[...]


def regroup_kernel(in_ref, keep_ref, send_ref):
    c = place("c")
    half, strip = 128, 64
    for out, core in ((keep_ref, c), (send_ref, 1 - c)):
        for h in range(4):
            s = (core * 4 + h) * 2
            total = in_ref[s, :half, :].astype(F32) + in_ref[s + 1, :half, :].astype(F32)
            out[h, :half, :] = total.astype(BF16)
            out[h, half : half + strip, :] = in_ref[s, half:, :]
            out[h, half + strip :, :] = in_ref[s + 1, half:, :]


def output_kernel(which, keep_ref, got_ref, *refs):
    qkv, rinv_ref, lats, gain_ref = refs[:3], refs[3], in_order(refs[4:8]), refs[8]
    weights, w_out_ref, outs, wide = refs[9:12], refs[12], refs[13:-1], refs[-1]
    rows, size = qkv[0].shape
    width = gain_ref.shape[1]
    half = rows // 2
    c = place("c")
    for ref, core in ((keep_ref, c), (got_ref, 1 - c)):
        span = pl.ds(pl.multiple_of(core * half, half), half)
        for h in range(4):
            at = slice(h * HEAD, (h + 1) * HEAD)
            wide[0, span, at] = ref[h, half:, :HEAD]
            wide[1, span, at] = ref[h, :half, :HEAD]
            wide[2, span, at] = ref[h, :half, HEAD:]
            wide[3, span, at] = ref[h, half:, HEAD:]
    both = sum(wide[n].astype(F32) * qkv[n][...].astype(F32) for n in range(3))
    factor = jnp.sum(both, axis=1, keepdims=True) * rinv_ref[...] / width
    places = tp_places()
    order = [(out, n, kind) for out, kinds in zip(outs, which) for n, kind in enumerate(kinds)]
    for out_ref, n, kind in order:
        at = places[kind]
        acc = sum(
            lax.dot_general(
                wide[i], piece_rows(weights[i], at, size), NT, preferred_element_type=F32
            )
            for i in range(3)
        )
        columns = pl.ds(pl.multiple_of(at * size, size), size)
        grad = gain_ref[:, columns] * acc - lats[kind][...].astype(F32) * factor
        out_ref[n, :rows, :] = grad.astype(BF16)
        mixed = jnp.dot(wide[3], w_out_ref[:, columns], preferred_element_type=F32)
        out_ref[n, rows:, :] = mixed.astype(BF16)


def outputs_for(which, pieces, keep, got, qkv, rinv, gain, weights, w_out):
    rows, size = pieces[0].shape[1:]
    return call(
        functools.partial(output_kernel, which),
        (keep, got, *qkv, rinv, *pieces, gain, *weights, w_out),
        [shape(len(kinds), 2 * rows, size) for kinds in which],
        [pltpu.VMEM((4, rows, size), BF16)],
        name="outputs",
        megabytes=28,
        micros=2.0,
    )


def far_kernel(own_ref, other_ref, out_ref):
    out_ref[...] = (own_ref[0].astype(F32) + other_ref[0].astype(F32)).astype(BF16)


def add_kernel(own_ref, other_ref, near_ref, side_ref, kept_ref):
    for n, ref in enumerate((near_ref, side_ref, kept_ref)):
        total = own_ref[n].astype(F32) + other_ref[n].astype(F32)
        ref[...] = total.astype(ref.dtype)


def pass_kernel(near_ref, far_ref, out_ref):
    out_ref[...] = (near_ref[...] + far_ref[...].astype(F32)).astype(BF16)


def final_kernel(valid_ref, rinv_ref, cot_ref, lat_ref, kept_ref, ahead_ref, side_ref, *outs):
    out_ref, grad_ref = outs
    rows = cot_ref.shape[0]
    total = kept_ref[...] + ahead_ref[...].astype(F32) + side_ref[...].astype(F32)
    valid = valid_ref[...] > 0.0
    grad_out = jnp.where(valid, cot_ref[...].astype(F32), 0.0)
    grad_ref[...] = grad_out + rinv_ref[...] * total[:rows]
    result = lat_ref[0].astype(F32) + total[rows:]
    out_ref[...] = jnp.where(valid, result, 0.0).astype(BF16)


def per_device(encoded, starts, w_up, norm_gain, w_query, w_key, w_value, w_out, cotangent):
    byte_rows, byte_width = encoded.shape
    shards, patch_cap = starts.shape
    columns = w_up.shape[1]
    rows = cotangent.shape[0]
    by_slot = starts.T
    gain = norm_gain.reshape(1, -1)
    weights = (w_query, w_key, w_value)
    is_valid = (starts < byte_rows).reshape(-1, rows)
    by_half = jnp.moveaxis(is_valid.reshape(-1, 2, rows // 2), 1, 0).reshape(2, -1, 1)
    bias = jnp.broadcast_to(jnp.where(by_half, 0.0, NEG), (*by_half.shape[:2], 128))
    row_valid = lax.dynamic_slice_in_dim(is_valid, lax.axis_index(SEQ), 1, 0)
    valid = row_valid.reshape(rows, 1).astype(F32)

    cot_a, cot_sibling, sibling_up = along_x(cotangent), other_core(cotangent), other_core(w_up)
    sibling_up = pltpu.with_memory_space_constraint(sibling_up, pltpu.HBM)
    sums, lead = call(
        pool_kernel,
        (by_slot, encoded),
        [shape(patch_cap, byte_width, dtype=F32), shape(1, byte_width, dtype=F32)],
        [pltpu.VMEM(encoded.shape, BF16), pltpu.SemaphoreType.DMA((4,))],
        name="pool",
        megabytes=4,
        stay=1,
    )
    next_lead = lax.ppermute(lead, ALL, [(i, i - 1) for i in range(1, shards)])
    patches = call(
        functools.partial(patch_kernel, byte_rows),
        (by_slot, sums, next_lead),
        [shape(patch_cap, byte_width)],
        name="patch",
        megabytes=4,
    )[0]
    patches, cot_a, cot_sibling = lax.optimization_barrier((patches, cot_a, cot_sibling))
    cot_f, cot_b = along_x(cot_a), along_x(cot_sibling)
    shifted = [lax.ppermute(patches, "x", [(i, (i + k) % 4) for i in range(4)]) for k in (1, 2, 3)]
    own_blocks = jnp.stack([patches, *shifted])
    own_blocks, cot_f = lax.optimization_barrier((own_blocks, cot_f))
    other_blocks = other_core(own_blocks)
    pair = call(
        latent_kernel,
        (own_blocks, other_blocks, w_up, sibling_up),
        [shape(2, rows, columns)],
        [pltpu.VMEM((8, patch_cap, byte_width), BF16)],
        name="latent",
        megabytes=8,
        micros=DELAY,
    )[0]
    lat_both = along_x(pair)
    cot_theirs = other_core(jnp.stack([cot_a, cot_b, cot_f]))
    cots = [cotangent, cot_sibling, cot_a, cot_b, cot_f, cot_theirs]
    d_attn = d_attn_of(cots, valid, w_out)
    lat_both, d_attn, bias = lax.optimization_barrier((lat_both, d_attn, bias))
    lat_far = along_x(lat_both[:1])
    theirs = other_core(jnp.concatenate([lat_both, lat_far]))
    pieces = [pair, lat_both, lat_far, theirs]
    keep, send, *qkv, rinv = project(pieces, d_attn, gain, weights)
    half = rows // 2
    packed = shape(shards // 8, half + half // 2, 2 * HEAD)
    sent = call(pack_kernel, (keep, other_core(send)), [packed], name="pack")[0]
    mine = lax.all_to_all(sent, SEQ, 0, 0, tiled=True)
    keep, send, strips = attention(bias, mine, other_core(mine[:, :half]))
    back = call(return_kernel, (keep, other_core(send), strips), [packed], name="return")[0]
    back = lax.all_to_all(back, SEQ, 0, 0, tiled=True)
    both = shape(4, rows, 2 * HEAD)
    keep, send = call(regroup_kernel, (back,), [both, both], name="regroup")
    got = other_core(send)
    rest = (qkv, rinv, gain, weights, w_out)
    block = (2 * rows, columns)
    far_given, far_own, given = outputs_for(((7,), (6,), (3, 2, 1)), pieces, keep, got, *rest)
    far_other = other_core(far_given)
    far_other, given = lax.optimization_barrier((far_other, given))
    from_other = other_core(given)
    far = call(far_kernel, (far_own, far_other), [shape(*block)], name="far")[0]
    far, got = lax.optimization_barrier((far, got))
    (for_own,) = outputs_for(((5, 4, 0),), pieces, keep, got, *rest)
    near, side, kept = call(
        add_kernel,
        (for_own, from_other),
        [shape(*block, dtype=F32), shape(*block), shape(*block, dtype=F32)],
        name="add",
        megabytes=16,
    )
    far_in = along_x(far)
    side_in = other_core(along_x(side))
    ahead = call(pass_kernel, (near, far_in), [shape(*block)], name="pass")[0]
    return tuple(
        call(
            final_kernel,
            (valid, rinv, cotangent, pair, kept, along_x(ahead), side_in),
            [shape(rows, columns), shape(rows, columns, dtype=F32)],
            name="final",
        )
    )


def solution(mesh):
    split = Mesh(mesh.devices.reshape(4, 4, 4, 2), ALL)
    in_specs = (
        P(ALL, None),
        P(),
        P(None, TP),
        P(),
        P(None, TP),
        P(None, TP),
        P(None, TP),
        P(TP, None),
        P(SEQ, TP),
    )
    out_specs = (P(SEQ, TP), P(SEQ, TP))
    return jax.shard_map(
        per_device, mesh=split, in_specs=in_specs, out_specs=out_specs, check_vma=False
    )
```

```python
import functools

import jax
import jax.numpy as jnp
from jax import lax
from jax.experimental import pallas as pl
from jax.experimental.pallas import tpu as pltpu
from jax.sharding import Mesh
from jax.sharding import PartitionSpec as P

HEAD = 128
SEQ = ("y", "z")
TP = ("x", "c")
ALL = ("y", "z", "x", "c")
EPS = 1e-05
NEG = -1e30
SCALE = HEAD ** (-0.5)
LOG2E = 1.4426950408889634
EXP2_SCALE = SCALE * LOG2E
DELAY = 8.0
F32 = jnp.float32
BF16 = jnp.bfloat16
NT = (((1,), (1,)), ((), ()))
TN = (((0,), (0,)), ((), ()))
VMEM = pl.BlockSpec(memory_space=pltpu.VMEM)
XC = ("x", "c")


def shape(*dims, dtype=BF16):
    return jax.ShapeDtypeStruct(dims, dtype)


def call(kernel, ins, outs, scratch=(), name=None, megabytes=8, micros=1.0, stay=0):
    here = len(ins) - stay
    if name != "latent":
        ins = [*ins[:here], *(pltpu.with_memory_space_constraint(a, pltpu.HBM) for a in ins[here:])]
    return pl.pallas_call(
        kernel,
        in_specs=[VMEM] * (len(ins) - stay) + [pl.BlockSpec(memory_space=pltpu.HBM)] * stay,
        out_specs=[VMEM] * len(outs),
        out_shape=list(outs),
        scratch_shapes=list(scratch),
        compiler_params=pltpu.CompilerParams(vmem_limit_bytes=megabytes * 1024 * 1024),
        cost_estimate=pl.CostEstimate(
            flops=int(micros * 1e9), transcendentals=0, bytes_accessed=int(micros * 3e6)
        ),
        name=name,
    )(*ins)


def place(axis):
    return lax.axis_index(axis)


def other_core(block):
    return lax.ppermute(block, "c", [(0, 1), (1, 0)])


def along_x(block):
    route = []
    for x in range(4):
        for c in range(2):
            route.append((x * 2 + c, ((x + 1 - 2 * c) % 4) * 2 + c))
    return lax.ppermute(block, XC, route)


def lane_of(table, lane):
    lanes = lax.broadcasted_iota(jnp.int32, table.shape, 1)
    return jnp.sum(jnp.where(lanes == lane, table.astype(F32), 0.0), axis=1, keepdims=True)


def bounds(starts_ref, shard, byte_rows):
    first = lane_of(starts_ref[...], shard)
    return first, jnp.concatenate([first[1:], jnp.full((1, 1), byte_rows, F32)], axis=0)


def pool_kernel(starts_ref, enc_ref, sums_ref, lead_ref, held, sems):
    byte_rows = enc_ref.shape[0]
    cap = starts_ref.shape[0]
    part = byte_rows // 4
    spans = [slice(n * part, (n + 1) * part) for n in range(4)]
    copies = [
        pltpu.make_async_copy(enc_ref.at[span, :], held.at[span, :], sems.at[n])
        for n, span in enumerate(spans)
    ]
    for copy in copies:
        copy.start()
    start, following = bounds(starts_ref, place(ALL), byte_rows)
    places = lax.broadcasted_iota(jnp.int32, (cap, byte_rows), 1).astype(F32)
    inside = ((places >= start) & (places < following)).astype(F32).astype(BF16)
    leading = (places[:8] < start[:1]).astype(F32).astype(BF16)
    for copy in copies:
        copy.wait()
    enc = held[...]
    sums_ref[...] = jnp.dot(inside, enc, preferred_element_type=F32)
    lead_ref[...] = jnp.dot(leading, enc, preferred_element_type=F32)[:1]


def patch_kernel(byte_rows, starts_ref, sums_ref, next_ref, out_ref):
    cap, shards = starts_ref.shape
    shard = place(ALL)
    start, following = bounds(starts_ref, shard, byte_rows)
    count = jnp.sum((start < byte_rows).astype(F32), axis=0, keepdims=True)
    slot = lax.broadcasted_iota(jnp.int32, (cap, 1), 0).astype(F32)
    last = (slot == count - 1.0).astype(F32)
    after = lane_of(starts_ref[...], jnp.minimum(shard + 1, shards - 1))[:1]
    after = jnp.where(shard + 1 < shards, after, 0.0)
    sizes = following - start + last * after
    total = sums_ref[...] + last * next_ref[...]
    out_ref[...] = (total / jnp.maximum(sizes, 1.0)).astype(BF16)


def latent_kernel(own_ref, other_ref, w_ref, sibling_w_ref, out_ref, group, held, sems):
    x, c = place("x"), place("c")
    count, rows, width = own_ref.shape
    spans = [slice(n * width // 4, (n + 1) * width // 4) for n in range(4)]
    copies = [
        pltpu.make_async_copy(sibling_w_ref.at[span, :], held.at[span, :], sems.at[n])
        for n, span in enumerate(spans)
    ]
    for copy in copies:
        copy.start()
    for k in range(count):
        at = lax.rem(x + count - k, count) * 2
        group[at + c] = own_ref[k]
        group[at + 1 - c] = other_ref[k]
    whole = group[...].reshape(2 * count * rows, width)
    out_ref[0] = jnp.dot(whole, w_ref[...], preferred_element_type=F32).astype(BF16)
    for copy in copies:
        copy.wait()
    out_ref[1] = jnp.dot(whole, held[...], preferred_element_type=F32).astype(BF16)


def tp_places():
    x, c = place("x"), place("c")
    back = lax.rem(x + 3 + 2 * c, 4) * 2
    ahead = lax.rem(x + 1 + 2 * c, 4) * 2
    far = lax.rem(x + 2, 4) * 2
    o = 1 - c
    return [2 * x + c, 2 * x + o, back + c, back + o, ahead + o, ahead + c, far + c, far + o]


def in_order(refs):
    pair, both, far, theirs = refs
    a, b, f = (theirs.at[n] for n in range(3))
    return [pair.at[0], pair.at[1], both.at[0], both.at[1], a, b, far.at[0], f]


def piece_rows(ref, at, size):
    return ref[pl.ds(pl.multiple_of(at * size, size), size), :]


def project_kernel(*refs):
    pieces, (do_ref, gain_ref), weights = in_order(refs[:4]), refs[4:6], refs[6:9]
    outs, (accs, heads) = refs[9:15], refs[15:17]
    keep_ref, send_ref, qkv_refs, rinv_ref = outs[0], outs[1], outs[2:5], outs[5]
    rows, size = pieces[0].shape
    width = gain_ref.shape[1]
    c = place("c")
    square = jnp.zeros((rows, 128), F32)
    for n, (piece, at) in enumerate(zip(pieces, tp_places())):
        wide = piece[...].astype(F32)
        squares = wide * wide
        for part in range(0, size, 128):
            square = square + squares[:, part : part + 128]
        gain = gain_ref[:, pl.ds(pl.multiple_of(at * size, size), size)]
        scaled = (wide * gain).astype(BF16)
        for kind in range(3):
            w = piece_rows(weights[kind], at, size)
            made = jnp.dot(scaled, w, preferred_element_type=F32)
            accs[kind] = made if n == 0 else accs[kind] + made
    total = jnp.sum(square, axis=1, keepdims=True)
    rinv = lax.rsqrt(total / width + EPS)
    rinv_ref[...] = rinv
    for h in range(4):
        heads[12 + h] = do_ref[:, h * HEAD : (h + 1) * HEAD]
    for kind in range(3):
        rounded = (rinv * accs[kind]).astype(BF16)
        qkv_refs[kind][...] = rounded
        for h in range(4):
            heads[kind * 4 + h] = rounded[:, h * HEAD : (h + 1) * HEAD]
    half = rows // 2
    for out, which in ((keep_ref, c), (send_ref, 1 - c)):
        span = pl.ds(pl.multiple_of(which * half, half), half)
        for h in range(4):
            out[h, :half, :HEAD] = heads[4 + h, span, :]
            out[h, :half, HEAD:] = heads[8 + h, span, :]
            out[h, half:, :HEAD] = heads[h, span, :]
            out[h, half:, HEAD:] = heads[12 + h, span, :]


def project(pieces, d_attn, gain, weights):
    rows, size = pieces[0].shape[1:]
    both = shape(4, rows, 2 * HEAD)
    return call(
        project_kernel,
        (*pieces, d_attn, gain, *weights),
        [both, both] + [shape(rows, size)] * 3 + [shape(rows, 1, dtype=F32)],
        [pltpu.VMEM((3, rows, size), F32), pltpu.VMEM((16, rows, HEAD), BF16)],
        name="project",
        megabytes=24,
        micros=5.0,
    )


def d_attn_kernel(valid_ref, w_ref, *refs):
    grads, (theirs, out_ref, pieces, sems) = refs[:5], refs[5:]
    grads = [*grads[:4], theirs.at[0], theirs.at[1], grads[4], theirs.at[2]]
    rows, size = grads[0].shape
    copies = [
        pltpu.make_async_copy(grad, pieces.at[n], sems.at[n]) for n, grad in enumerate(grads)
    ]
    for copy in copies:
        copy.start()
    acc = 0.0
    for n, at in enumerate(tp_places()):
        copies[n].wait()
        w = w_ref[:, pl.ds(pl.multiple_of(at * size, size), size)]
        acc = acc + lax.dot_general(pieces[n], w, NT, preferred_element_type=F32)
    out_ref[...] = jnp.where(valid_ref[...] > 0.0, acc, 0.0).astype(BF16)


def d_attn_of(grads, valid, w_out):
    rows, size = grads[0].shape
    return call(
        d_attn_kernel,
        (valid, w_out, *grads),
        [shape(rows, size)],
        [pltpu.VMEM((8, rows, size), BF16), pltpu.SemaphoreType.DMA((8,))],
        name="d_attn",
        megabytes=12,
        micros=DELAY,
        stay=6,
    )[0]


def pack_kernel(keep_ref, got_ref, out_ref):
    c = place("c")
    half = keep_ref.shape[1] // 2
    strip = half // 2
    for ref, core in ((keep_ref, c), (got_ref, 1 - c)):
        for h in range(4):
            for e in range(2):
                s = (core * 4 + h) * 2 + e
                out_ref[s, :half, :] = ref[h, :half, :]
                out_ref[s, half:, :] = ref[h, half + e * strip : half + (e + 1) * strip, :]


def attention_kernel(bias_ref, mine_ref, theirs_ref, keep_ref, send_ref, strip_ref, *scratch):
    scores, dks, dvs, biases = scratch
    c, e = place("c"), lax.rem(place("z"), 2)
    blocks = mine_ref.shape[0]
    half, strip, span, rows = 128, 64, 512, 256
    sources = (mine_ref, theirs_ref)

    def kv_of(side, u):
        ref = sources[side]
        keys = ref[4 * u : 4 * u + 4, :half, :HEAD].reshape(span, HEAD)
        return keys, ref[4 * u : 4 * u + 4, :half, HEAD:].reshape(span, HEAD)

    biases[0], biases[1] = bias_ref[c], bias_ref[1 - c]
    dks[...] = jnp.zeros_like(dks)
    dvs[...] = jnp.zeros_like(dvs)
    lane = lax.broadcasted_iota(jnp.int32, (1, rows), 1)
    place_q = (lane // strip) * 256 + lax.rem(lane, strip) + c * half + e * strip
    line = lax.broadcasted_iota(jnp.int32, (span, 1), 0)
    place_k = (line // half) * 256 + lax.rem(line, half)
    allowed = [place_k + which * half <= place_q for which in (c, 1 - c)]
    for t in range(4):
        q = mine_ref[4 * t : 4 * t + 4, half:, :HEAD].reshape(rows, HEAD)
        do = mine_ref[4 * t : 4 * t + 4, half:, HEAD:].reshape(rows, HEAD)
        peak = jnp.full((1, rows), NEG, F32)
        for side in range(2):
            for u in range(t + 1):
                keys, _ = kv_of(side, u)
                s = lax.dot_general(keys, q, NT, preferred_element_type=F32)
                bias = biases[side, u * span : (u + 1) * span, :]
                s = s + jnp.concatenate([bias, bias], axis=1)
                if u == t:
                    s = jnp.where(allowed[side], s, NEG)
                scores[side * 4 + u] = s
                peak = jnp.maximum(peak, jnp.max(s, axis=0, keepdims=True))
        total = jnp.zeros((1, rows), F32)
        mixed = jnp.zeros((HEAD, rows), F32)
        for side in range(2):
            for u in range(t + 1):
                _, values = kv_of(side, u)
                p = jnp.exp2((scores[side * 4 + u] - peak) * EXP2_SCALE)
                total = total + jnp.sum(p, axis=0, keepdims=True)
                scores[side * 4 + u] = p
                mixed = mixed + lax.dot_general(
                    values, p.astype(BF16), TN, preferred_element_type=F32
                )
        inverse = 1.0 / total
        attn = jnp.transpose(mixed * inverse).astype(BF16)
        products = do.astype(F32) * attn.astype(F32)
        delta = jnp.sum(jnp.transpose(products), axis=0, keepdims=True)
        dq = jnp.zeros((HEAD, rows), F32)
        for side in range(2):
            for u in range(t + 1):
                keys, values = kv_of(side, u)
                p = scores[side * 4 + u] * inverse
                dp = lax.dot_general(values, do, NT, preferred_element_type=F32)
                ds = (p * (dp - delta)).astype(BF16)
                at = slice(u * span, (u + 1) * span)
                dvs[side, at, :] += jnp.dot(p.astype(BF16), do, preferred_element_type=F32)
                dks[side, at, :] += jnp.dot(ds, q, preferred_element_type=F32)
                dq = dq + lax.dot_general(keys, ds, TN, preferred_element_type=F32)
        dq = jnp.transpose(dq * SCALE).astype(BF16)
        strip_ref[4 * t : 4 * t + 4, :, :HEAD] = dq.reshape(4, strip, HEAD)
        strip_ref[4 * t : 4 * t + 4, :, HEAD:] = attn.reshape(4, strip, HEAD)
    for side, ref in ((0, keep_ref), (1, send_ref)):
        ref[:, :, :HEAD] = (dks[side] * SCALE).astype(BF16).reshape(blocks, half, HEAD)
        ref[:, :, HEAD:] = dvs[side].astype(BF16).reshape(blocks, half, HEAD)


def attention(bias, mine, theirs):
    blocks, _, both = mine.shape
    grads = shape(blocks, 128, both)
    return call(
        attention_kernel,
        (bias, mine, theirs),
        [grads, grads, shape(blocks, 64, both)],
        [pltpu.VMEM((8, 512, 256), F32)] + [pltpu.VMEM((2, blocks * 128, HEAD), F32)] * 3,
        name="attention",
        megabytes=28,
        micros=12.0,
    )


def return_kernel(keep_ref, got_ref, strip_ref, out_ref):
    half = keep_ref.shape[1]
    out_ref[:, :half, :] = (keep_ref[...].astype(F32) + got_ref[...].astype(F32)).astype(BF16)
    out_ref[:, half:, :] = strip_ref[...]


def regroup_kernel(in_ref, keep_ref, send_ref):
    c = place("c")
    half, strip = 128, 64
    for out, core in ((keep_ref, c), (send_ref, 1 - c)):
        for h in range(4):
            s = (core * 4 + h) * 2
            total = in_ref[s, :half, :].astype(F32) + in_ref[s + 1, :half, :].astype(F32)
            out[h, :half, :] = total.astype(BF16)
            out[h, half : half + strip, :] = in_ref[s, half:, :]
            out[h, half + strip :, :] = in_ref[s + 1, half:, :]


def output_kernel(which, keep_ref, got_ref, *refs):
    qkv, rinv_ref, lats, gain_ref = refs[:3], refs[3], in_order(refs[4:8]), refs[8]
    weights, w_out_ref, outs, wide = refs[9:12], refs[12], refs[13:-1], refs[-1]
    rows, size = qkv[0].shape
    width = gain_ref.shape[1]
    half = rows // 2
    c = place("c")
    for ref, core in ((keep_ref, c), (got_ref, 1 - c)):
        span = pl.ds(pl.multiple_of(core * half, half), half)
        for h in range(4):
            at = slice(h * HEAD, (h + 1) * HEAD)
            wide[0, span, at] = ref[h, half:, :HEAD]
            wide[1, span, at] = ref[h, :half, :HEAD]
            wide[2, span, at] = ref[h, :half, HEAD:]
            wide[3, span, at] = ref[h, half:, HEAD:]
    both = sum(wide[n].astype(F32) * qkv[n][...].astype(F32) for n in range(3))
    factor = jnp.sum(both, axis=1, keepdims=True) * rinv_ref[...] / width
    places = tp_places()
    order = [(out, n, kind) for out, kinds in zip(outs, which) for n, kind in enumerate(kinds)]
    for out_ref, n, kind in order:
        at = places[kind]
        acc = sum(
            lax.dot_general(
                wide[i], piece_rows(weights[i], at, size), NT, preferred_element_type=F32
            )
            for i in range(3)
        )
        columns = pl.ds(pl.multiple_of(at * size, size), size)
        grad = gain_ref[:, columns] * acc - lats[kind][...].astype(F32) * factor
        out_ref[n, :rows, :] = grad.astype(BF16)
        mixed = jnp.dot(wide[3], w_out_ref[:, columns], preferred_element_type=F32)
        out_ref[n, rows:, :] = mixed.astype(BF16)


def outputs_for(which, pieces, keep, got, qkv, rinv, gain, weights, w_out):
    rows, size = pieces[0].shape[1:]
    return call(
        functools.partial(output_kernel, which),
        (keep, got, *qkv, rinv, *pieces, gain, *weights, w_out),
        [shape(len(kinds), 2 * rows, size) for kinds in which],
        [pltpu.VMEM((4, rows, size), BF16)],
        name="outputs",
        megabytes=28,
        micros=2.0,
    )


def far_kernel(own_ref, other_ref, out_ref):
    out_ref[...] = (own_ref[0].astype(F32) + other_ref[0].astype(F32)).astype(BF16)


def add_kernel(own_ref, other_ref, near_ref, side_ref, kept_ref):
    for n, ref in enumerate((near_ref, side_ref, kept_ref)):
        total = own_ref[n].astype(F32) + other_ref[n].astype(F32)
        ref[...] = total.astype(ref.dtype)


def pass_kernel(near_ref, far_ref, out_ref):
    out_ref[...] = (near_ref[...] + far_ref[...].astype(F32)).astype(BF16)


def final_kernel(valid_ref, rinv_ref, cot_ref, lat_ref, kept_ref, ahead_ref, side_ref, *outs):
    out_ref, grad_ref = outs
    rows = cot_ref.shape[0]
    total = kept_ref[...] + ahead_ref[...].astype(F32) + side_ref[...].astype(F32)
    valid = valid_ref[...] > 0.0
    grad_out = jnp.where(valid, cot_ref[...].astype(F32), 0.0)
    grad_ref[...] = grad_out + rinv_ref[...] * total[:rows]
    result = lat_ref[0].astype(F32) + total[rows:]
    out_ref[...] = jnp.where(valid, result, 0.0).astype(BF16)


def per_device(encoded, starts, w_up, norm_gain, w_query, w_key, w_value, w_out, cotangent):
    byte_rows, byte_width = encoded.shape
    shards, patch_cap = starts.shape
    columns = w_up.shape[1]
    rows = cotangent.shape[0]
    by_slot = starts.T
    gain = norm_gain.reshape(1, -1)
    weights = (w_query, w_key, w_value)
    is_valid = (starts < byte_rows).reshape(-1, rows)
    by_half = jnp.moveaxis(is_valid.reshape(-1, 2, rows // 2), 1, 0).reshape(2, -1, 1)
    bias = jnp.broadcast_to(jnp.where(by_half, 0.0, NEG), (*by_half.shape[:2], 128))
    row_valid = lax.dynamic_slice_in_dim(is_valid, lax.axis_index(SEQ), 1, 0)
    valid = row_valid.reshape(rows, 1).astype(F32)

    cot_a, cot_sibling, sibling_up = along_x(cotangent), other_core(cotangent), other_core(w_up)
    sibling_up = pltpu.with_memory_space_constraint(sibling_up, pltpu.HBM)
    cot_b = along_x(cot_sibling)
    sums, lead = call(
        pool_kernel,
        (by_slot, encoded),
        [shape(patch_cap, byte_width, dtype=F32), shape(1, byte_width, dtype=F32)],
        [pltpu.VMEM(encoded.shape, BF16), pltpu.SemaphoreType.DMA((4,))],
        name="pool",
        megabytes=4,
        stay=1,
    )
    next_lead = lax.ppermute(lead, ALL, [(i, i - 1) for i in range(1, shards)])
    next_lead, cot_a, cot_b = lax.optimization_barrier((next_lead, cot_a, cot_b))
    cot_f = along_x(cot_a)
    patches = call(
        functools.partial(patch_kernel, byte_rows),
        (by_slot, sums, next_lead),
        [shape(patch_cap, byte_width)],
        name="patch",
        megabytes=4,
    )[0]
    shifted = [lax.ppermute(patches, "x", [(i, (i + k) % 4) for i in range(4)]) for k in (1, 2, 3)]
    own_blocks = jnp.stack([patches, *shifted])
    own_blocks, cot_f = lax.optimization_barrier((own_blocks, cot_f))
    other_blocks = other_core(own_blocks)
    pair = call(
        latent_kernel,
        (own_blocks, other_blocks, w_up, sibling_up),
        [shape(2, rows, columns)],
        [
            pltpu.VMEM((8, patch_cap, byte_width), BF16),
            pltpu.VMEM(w_up.shape, BF16),
            pltpu.SemaphoreType.DMA((4,)),
        ],
        name="latent",
        megabytes=8,
        micros=DELAY,
        stay=1,
    )[0]
    lat_both = along_x(pair)
    ready = (lat_both, cot_a, cot_b, cot_f)
    lat_both, cot_a, cot_b, cot_f = lax.optimization_barrier(ready)
    lat_far = along_x(lat_both[:1])
    cot_theirs = other_core(jnp.stack([cot_a, cot_b, cot_f]))
    cots = [cotangent, cot_sibling, cot_a, cot_b, cot_f, cot_theirs]
    d_attn = d_attn_of(cots, valid, w_out)
    theirs = other_core(jnp.concatenate([lat_both, lat_far]))
    pieces = [pair, lat_both, lat_far, theirs]
    keep, send, *qkv, rinv = project(pieces, d_attn, gain, weights)
    half = rows // 2
    packed = shape(shards // 8, half + half // 2, 2 * HEAD)
    sent = call(pack_kernel, (keep, other_core(send)), [packed], name="pack")[0]
    mine = lax.all_to_all(sent, SEQ, 0, 0, tiled=True)
    keep, send, strips = attention(bias, mine, other_core(mine[:, :half]))
    back = call(return_kernel, (keep, other_core(send), strips), [packed], name="return")[0]
    back = lax.all_to_all(back, SEQ, 0, 0, tiled=True)
    both = shape(4, rows, 2 * HEAD)
    keep, send = call(regroup_kernel, (back,), [both, both], name="regroup")
    got = other_core(send)
    rest = (qkv, rinv, gain, weights, w_out)
    block = (2 * rows, columns)
    far_given, far_own, given = outputs_for(((7,), (6,), (3, 2, 1)), pieces, keep, got, *rest)
    far_other = other_core(far_given)
    far_other, given = lax.optimization_barrier((far_other, given))
    from_other = other_core(given)
    far = call(far_kernel, (far_own, far_other), [shape(*block)], name="far")[0]
    far, got = lax.optimization_barrier((far, got))
    (for_own,) = outputs_for(((5, 4, 0),), pieces, keep, got, *rest)
    near, side, kept = call(
        add_kernel,
        (for_own, from_other),
        [shape(*block, dtype=F32), shape(*block), shape(*block, dtype=F32)],
        name="add",
        megabytes=16,
    )
    far_in = along_x(far)
    side_in = other_core(along_x(side))
    ahead = call(pass_kernel, (near, far_in), [shape(*block)], name="pass")[0]
    return tuple(
        call(
            final_kernel,
            (valid, rinv, cotangent, pair, kept, along_x(ahead), side_in),
            [shape(rows, columns), shape(rows, columns, dtype=F32)],
            name="final",
        )
    )


def solution(mesh):
    split = Mesh(mesh.devices.reshape(4, 4, 4, 2), ALL)
    in_specs = (
        P(ALL, None),
        P(),
        P(None, TP),
        P(),
        P(None, TP),
        P(None, TP),
        P(None, TP),
        P(TP, None),
        P(SEQ, TP),
    )
    out_specs = (P(SEQ, TP), P(SEQ, TP))
    return jax.shard_map(
        per_device, mesh=split, in_specs=in_specs, out_specs=out_specs, check_vma=False
    )
```

```python
import functools

import jax
import jax.numpy as jnp
from jax import lax
from jax.experimental import pallas as pl
from jax.experimental.pallas import tpu as pltpu
from jax.sharding import Mesh
from jax.sharding import PartitionSpec as P

HEAD = 128
SEQ = ("y", "z")
TP = ("x", "c")
ALL = ("y", "z", "x", "c")
EPS = 1e-05
NEG = -1e30
SCALE = HEAD ** (-0.5)
LOG2E = 1.4426950408889634
EXP2_SCALE = SCALE * LOG2E
DELAY = 8.0
F32 = jnp.float32
BF16 = jnp.bfloat16
NT = (((1,), (1,)), ((), ()))
TN = (((0,), (0,)), ((), ()))
VMEM = pl.BlockSpec(memory_space=pltpu.VMEM)
XC = ("x", "c")


def shape(*dims, dtype=BF16):
    return jax.ShapeDtypeStruct(dims, dtype)


def call(kernel, ins, outs, scratch=(), name=None, megabytes=8, micros=1.0, stay=0):
    here = len(ins) - stay
    ins = [*ins[:here], *(pltpu.with_memory_space_constraint(a, pltpu.HBM) for a in ins[here:])]
    return pl.pallas_call(
        kernel,
        in_specs=[VMEM] * (len(ins) - stay) + [pl.BlockSpec(memory_space=pltpu.HBM)] * stay,
        out_specs=[VMEM] * len(outs),
        out_shape=list(outs),
        scratch_shapes=list(scratch),
        compiler_params=pltpu.CompilerParams(vmem_limit_bytes=megabytes * 1024 * 1024),
        cost_estimate=pl.CostEstimate(
            flops=int(micros * 1e9), transcendentals=0, bytes_accessed=int(micros * 3e6)
        ),
        name=name,
    )(*ins)


def place(axis):
    return lax.axis_index(axis)


def other_core(block):
    return lax.ppermute(block, "c", [(0, 1), (1, 0)])


def along_x(block):
    route = []
    for x in range(4):
        for c in range(2):
            route.append((x * 2 + c, ((x + 1 - 2 * c) % 4) * 2 + c))
    return lax.ppermute(block, XC, route)


def lane_of(table, lane):
    lanes = lax.broadcasted_iota(jnp.int32, table.shape, 1)
    return jnp.sum(jnp.where(lanes == lane, table.astype(F32), 0.0), axis=1, keepdims=True)


def bounds(starts_ref, shard, byte_rows):
    first = lane_of(starts_ref[...], shard)
    return first, jnp.concatenate([first[1:], jnp.full((1, 1), byte_rows, F32)], axis=0)


def pool_kernel(starts_ref, enc_ref, sums_ref, lead_ref, held, sems):
    byte_rows = enc_ref.shape[0]
    cap = starts_ref.shape[0]
    part = byte_rows // 4
    spans = [slice(n * part, (n + 1) * part) for n in range(4)]
    copies = [
        pltpu.make_async_copy(enc_ref.at[span, :], held.at[span, :], sems.at[n])
        for n, span in enumerate(spans)
    ]
    for copy in copies:
        copy.start()
    start, following = bounds(starts_ref, place(ALL), byte_rows)
    places = lax.broadcasted_iota(jnp.int32, (cap, byte_rows), 1).astype(F32)
    inside = ((places >= start) & (places < following)).astype(F32).astype(BF16)
    leading = (places[:8] < start[:1]).astype(F32).astype(BF16)
    for copy in copies:
        copy.wait()
    enc = held[...]
    sums_ref[...] = jnp.dot(inside, enc, preferred_element_type=F32)
    lead_ref[...] = jnp.dot(leading, enc, preferred_element_type=F32)[:1]


def patch_kernel(byte_rows, starts_ref, sums_ref, next_ref, out_ref):
    cap, shards = starts_ref.shape
    shard = place(ALL)
    start, following = bounds(starts_ref, shard, byte_rows)
    count = jnp.sum((start < byte_rows).astype(F32), axis=0, keepdims=True)
    slot = lax.broadcasted_iota(jnp.int32, (cap, 1), 0).astype(F32)
    last = (slot == count - 1.0).astype(F32)
    after = lane_of(starts_ref[...], jnp.minimum(shard + 1, shards - 1))[:1]
    after = jnp.where(shard + 1 < shards, after, 0.0)
    sizes = following - start + last * after
    total = sums_ref[...] + last * next_ref[...]
    out_ref[...] = (total / jnp.maximum(sizes, 1.0)).astype(BF16)


def latent_kernel(own_ref, other_ref, w_ref, sibling_w_ref, out_ref, group):
    x, c = place("x"), place("c")
    count, rows, width = own_ref.shape
    for k in range(count):
        at = lax.rem(x + count - k, count) * 2
        group[at + c] = own_ref[k]
        group[at + 1 - c] = other_ref[k]
    whole = group[...].reshape(2 * count * rows, width)
    for n, ref in enumerate((w_ref, sibling_w_ref)):
        out_ref[n] = jnp.dot(whole, ref[...], preferred_element_type=F32).astype(BF16)


def tp_places():
    x, c = place("x"), place("c")
    back = lax.rem(x + 3 + 2 * c, 4) * 2
    ahead = lax.rem(x + 1 + 2 * c, 4) * 2
    far = lax.rem(x + 2, 4) * 2
    o = 1 - c
    return [2 * x + c, 2 * x + o, back + c, back + o, ahead + o, ahead + c, far + c, far + o]


def in_order(refs):
    pair, both, far, their_both, their_far = refs
    theirs = [their_both.at[0], their_both.at[1]]
    return [pair.at[0], pair.at[1], both.at[0], both.at[1], *theirs, far.at[0], their_far.at[0]]


def piece_rows(ref, at, size):
    return ref[pl.ds(pl.multiple_of(at * size, size), size), :]


def add_products(pieces, places, gain_ref, weights, accs, square, first):
    size = pieces[0].shape[1]
    for n, (piece, at) in enumerate(zip(pieces, places)):
        wide = piece[...].astype(F32)
        squares = wide * wide
        for part in range(0, size, 128):
            square = square + squares[:, part : part + 128]
        gain = gain_ref[:, pl.ds(pl.multiple_of(at * size, size), size)]
        scaled = (wide * gain).astype(BF16)
        for kind in range(3):
            w = piece_rows(weights[kind], at, size)
            made = jnp.dot(scaled, w, preferred_element_type=F32)
            accs[kind] = made if first and n == 0 else accs[kind] + made
    return square


def near_kernel(pair_ref, both_ref, gain_ref, wq_ref, wk_ref, wv_ref, accs, square_ref):
    pieces = [pair_ref.at[0], pair_ref.at[1], both_ref.at[0], both_ref.at[1]]
    square = jnp.zeros(square_ref.shape, F32)
    weights = (wq_ref, wk_ref, wv_ref)
    square_ref[...] = add_products(pieces, tp_places()[:4], gain_ref, weights, accs, square, True)


def near_part(pair, both, gain, weights):
    rows, size = pair.shape[1:]
    return call(
        near_kernel,
        (pair, both, gain, *weights),
        [shape(3, rows, size, dtype=F32), shape(rows, 128, dtype=F32)],
        name="project_near",
        megabytes=20,
        micros=2.0,
    )


def project_kernel(far_ref, their_both, their_far, given, square_ref, do_ref, gain_ref, *refs):
    weights, outs, (accs, heads) = refs[:3], refs[3:9], refs[9:11]
    keep_ref, send_ref, qkv_refs, rinv_ref = outs[0], outs[1], outs[2:5], outs[5]
    rows, size = do_ref.shape
    width = gain_ref.shape[1]
    c = place("c")
    pieces = [their_both.at[0], their_both.at[1], far_ref.at[0], their_far.at[0]]
    accs[...] = given[...]
    square = square_ref[...]
    square = add_products(pieces, tp_places()[4:], gain_ref, weights, accs, square, False)
    total = jnp.sum(square, axis=1, keepdims=True)
    rinv = lax.rsqrt(total / width + EPS)
    rinv_ref[...] = rinv
    for h in range(4):
        heads[12 + h] = do_ref[:, h * HEAD : (h + 1) * HEAD]
    for kind in range(3):
        rounded = (rinv * accs[kind]).astype(BF16)
        qkv_refs[kind][...] = rounded
        for h in range(4):
            heads[kind * 4 + h] = rounded[:, h * HEAD : (h + 1) * HEAD]
    half = rows // 2
    for out, which in ((keep_ref, c), (send_ref, 1 - c)):
        span = pl.ds(pl.multiple_of(which * half, half), half)
        for h in range(4):
            out[h, :half, :HEAD] = heads[4 + h, span, :]
            out[h, :half, HEAD:] = heads[8 + h, span, :]
            out[h, half:, :HEAD] = heads[h, span, :]
            out[h, half:, HEAD:] = heads[12 + h, span, :]


def project(far, theirs, near, d_attn, gain, weights):
    rows, size = d_attn.shape
    both = shape(4, rows, 2 * HEAD)
    return call(
        project_kernel,
        (far, *theirs, *near, d_attn, gain, *weights),
        [both, both] + [shape(rows, size)] * 3 + [shape(rows, 1, dtype=F32)],
        [pltpu.VMEM((3, rows, size), F32), pltpu.VMEM((16, rows, HEAD), BF16)],
        name="project",
        megabytes=24,
        micros=3.0,
    )


def d_attn_kernel(valid_ref, w_ref, *refs):
    grads, (theirs, out_ref, pieces, sems) = refs[:5], refs[5:]
    grads = [*grads[:4], theirs.at[0], theirs.at[1], grads[4], theirs.at[2]]
    rows, size = grads[0].shape
    copies = [
        pltpu.make_async_copy(grad, pieces.at[n], sems.at[n]) for n, grad in enumerate(grads)
    ]
    for copy in copies:
        copy.start()
    acc = 0.0
    for n, at in enumerate(tp_places()):
        copies[n].wait()
        w = w_ref[:, pl.ds(pl.multiple_of(at * size, size), size)]
        acc = acc + lax.dot_general(pieces[n], w, NT, preferred_element_type=F32)
    out_ref[...] = jnp.where(valid_ref[...] > 0.0, acc, 0.0).astype(BF16)


def d_attn_of(grads, valid, w_out):
    rows, size = grads[0].shape
    return call(
        d_attn_kernel,
        (valid, w_out, *grads),
        [shape(rows, size)],
        [pltpu.VMEM((8, rows, size), BF16), pltpu.SemaphoreType.DMA((8,))],
        name="d_attn",
        megabytes=12,
        micros=DELAY,
        stay=6,
    )[0]


def pack_kernel(keep_ref, got_ref, out_ref):
    c = place("c")
    half = keep_ref.shape[1] // 2
    strip = half // 2
    for ref, core in ((keep_ref, c), (got_ref, 1 - c)):
        for h in range(4):
            for e in range(2):
                s = (core * 4 + h) * 2 + e
                out_ref[s, :half, :] = ref[h, :half, :]
                out_ref[s, half:, :] = ref[h, half + e * strip : half + (e + 1) * strip, :]


def attention_kernel(bias_ref, mine_ref, theirs_ref, keep_ref, send_ref, strip_ref, *scratch):
    scores, dks, dvs, biases = scratch
    c, e = place("c"), lax.rem(place("z"), 2)
    blocks = mine_ref.shape[0]
    half, strip, span, rows = 128, 64, 512, 256
    sources = (mine_ref, theirs_ref)

    def kv_of(side, u):
        ref = sources[side]
        keys = ref[4 * u : 4 * u + 4, :half, :HEAD].reshape(span, HEAD)
        return keys, ref[4 * u : 4 * u + 4, :half, HEAD:].reshape(span, HEAD)

    biases[0], biases[1] = bias_ref[c], bias_ref[1 - c]
    dks[...] = jnp.zeros_like(dks)
    dvs[...] = jnp.zeros_like(dvs)
    lane = lax.broadcasted_iota(jnp.int32, (1, rows), 1)
    place_q = (lane // strip) * 256 + lax.rem(lane, strip) + c * half + e * strip
    line = lax.broadcasted_iota(jnp.int32, (span, 1), 0)
    place_k = (line // half) * 256 + lax.rem(line, half)
    allowed = [place_k + which * half <= place_q for which in (c, 1 - c)]
    for t in range(4):
        q = mine_ref[4 * t : 4 * t + 4, half:, :HEAD].reshape(rows, HEAD)
        do = mine_ref[4 * t : 4 * t + 4, half:, HEAD:].reshape(rows, HEAD)
        peak = jnp.full((1, rows), NEG, F32)
        for side in range(2):
            for u in range(t + 1):
                keys, _ = kv_of(side, u)
                s = lax.dot_general(keys, q, NT, preferred_element_type=F32)
                bias = biases[side, u * span : (u + 1) * span, :]
                s = s + jnp.concatenate([bias, bias], axis=1)
                if u == t:
                    s = jnp.where(allowed[side], s, NEG)
                scores[side * 4 + u] = s
                peak = jnp.maximum(peak, jnp.max(s, axis=0, keepdims=True))
        total = jnp.zeros((1, rows), F32)
        mixed = jnp.zeros((HEAD, rows), F32)
        for side in range(2):
            for u in range(t + 1):
                _, values = kv_of(side, u)
                p = jnp.exp2((scores[side * 4 + u] - peak) * EXP2_SCALE)
                total = total + jnp.sum(p, axis=0, keepdims=True)
                scores[side * 4 + u] = p
                mixed = mixed + lax.dot_general(
                    values, p.astype(BF16), TN, preferred_element_type=F32
                )
        inverse = 1.0 / total
        attn = jnp.transpose(mixed * inverse).astype(BF16)
        products = do.astype(F32) * attn.astype(F32)
        delta = jnp.sum(jnp.transpose(products), axis=0, keepdims=True)
        dq = jnp.zeros((HEAD, rows), F32)
        for side in range(2):
            for u in range(t + 1):
                keys, values = kv_of(side, u)
                p = scores[side * 4 + u] * inverse
                dp = lax.dot_general(values, do, NT, preferred_element_type=F32)
                ds = (p * (dp - delta)).astype(BF16)
                at = slice(u * span, (u + 1) * span)
                dvs[side, at, :] += jnp.dot(p.astype(BF16), do, preferred_element_type=F32)
                dks[side, at, :] += jnp.dot(ds, q, preferred_element_type=F32)
                dq = dq + lax.dot_general(keys, ds, TN, preferred_element_type=F32)
        dq = jnp.transpose(dq * SCALE).astype(BF16)
        strip_ref[4 * t : 4 * t + 4, :, :HEAD] = dq.reshape(4, strip, HEAD)
        strip_ref[4 * t : 4 * t + 4, :, HEAD:] = attn.reshape(4, strip, HEAD)
    for side, ref in ((0, keep_ref), (1, send_ref)):
        ref[:, :, :HEAD] = (dks[side] * SCALE).astype(BF16).reshape(blocks, half, HEAD)
        ref[:, :, HEAD:] = dvs[side].astype(BF16).reshape(blocks, half, HEAD)


def attention(bias, mine, theirs):
    blocks, _, both = mine.shape
    grads = shape(blocks, 128, both)
    return call(
        attention_kernel,
        (bias, mine, theirs),
        [grads, grads, shape(blocks, 64, both)],
        [pltpu.VMEM((8, 512, 256), F32)] + [pltpu.VMEM((2, blocks * 128, HEAD), F32)] * 3,
        name="attention",
        megabytes=28,
        micros=12.0,
    )


def return_kernel(keep_ref, got_ref, strip_ref, out_ref):
    half = keep_ref.shape[1]
    out_ref[:, :half, :] = (keep_ref[...].astype(F32) + got_ref[...].astype(F32)).astype(BF16)
    out_ref[:, half:, :] = strip_ref[...]


def regroup_kernel(in_ref, keep_ref, send_ref):
    c = place("c")
    half, strip = 128, 64
    for out, core in ((keep_ref, c), (send_ref, 1 - c)):
        for h in range(4):
            s = (core * 4 + h) * 2
            total = in_ref[s, :half, :].astype(F32) + in_ref[s + 1, :half, :].astype(F32)
            out[h, :half, :] = total.astype(BF16)
            out[h, half : half + strip, :] = in_ref[s, half:, :]
            out[h, half + strip :, :] = in_ref[s + 1, half:, :]


def output_kernel(which, keep_ref, got_ref, *refs):
    qkv, rinv_ref, lats, gain_ref = refs[:3], refs[3], in_order(refs[4:9]), refs[9]
    weights, w_out_ref, outs, wide = refs[10:13], refs[13], refs[14:-1], refs[-1]
    rows, size = qkv[0].shape
    width = gain_ref.shape[1]
    half = rows // 2
    c = place("c")
    for ref, core in ((keep_ref, c), (got_ref, 1 - c)):
        span = pl.ds(pl.multiple_of(core * half, half), half)
        for h in range(4):
            at = slice(h * HEAD, (h + 1) * HEAD)
            wide[0, span, at] = ref[h, half:, :HEAD]
            wide[1, span, at] = ref[h, :half, :HEAD]
            wide[2, span, at] = ref[h, :half, HEAD:]
            wide[3, span, at] = ref[h, half:, HEAD:]
    both = sum(wide[n].astype(F32) * qkv[n][...].astype(F32) for n in range(3))
    factor = jnp.sum(both, axis=1, keepdims=True) * rinv_ref[...] / width
    places = tp_places()
    order = [(out, n, kind) for out, kinds in zip(outs, which) for n, kind in enumerate(kinds)]
    for out_ref, n, kind in order:
        at = places[kind]
        acc = sum(
            lax.dot_general(
                wide[i], piece_rows(weights[i], at, size), NT, preferred_element_type=F32
            )
            for i in range(3)
        )
        columns = pl.ds(pl.multiple_of(at * size, size), size)
        grad = gain_ref[:, columns] * acc - lats[kind][...].astype(F32) * factor
        out_ref[n, :rows, :] = grad.astype(BF16)
        mixed = jnp.dot(wide[3], w_out_ref[:, columns], preferred_element_type=F32)
        out_ref[n, rows:, :] = mixed.astype(BF16)


def outputs_for(which, pieces, keep, got, qkv, rinv, gain, weights, w_out):
    rows, size = pieces[0].shape[1:]
    return call(
        functools.partial(output_kernel, which),
        (keep, got, *qkv, rinv, *pieces, gain, *weights, w_out),
        [shape(len(kinds), 2 * rows, size) for kinds in which],
        [pltpu.VMEM((4, rows, size), BF16)],
        name="outputs",
        megabytes=28,
        micros=2.0,
    )


def far_kernel(own_ref, other_ref, out_ref):
    out_ref[...] = (own_ref[0].astype(F32) + other_ref[0].astype(F32)).astype(BF16)


def add_kernel(own_ref, other_ref, near_ref, side_ref, kept_ref):
    for n, ref in enumerate((near_ref, side_ref, kept_ref)):
        total = own_ref[n].astype(F32) + other_ref[n].astype(F32)
        ref[...] = total.astype(ref.dtype)


def pass_kernel(near_ref, far_ref, out_ref):
    out_ref[...] = (near_ref[...] + far_ref[...].astype(F32)).astype(BF16)


def final_kernel(valid_ref, rinv_ref, cot_ref, lat_ref, kept_ref, ahead_ref, side_ref, *outs):
    out_ref, grad_ref = outs
    rows = cot_ref.shape[0]
    total = kept_ref[...] + ahead_ref[...].astype(F32) + side_ref[...].astype(F32)
    valid = valid_ref[...] > 0.0
    grad_out = jnp.where(valid, cot_ref[...].astype(F32), 0.0)
    grad_ref[...] = grad_out + rinv_ref[...] * total[:rows]
    result = lat_ref[0].astype(F32) + total[rows:]
    out_ref[...] = jnp.where(valid, result, 0.0).astype(BF16)


def per_device(encoded, starts, w_up, norm_gain, w_query, w_key, w_value, w_out, cotangent):
    byte_rows, byte_width = encoded.shape
    shards, patch_cap = starts.shape
    columns = w_up.shape[1]
    rows = cotangent.shape[0]
    by_slot = starts.T
    gain = norm_gain.reshape(1, -1)
    weights = (w_query, w_key, w_value)
    is_valid = (starts < byte_rows).reshape(-1, rows)
    by_half = jnp.moveaxis(is_valid.reshape(-1, 2, rows // 2), 1, 0).reshape(2, -1, 1)
    bias = jnp.broadcast_to(jnp.where(by_half, 0.0, NEG), (*by_half.shape[:2], 128))
    row_valid = lax.dynamic_slice_in_dim(is_valid, lax.axis_index(SEQ), 1, 0)
    valid = row_valid.reshape(rows, 1).astype(F32)

    cot_a, cot_sibling, sibling_up = along_x(cotangent), other_core(cotangent), other_core(w_up)
    sibling_up = pltpu.with_memory_space_constraint(sibling_up, pltpu.HBM)
    sums, lead = call(
        pool_kernel,
        (by_slot, encoded),
        [shape(patch_cap, byte_width, dtype=F32), shape(1, byte_width, dtype=F32)],
        [pltpu.VMEM(encoded.shape, BF16), pltpu.SemaphoreType.DMA((4,))],
        name="pool",
        megabytes=4,
        stay=1,
    )
    next_lead = lax.ppermute(lead, ALL, [(i, i - 1) for i in range(1, shards)])
    patches = call(
        functools.partial(patch_kernel, byte_rows),
        (by_slot, sums, next_lead),
        [shape(patch_cap, byte_width)],
        name="patch",
        megabytes=4,
    )[0]
    patches, cot_a, cot_sibling = lax.optimization_barrier((patches, cot_a, cot_sibling))
    cot_f, cot_b = along_x(cot_a), along_x(cot_sibling)
    shifted = [lax.ppermute(patches, "x", [(i, (i + k) % 4) for i in range(4)]) for k in (1, 2, 3)]
    own_blocks = jnp.stack([patches, *shifted])
    own_blocks, cot_f = lax.optimization_barrier((own_blocks, cot_f))
    other_blocks = other_core(own_blocks)
    pair = call(
        latent_kernel,
        (own_blocks, other_blocks, w_up, sibling_up),
        [shape(2, rows, columns)],
        [pltpu.VMEM((8, patch_cap, byte_width), BF16)],
        name="latent",
        megabytes=8,
        micros=DELAY,
    )[0]
    lat_both = along_x(pair)
    cot_theirs = other_core(jnp.stack([cot_a, cot_b, cot_f]))
    cots = [cotangent, cot_sibling, cot_a, cot_b, cot_f, cot_theirs]
    d_attn = d_attn_of(cots, valid, w_out)
    lat_both, d_attn, bias = lax.optimization_barrier((lat_both, d_attn, bias))
    lat_far = along_x(lat_both[:1])
    their_both = other_core(lat_both)
    near = near_part(pair, lat_both, gain, weights)
    lat_far, near, their_both = lax.optimization_barrier((lat_far, near, their_both))
    theirs = (their_both, other_core(lat_far))
    pieces = [pair, lat_both, lat_far, *theirs]
    keep, send, *qkv, rinv = project(lat_far, theirs, near, d_attn, gain, weights)
    half = rows // 2
    packed = shape(shards // 8, half + half // 2, 2 * HEAD)
    sent = call(pack_kernel, (keep, other_core(send)), [packed], name="pack")[0]
    mine = lax.all_to_all(sent, SEQ, 0, 0, tiled=True)
    keep, send, strips = attention(bias, mine, other_core(mine[:, :half]))
    back = call(return_kernel, (keep, other_core(send), strips), [packed], name="return")[0]
    back = lax.all_to_all(back, SEQ, 0, 0, tiled=True)
    both = shape(4, rows, 2 * HEAD)
    keep, send = call(regroup_kernel, (back,), [both, both], name="regroup")
    got = other_core(send)
    rest = (qkv, rinv, gain, weights, w_out)
    block = (2 * rows, columns)
    far_given, far_own, given = outputs_for(((7,), (6,), (3, 2, 1)), pieces, keep, got, *rest)
    far_other = other_core(far_given)
    far_other, given = lax.optimization_barrier((far_other, given))
    from_other = other_core(given)
    far = call(far_kernel, (far_own, far_other), [shape(*block)], name="far")[0]
    far, got = lax.optimization_barrier((far, got))
    (for_own,) = outputs_for(((5, 4, 0),), pieces, keep, got, *rest)
    near, side, kept = call(
        add_kernel,
        (for_own, from_other),
        [shape(*block, dtype=F32), shape(*block), shape(*block, dtype=F32)],
        name="add",
        megabytes=16,
    )
    far_in = along_x(far)
    side_in = other_core(along_x(side))
    ahead = call(pass_kernel, (near, far_in), [shape(*block)], name="pass")[0]
    return tuple(
        call(
            final_kernel,
            (valid, rinv, cotangent, pair, kept, along_x(ahead), side_in),
            [shape(rows, columns), shape(rows, columns, dtype=F32)],
            name="final",
        )
    )


def solution(mesh):
    split = Mesh(mesh.devices.reshape(4, 4, 4, 2), ALL)
    in_specs = (
        P(ALL, None),
        P(),
        P(None, TP),
        P(),
        P(None, TP),
        P(None, TP),
        P(None, TP),
        P(TP, None),
        P(SEQ, TP),
    )
    out_specs = (P(SEQ, TP), P(SEQ, TP))
    return jax.shard_map(
        per_device, mesh=split, in_specs=in_specs, out_specs=out_specs, check_vma=False
    )
```

```python
import functools

import jax
import jax.numpy as jnp
from jax import lax
from jax.experimental import pallas as pl
from jax.experimental.pallas import tpu as pltpu
from jax.sharding import Mesh
from jax.sharding import PartitionSpec as P

HEAD = 128
SEQ = ("y", "z")
TP = ("x", "c")
ALL = ("y", "z", "x", "c")
EPS = 1e-05
NEG = -1e30
SCALE = HEAD ** (-0.5)
LOG2E = 1.4426950408889634
EXP2_SCALE = SCALE * LOG2E
DELAY = 8.0
F32 = jnp.float32
BF16 = jnp.bfloat16
NT = (((1,), (1,)), ((), ()))
TN = (((0,), (0,)), ((), ()))
VMEM = pl.BlockSpec(memory_space=pltpu.VMEM)
XC = ("x", "c")


def shape(*dims, dtype=BF16):
    return jax.ShapeDtypeStruct(dims, dtype)


def call(kernel, ins, outs, scratch=(), name=None, megabytes=8, micros=1.0, stay=0):
    here = len(ins) - stay
    ins = [*ins[:here], *(pltpu.with_memory_space_constraint(a, pltpu.HBM) for a in ins[here:])]
    return pl.pallas_call(
        kernel,
        in_specs=[VMEM] * (len(ins) - stay) + [pl.BlockSpec(memory_space=pltpu.HBM)] * stay,
        out_specs=[VMEM] * len(outs),
        out_shape=list(outs),
        scratch_shapes=list(scratch),
        compiler_params=pltpu.CompilerParams(vmem_limit_bytes=megabytes * 1024 * 1024),
        cost_estimate=pl.CostEstimate(
            flops=int(micros * 1e9), transcendentals=0, bytes_accessed=int(micros * 3e6)
        ),
        name=name,
    )(*ins)


def place(axis):
    return lax.axis_index(axis)


def other_core(block):
    return lax.ppermute(block, "c", [(0, 1), (1, 0)])


def along_x(block):
    route = []
    for x in range(4):
        for c in range(2):
            route.append((x * 2 + c, ((x + 1 - 2 * c) % 4) * 2 + c))
    return lax.ppermute(block, XC, route)


def lane_of(table, lane):
    lanes = lax.broadcasted_iota(jnp.int32, table.shape, 1)
    return jnp.sum(jnp.where(lanes == lane, table.astype(F32), 0.0), axis=1, keepdims=True)


def bounds(starts_ref, shard, byte_rows):
    first = lane_of(starts_ref[...], shard)
    return first, jnp.concatenate([first[1:], jnp.full((1, 1), byte_rows, F32)], axis=0)


def pool_kernel(starts_ref, enc_ref, sums_ref, lead_ref, held, sems):
    byte_rows = enc_ref.shape[0]
    cap = starts_ref.shape[0]
    part = byte_rows // 4
    spans = [slice(n * part, (n + 1) * part) for n in range(4)]
    copies = [
        pltpu.make_async_copy(enc_ref.at[span, :], held.at[span, :], sems.at[n])
        for n, span in enumerate(spans)
    ]
    for copy in copies:
        copy.start()
    start, following = bounds(starts_ref, place(ALL), byte_rows)
    places = lax.broadcasted_iota(jnp.int32, (cap, byte_rows), 1).astype(F32)
    inside = ((places >= start) & (places < following)).astype(F32).astype(BF16)
    leading = (places[:8] < start[:1]).astype(F32).astype(BF16)
    for copy in copies:
        copy.wait()
    enc = held[...]
    sums_ref[...] = jnp.dot(inside, enc, preferred_element_type=F32)
    lead_ref[...] = jnp.dot(leading, enc, preferred_element_type=F32)[:1]


def patch_kernel(byte_rows, starts_ref, sums_ref, next_ref, out_ref):
    cap, shards = starts_ref.shape
    shard = place(ALL)
    start, following = bounds(starts_ref, shard, byte_rows)
    count = jnp.sum((start < byte_rows).astype(F32), axis=0, keepdims=True)
    slot = lax.broadcasted_iota(jnp.int32, (cap, 1), 0).astype(F32)
    last = (slot == count - 1.0).astype(F32)
    after = lane_of(starts_ref[...], jnp.minimum(shard + 1, shards - 1))[:1]
    after = jnp.where(shard + 1 < shards, after, 0.0)
    sizes = following - start + last * after
    total = sums_ref[...] + last * next_ref[...]
    out_ref[...] = (total / jnp.maximum(sizes, 1.0)).astype(BF16)


def latent_kernel(own_ref, other_ref, w_ref, sibling_w_ref, out_ref, group):
    x, c = place("x"), place("c")
    count, rows, width = own_ref.shape
    for k in range(count):
        at = lax.rem(x + count - k, count) * 2
        group[at + c] = own_ref[k]
        group[at + 1 - c] = other_ref[k]
    whole = group[...].reshape(2 * count * rows, width)
    for n, ref in enumerate((w_ref, sibling_w_ref)):
        out_ref[n] = jnp.dot(whole, ref[...], preferred_element_type=F32).astype(BF16)


def tp_places():
    x, c = place("x"), place("c")
    back = lax.rem(x + 3 + 2 * c, 4) * 2
    ahead = lax.rem(x + 1 + 2 * c, 4) * 2
    far = lax.rem(x + 2, 4) * 2
    o = 1 - c
    return [2 * x + c, 2 * x + o, back + c, back + o, ahead + o, ahead + c, far + c, far + o]


def in_order(refs):
    pair, both, far, their_both, their_far = refs
    theirs = [their_both.at[0], their_both.at[1]]
    return [pair.at[0], pair.at[1], both.at[0], both.at[1], *theirs, far.at[0], their_far.at[0]]


def piece_rows(ref, at, size):
    return ref[pl.ds(pl.multiple_of(at * size, size), size), :]


def add_products(pieces, places, gain_ref, weights, accs, square, first):
    size = pieces[0].shape[1]
    for n, (piece, at) in enumerate(zip(pieces, places)):
        wide = piece[...].astype(F32)
        squares = wide * wide
        for part in range(0, size, 128):
            square = square + squares[:, part : part + 128]
        gain = gain_ref[:, pl.ds(pl.multiple_of(at * size, size), size)]
        scaled = (wide * gain).astype(BF16)
        for kind in range(3):
            w = piece_rows(weights[kind], at, size)
            made = jnp.dot(scaled, w, preferred_element_type=F32)
            accs[kind] = made if first and n == 0 else accs[kind] + made
    return square


def near_kernel(pair_ref, both_ref, gain_ref, wq_ref, wk_ref, wv_ref, accs, square_ref):
    pieces = [pair_ref.at[0], pair_ref.at[1], both_ref.at[0], both_ref.at[1]]
    square = jnp.zeros(square_ref.shape, F32)
    weights = (wq_ref, wk_ref, wv_ref)
    square_ref[...] = add_products(pieces, tp_places()[:4], gain_ref, weights, accs, square, True)


def near_part(pair, both, gain, weights):
    rows, size = pair.shape[1:]
    return call(
        near_kernel,
        (pair, both, gain, *weights),
        [shape(3, rows, size, dtype=F32), shape(rows, 128, dtype=F32)],
        name="project_near",
        megabytes=20,
        micros=2.0,
    )


def project_kernel(far_ref, their_both, their_far, given, square_ref, do_ref, gain_ref, *refs):
    weights, outs, (accs, heads) = refs[:3], refs[3:9], refs[9:11]
    keep_ref, send_ref, qkv_refs, rinv_ref = outs[0], outs[1], outs[2:5], outs[5]
    rows, size = do_ref.shape
    width = gain_ref.shape[1]
    c = place("c")
    pieces = [their_both.at[0], their_both.at[1], far_ref.at[0], their_far.at[0]]
    accs[...] = given[...]
    square = square_ref[...]
    square = add_products(pieces, tp_places()[4:], gain_ref, weights, accs, square, False)
    total = jnp.sum(square, axis=1, keepdims=True)
    rinv = lax.rsqrt(total / width + EPS)
    rinv_ref[...] = rinv
    for h in range(4):
        heads[12 + h] = do_ref[:, h * HEAD : (h + 1) * HEAD]
    for kind in range(3):
        rounded = (rinv * accs[kind]).astype(BF16)
        qkv_refs[kind][...] = rounded
        for h in range(4):
            heads[kind * 4 + h] = rounded[:, h * HEAD : (h + 1) * HEAD]
    half = rows // 2
    for out, which in ((keep_ref, c), (send_ref, 1 - c)):
        span = pl.ds(pl.multiple_of(which * half, half), half)
        for h in range(4):
            out[h, :half, :HEAD] = heads[4 + h, span, :]
            out[h, :half, HEAD:] = heads[8 + h, span, :]
            out[h, half:, :HEAD] = heads[h, span, :]
            out[h, half:, HEAD:] = heads[12 + h, span, :]


def project(far, theirs, near, d_attn, gain, weights):
    rows, size = d_attn.shape
    both = shape(4, rows, 2 * HEAD)
    return call(
        project_kernel,
        (far, *theirs, *near, d_attn, gain, *weights),
        [both, both] + [shape(rows, size)] * 3 + [shape(rows, 1, dtype=F32)],
        [pltpu.VMEM((3, rows, size), F32), pltpu.VMEM((16, rows, HEAD), BF16)],
        name="project",
        megabytes=24,
        micros=3.0,
    )


def d_attn_kernel(valid_ref, w_ref, *refs):
    grads, (theirs, out_ref, pieces, sems) = refs[:5], refs[5:]
    grads = [*grads[:4], theirs.at[0], theirs.at[1], grads[4], theirs.at[2]]
    rows, size = grads[0].shape
    copies = [
        pltpu.make_async_copy(grad, pieces.at[n], sems.at[n]) for n, grad in enumerate(grads)
    ]
    for copy in copies:
        copy.start()
    acc = 0.0
    for n, at in enumerate(tp_places()):
        copies[n].wait()
        w = w_ref[:, pl.ds(pl.multiple_of(at * size, size), size)]
        acc = acc + lax.dot_general(pieces[n], w, NT, preferred_element_type=F32)
    out_ref[...] = jnp.where(valid_ref[...] > 0.0, acc, 0.0).astype(BF16)


def d_attn_of(grads, valid, w_out):
    rows, size = grads[0].shape
    return call(
        d_attn_kernel,
        (valid, w_out, *grads),
        [shape(rows, size)],
        [pltpu.VMEM((8, rows, size), BF16), pltpu.SemaphoreType.DMA((8,))],
        name="d_attn",
        megabytes=12,
        micros=DELAY,
        stay=6,
    )[0]


def pack_kernel(keep_ref, got_ref, out_ref):
    c = place("c")
    half = keep_ref.shape[1] // 2
    strip = half // 2
    for ref, core in ((keep_ref, c), (got_ref, 1 - c)):
        for h in range(4):
            for e in range(2):
                s = (core * 4 + h) * 2 + e
                out_ref[s, :half, :] = ref[h, :half, :]
                out_ref[s, half:, :] = ref[h, half + e * strip : half + (e + 1) * strip, :]


def attention_kernel(bias_ref, mine_ref, theirs_ref, keep_ref, send_ref, strip_ref, *scratch):
    scores, dks, dvs, biases = scratch
    c, e = place("c"), lax.rem(place("z"), 2)
    blocks = mine_ref.shape[0]
    half, strip, span, rows = 128, 64, 512, 256
    sources = (mine_ref, theirs_ref)

    def kv_of(side, u):
        ref = sources[side]
        keys = ref[4 * u : 4 * u + 4, :half, :HEAD].reshape(span, HEAD)
        return keys, ref[4 * u : 4 * u + 4, :half, HEAD:].reshape(span, HEAD)

    biases[0], biases[1] = bias_ref[c], bias_ref[1 - c]
    lane = lax.broadcasted_iota(jnp.int32, (1, rows), 1)
    place_q = (lane // strip) * 256 + lax.rem(lane, strip) + c * half + e * strip
    line = lax.broadcasted_iota(jnp.int32, (span, 1), 0)
    place_k = (line // half) * 256 + lax.rem(line, half)
    allowed = [place_k + which * half <= place_q for which in (c, 1 - c)]
    for t in range(4):
        q = mine_ref[4 * t : 4 * t + 4, half:, :HEAD].reshape(rows, HEAD)
        do = mine_ref[4 * t : 4 * t + 4, half:, HEAD:].reshape(rows, HEAD)
        peak = jnp.full((1, rows), NEG, F32)
        for side in range(2):
            for u in range(t + 1):
                keys, _ = kv_of(side, u)
                s = lax.dot_general(keys, q, NT, preferred_element_type=F32)
                bias = biases[side, u * span : (u + 1) * span, :]
                s = s + jnp.concatenate([bias, bias], axis=1)
                if u == t:
                    s = jnp.where(allowed[side], s, NEG)
                scores[side * 4 + u] = s
                peak = jnp.maximum(peak, jnp.max(s, axis=0, keepdims=True))
        total = jnp.zeros((1, rows), F32)
        mixed = jnp.zeros((HEAD, rows), F32)
        for side in range(2):
            for u in range(t + 1):
                _, values = kv_of(side, u)
                p = jnp.exp2((scores[side * 4 + u] - peak) * EXP2_SCALE)
                total = total + jnp.sum(p, axis=0, keepdims=True)
                scores[side * 4 + u] = p
                mixed = mixed + lax.dot_general(
                    values, p.astype(BF16), TN, preferred_element_type=F32
                )
        inverse = 1.0 / total
        attn = jnp.transpose(mixed * inverse).astype(BF16)
        products = do.astype(F32) * attn.astype(F32)
        delta = jnp.sum(jnp.transpose(products), axis=0, keepdims=True)
        dq = jnp.zeros((HEAD, rows), F32)
        for side in range(2):
            for u in range(t + 1):
                keys, values = kv_of(side, u)
                p = scores[side * 4 + u] * inverse
                dp = lax.dot_general(values, do, NT, preferred_element_type=F32)
                ds = (p * (dp - delta)).astype(BF16)
                at = slice(u * span, (u + 1) * span)
                dv = jnp.dot(p.astype(BF16), do, preferred_element_type=F32)
                dk = jnp.dot(ds, q, preferred_element_type=F32)
                dvs[side, at, :] = dv if u == t else dvs[side, at, :] + dv
                dks[side, at, :] = dk if u == t else dks[side, at, :] + dk
                dq = dq + lax.dot_general(keys, ds, TN, preferred_element_type=F32)
        dq = jnp.transpose(dq * SCALE).astype(BF16)
        strip_ref[4 * t : 4 * t + 4, :, :HEAD] = dq.reshape(4, strip, HEAD)
        strip_ref[4 * t : 4 * t + 4, :, HEAD:] = attn.reshape(4, strip, HEAD)
    for side, ref in ((0, keep_ref), (1, send_ref)):
        ref[:, :, :HEAD] = (dks[side] * SCALE).astype(BF16).reshape(blocks, half, HEAD)
        ref[:, :, HEAD:] = dvs[side].astype(BF16).reshape(blocks, half, HEAD)


def attention(bias, mine, theirs):
    blocks, _, both = mine.shape
    grads = shape(blocks, 128, both)
    return call(
        attention_kernel,
        (bias, mine, theirs),
        [grads, grads, shape(blocks, 64, both)],
        [pltpu.VMEM((8, 512, 256), F32)] + [pltpu.VMEM((2, blocks * 128, HEAD), F32)] * 3,
        name="attention",
        megabytes=28,
        micros=12.0,
    )


def return_kernel(keep_ref, got_ref, strip_ref, out_ref):
    half = keep_ref.shape[1]
    out_ref[:, :half, :] = (keep_ref[...].astype(F32) + got_ref[...].astype(F32)).astype(BF16)
    out_ref[:, half:, :] = strip_ref[...]


def regroup_kernel(in_ref, keep_ref, send_ref):
    c = place("c")
    half, strip = 128, 64
    for out, core in ((keep_ref, c), (send_ref, 1 - c)):
        for h in range(4):
            s = (core * 4 + h) * 2
            total = in_ref[s, :half, :].astype(F32) + in_ref[s + 1, :half, :].astype(F32)
            out[h, :half, :] = total.astype(BF16)
            out[h, half : half + strip, :] = in_ref[s, half:, :]
            out[h, half + strip :, :] = in_ref[s + 1, half:, :]


def output_kernel(which, keep_ref, got_ref, *refs):
    qkv, rinv_ref, lats, gain_ref = refs[:3], refs[3], in_order(refs[4:9]), refs[9]
    weights, w_out_ref, outs, wide = refs[10:13], refs[13], refs[14:-1], refs[-1]
    rows, size = qkv[0].shape
    width = gain_ref.shape[1]
    half = rows // 2
    c = place("c")
    for ref, core in ((keep_ref, c), (got_ref, 1 - c)):
        span = pl.ds(pl.multiple_of(core * half, half), half)
        for h in range(4):
            at = slice(h * HEAD, (h + 1) * HEAD)
            wide[0, span, at] = ref[h, half:, :HEAD]
            wide[1, span, at] = ref[h, :half, :HEAD]
            wide[2, span, at] = ref[h, :half, HEAD:]
            wide[3, span, at] = ref[h, half:, HEAD:]
    both = sum(wide[n].astype(F32) * qkv[n][...].astype(F32) for n in range(3))
    factor = jnp.sum(both, axis=1, keepdims=True) * rinv_ref[...] / width
    places = tp_places()
    order = [(out, n, kind) for out, kinds in zip(outs, which) for n, kind in enumerate(kinds)]
    for out_ref, n, kind in order:
        at = places[kind]
        acc = sum(
            lax.dot_general(
                wide[i], piece_rows(weights[i], at, size), NT, preferred_element_type=F32
            )
            for i in range(3)
        )
        columns = pl.ds(pl.multiple_of(at * size, size), size)
        grad = gain_ref[:, columns] * acc - lats[kind][...].astype(F32) * factor
        out_ref[n, :rows, :] = grad.astype(BF16)
        mixed = jnp.dot(wide[3], w_out_ref[:, columns], preferred_element_type=F32)
        out_ref[n, rows:, :] = mixed.astype(BF16)


def outputs_for(which, pieces, keep, got, qkv, rinv, gain, weights, w_out):
    rows, size = pieces[0].shape[1:]
    return call(
        functools.partial(output_kernel, which),
        (keep, got, *qkv, rinv, *pieces, gain, *weights, w_out),
        [shape(len(kinds), 2 * rows, size) for kinds in which],
        [pltpu.VMEM((4, rows, size), BF16)],
        name="outputs",
        megabytes=28,
        micros=2.0,
    )


def far_kernel(own_ref, other_ref, out_ref):
    out_ref[...] = (own_ref[0].astype(F32) + other_ref[0].astype(F32)).astype(BF16)


def add_kernel(own_ref, other_ref, near_ref, side_ref, kept_ref):
    for n, ref in enumerate((near_ref, side_ref, kept_ref)):
        total = own_ref[n].astype(F32) + other_ref[n].astype(F32)
        ref[...] = total.astype(ref.dtype)


def pass_kernel(near_ref, far_ref, out_ref):
    out_ref[...] = (near_ref[...] + far_ref[...].astype(F32)).astype(BF16)


def final_kernel(valid_ref, rinv_ref, cot_ref, lat_ref, kept_ref, ahead_ref, side_ref, *outs):
    out_ref, grad_ref = outs
    rows = cot_ref.shape[0]
    total = kept_ref[...] + ahead_ref[...].astype(F32) + side_ref[...].astype(F32)
    valid = valid_ref[...] > 0.0
    grad_out = jnp.where(valid, cot_ref[...].astype(F32), 0.0)
    grad_ref[...] = grad_out + rinv_ref[...] * total[:rows]
    result = lat_ref[0].astype(F32) + total[rows:]
    out_ref[...] = jnp.where(valid, result, 0.0).astype(BF16)


def per_device(encoded, starts, w_up, norm_gain, w_query, w_key, w_value, w_out, cotangent):
    byte_rows, byte_width = encoded.shape
    shards, patch_cap = starts.shape
    columns = w_up.shape[1]
    rows = cotangent.shape[0]
    by_slot = starts.T
    gain = norm_gain.reshape(1, -1)
    weights = (w_query, w_key, w_value)
    is_valid = (starts < byte_rows).reshape(-1, rows)
    by_half = jnp.moveaxis(is_valid.reshape(-1, 2, rows // 2), 1, 0).reshape(2, -1, 1)
    bias = jnp.broadcast_to(jnp.where(by_half, 0.0, NEG), (*by_half.shape[:2], 128))
    row_valid = lax.dynamic_slice_in_dim(is_valid, lax.axis_index(SEQ), 1, 0)
    valid = row_valid.reshape(rows, 1).astype(F32)

    cot_a, cot_sibling, sibling_up = along_x(cotangent), other_core(cotangent), other_core(w_up)
    sibling_up = pltpu.with_memory_space_constraint(sibling_up, pltpu.HBM)
    sums, lead = call(
        pool_kernel,
        (by_slot, encoded),
        [shape(patch_cap, byte_width, dtype=F32), shape(1, byte_width, dtype=F32)],
        [pltpu.VMEM(encoded.shape, BF16), pltpu.SemaphoreType.DMA((4,))],
        name="pool",
        megabytes=4,
        stay=1,
    )
    next_lead = lax.ppermute(lead, ALL, [(i, i - 1) for i in range(1, shards)])
    patches = call(
        functools.partial(patch_kernel, byte_rows),
        (by_slot, sums, next_lead),
        [shape(patch_cap, byte_width)],
        name="patch",
        megabytes=4,
    )[0]
    patches, cot_a, cot_sibling = lax.optimization_barrier((patches, cot_a, cot_sibling))
    cot_f, cot_b = along_x(cot_a), along_x(cot_sibling)
    shifted = [lax.ppermute(patches, "x", [(i, (i + k) % 4) for i in range(4)]) for k in (1, 2, 3)]
    own_blocks = jnp.stack([patches, *shifted])
    own_blocks, cot_f = lax.optimization_barrier((own_blocks, cot_f))
    other_blocks = other_core(own_blocks)
    pair = call(
        latent_kernel,
        (own_blocks, other_blocks, w_up, sibling_up),
        [shape(2, rows, columns)],
        [pltpu.VMEM((8, patch_cap, byte_width), BF16)],
        name="latent",
        megabytes=8,
        micros=DELAY,
    )[0]
    lat_both = along_x(pair)
    cot_theirs = other_core(jnp.stack([cot_a, cot_b, cot_f]))
    cots = [cotangent, cot_sibling, cot_a, cot_b, cot_f, cot_theirs]
    d_attn = d_attn_of(cots, valid, w_out)
    lat_both, d_attn, bias = lax.optimization_barrier((lat_both, d_attn, bias))
    lat_far = along_x(lat_both[:1])
    their_both = other_core(lat_both)
    near = near_part(pair, lat_both, gain, weights)
    lat_far, near, their_both = lax.optimization_barrier((lat_far, near, their_both))
    theirs = (their_both, other_core(lat_far))
    pieces = [pair, lat_both, lat_far, *theirs]
    keep, send, *qkv, rinv = project(lat_far, theirs, near, d_attn, gain, weights)
    half = rows // 2
    packed = shape(shards // 8, half + half // 2, 2 * HEAD)
    sent = call(pack_kernel, (keep, other_core(send)), [packed], name="pack")[0]
    mine = lax.all_to_all(sent, SEQ, 0, 0, tiled=True)
    keep, send, strips = attention(bias, mine, other_core(mine[:, :half]))
    back = call(return_kernel, (keep, other_core(send), strips), [packed], name="return")[0]
    back = lax.all_to_all(back, SEQ, 0, 0, tiled=True)
    both = shape(4, rows, 2 * HEAD)
    keep, send = call(regroup_kernel, (back,), [both, both], name="regroup")
    got = other_core(send)
    rest = (qkv, rinv, gain, weights, w_out)
    block = (2 * rows, columns)
    far_given, far_own, given = outputs_for(((7,), (6,), (3, 2, 1)), pieces, keep, got, *rest)
    far_other = other_core(far_given)
    far_other, given = lax.optimization_barrier((far_other, given))
    from_other = other_core(given)
    far = call(far_kernel, (far_own, far_other), [shape(*block)], name="far")[0]
    far, got = lax.optimization_barrier((far, got))
    (for_own,) = outputs_for(((5, 4, 0),), pieces, keep, got, *rest)
    near, side, kept = call(
        add_kernel,
        (for_own, from_other),
        [shape(*block, dtype=F32), shape(*block), shape(*block, dtype=F32)],
        name="add",
        megabytes=16,
    )
    far_in = along_x(far)
    side_in = other_core(along_x(side))
    ahead = call(pass_kernel, (near, far_in), [shape(*block)], name="pass")[0]
    return tuple(
        call(
            final_kernel,
            (valid, rinv, cotangent, pair, kept, along_x(ahead), side_in),
            [shape(rows, columns), shape(rows, columns, dtype=F32)],
            name="final",
        )
    )


def solution(mesh):
    split = Mesh(mesh.devices.reshape(4, 4, 4, 2), ALL)
    in_specs = (
        P(ALL, None),
        P(),
        P(None, TP),
        P(),
        P(None, TP),
        P(None, TP),
        P(None, TP),
        P(TP, None),
        P(SEQ, TP),
    )
    out_specs = (P(SEQ, TP), P(SEQ, TP))
    return jax.shard_map(
        per_device, mesh=split, in_specs=in_specs, out_specs=out_specs, check_vma=False
    )
```
